256 devices in a mesh: inner: 32 (over z, y), cols: 8 (over x, core).
Axes of the slice: x: 4, y: 4, z: 8, core: 2. Of those that a mesh axis runs over, the one named last changes fastest.
Arguments:
- left_u: bfloat16 [256, 512, 128], P(('inner', 'cols')), may hold values from -6 to 6
- left_v: bfloat16 [256, 512, 128], P(('inner', 'cols')), may hold values from -0.0234375 to 0.0234375
- right_u: bfloat16 [32, 256, 512, 128], P('cols', 'inner'), may hold values from -6 to 6
- right_v: bfloat16 [32, 256, 512, 128], P('cols', 'inner'), may hold values from -0.09375 to 0.09375
- sketch: bfloat16 [32, 512, 128], P('cols'), may hold values from -0.25 to 0.25
- tile_index: int32 [32, 256], P('cols', 'inner'), may hold values from 0 to 255, as said below
- slot_mask: int32 [32, 256], P('cols', 'inner'), may hold values from 0 to 1, as said below
Outputs:
- basis: float32 [32, 512, 128], P('cols', 'inner')
- coeff: float32 [32, 512, 128], P('cols', 'inner')
The draws below stay inside these ranges and needn't reach their ends.
Inputs may be any that keep to these rules, and one draw needn't show every extreme that they name: `tile_index`: slot s of an output tile belongs to inner group g = s // 8 and names a left tile of that group, g * 8 to g * 8 + 7; the tiles named by one output tile's slots of one group are distinct. `slot_mask`: in each output tile and inner group the live slots come first and there is at least one; in every output tile some group has all 8 slots live, and the others at most 4.
All inputs are finite; a program needn't handle non-finite values.
Results may differ from the reference program's by a relative error of at most 0.0045.
Values may be sent and summed in bfloat16 or wider, within the bound.
No kernel may reach another device: no remote copies, remote signals or barrier semaphores. Data moves between devices by JAX's collectives and lax.ppermute only.
A program may use at most 64 MiB of HBM per device.

```python
import math
import jax
import jax.numpy as jnp
from jax import lax

NB = 512
R = 128
SLOTS = 8
OUT = 32
LISTS = 256
TILES = 256


def draw_tile_index(key, part):
    groups = LISTS // SLOTS
    keys = jax.random.split(jax.random.fold_in(key, 11), OUT * groups)
    orders = jax.vmap(lambda sub_key: jax.random.permutation(sub_key, SLOTS))(keys)
    orders = orders.reshape(OUT, groups, SLOTS).astype(jnp.int32)
    offsets = (jnp.arange(groups, dtype=jnp.int32) * SLOTS)[None, :, None]
    return (orders + offsets).reshape(OUT, LISTS).astype(jnp.int32)


def draw_slot_mask(key, part):
    groups = LISTS // SLOTS
    first_key, second_key = jax.random.split(jax.random.fold_in(key, 23))
    counts = jax.random.randint(first_key, (OUT, groups), 1, SLOTS // 2 + 1)
    busiest = jax.random.randint(second_key, (OUT,), 0, groups)
    counts = jnp.where(jnp.arange(groups)[None, :] == busiest[:, None], SLOTS, counts)
    filled = jnp.arange(SLOTS)[None, None, :] < counts[:, :, None]
    return filled.astype(jnp.int32).reshape(OUT, LISTS)


def level_of(stream_key, extent, shards, smallest, high):
    gain, own = 1.0, jax.random.fold_in(stream_key, 6)
    for position, blocks in shards:
        heights = jnp.exp(jax.random.uniform(jax.random.fold_in(own, position), (blocks,), jnp.float32, smallest / len(shards), high / len(shards)))
        gain = gain * jnp.repeat(heights, extent[position] // blocks).reshape([-1 if axis == position else 1 for axis in range(len(extent))])
    return gain


def gaussian(stream_key, extent, width, reach, cuts=(), kind=jnp.bfloat16):
    array = jax.random.normal(stream_key, extent, jnp.float32) * width
    if len(cuts) > 0:
        array = level_of(stream_key, extent, cuts, -0.22, 0.18) * array
    return jnp.clip(array, min=-reach, max=reach).astype(kind)


def setup_inputs(seed: int = 0) -> dict:
    key_list = jax.random.split(jax.random.key(seed), 8)
    return {
        "left_u": gaussian(key_list[0], (TILES, NB, R), 1.0, 6.0, ((0, 256),)),
        "left_v": gaussian(key_list[1], (TILES, NB, R), (R * NB) ** -0.5, 0.0234375, ((0, 256),)),
        "right_u": gaussian(key_list[2], (OUT, LISTS, NB, R), 1.0, 6.0, ((0, 8), (1, 32))),
        "right_v": gaussian(key_list[3], (OUT, LISTS, NB, R), (R * LISTS // SLOTS) ** -0.5, 0.09375, ((0, 8), (1, 32))),
        "sketch": gaussian(key_list[4], (OUT, NB, R), NB ** -0.5, 0.25, ((0, 8),)),
        "tile_index": draw_tile_index(jax.random.fold_in(key_list[7], 71), 0),
        "slot_mask": draw_slot_mask(jax.random.fold_in(key_list[7], 71), 0),
    }


HIGH = lax.Precision.HIGHEST

def one_tile(left_u, left_v, right_ub, right_vb, sketch_j, index_j, mask_j):
    live_mask = mask_j.astype(jnp.float32)
    tile_u = jnp.take(left_u, index_j, axis=0).astype(jnp.float32)
    tile_v = jnp.take(left_v, index_j, axis=0).astype(jnp.float32)
    right_uf = right_ub.astype(jnp.float32)
    right_vf = right_vb.astype(jnp.float32)
    pairing = jnp.einsum('sna,snb->sab', tile_v, right_uf, precision=HIGH)
    probe = jnp.einsum('snb,nt->sbt', right_vf, sketch_j.astype(jnp.float32), precision=HIGH)
    mixing = (live_mask[:, None, None] * jnp.einsum('sab,sbt->sat', pairing, probe, precision=HIGH)).astype(jnp.bfloat16)
    sketched = jnp.einsum('sna,sat->nt', tile_u, mixing.astype(jnp.float32), precision=HIGH)
    gram_mat = jnp.dot(sketched.T, sketched, precision=HIGH)
    factor = jnp.linalg.cholesky(gram_mat)
    ortho = jax.scipy.linalg.solve_triangular(factor, sketched.T, lower=True).T
    basis = ortho * math.sqrt(NB)
    ortho_b = ortho.astype(jnp.bfloat16)
    projected = jnp.einsum('sna,nt->sat', tile_u, ortho_b.astype(jnp.float32), precision=HIGH)
    backward = (live_mask[:, None, None] * jnp.einsum('sab,sat->sbt', pairing, projected, precision=HIGH)).astype(jnp.bfloat16)
    coeff = jnp.einsum('snb,sbt->nt', right_vf, backward.astype(jnp.float32), precision=HIGH)
    return (basis, coeff)

def reference(left_u, left_v, right_u, right_v, sketch, tile_index, slot_mask):

    def per_tile(items):
        return one_tile(left_u, left_v, items[0], items[1], items[2], items[3], items[4])
    basis, coeff = lax.map(per_tile, (right_u, right_v, sketch, tile_index, slot_mask))
    return (basis, coeff)
```

```python
import math

import jax
import jax.numpy as jnp
from jax import lax
from jax.sharding import PartitionSpec as P

NB = 512
R = 128
YS = 4
HIGH = lax.Precision.HIGHEST
BF = jnp.bfloat16
F32 = jnp.float32


def shift_y(array, step, zs):
    pairs = [(z * YS + y, z * YS + (y + step) % YS) for z in range(zs) for y in range(YS)]
    return lax.ppermute(array, "inner", pairs)


def shift_z(array, step, zs):
    pairs = [(z * YS + y, ((z + step) % zs) * YS + y) for z in range(zs) for y in range(YS)]
    return lax.ppermute(array, "inner", pairs)


def pick(array, index, axis=0):
    return lax.dynamic_index_in_dim(array, index, axis, keepdims=False)


def body(left_u, left_v, right_u, right_v, sketch, tile_index, slot_mask):
    inner = lax.axis_index("inner")
    zs = lax.axis_size("inner") // YS
    z, y = inner // YS, inner % YS
    group = lax.all_gather(jnp.stack([left_u, left_v], 1), "cols", axis=0, tiled=True)
    group_u, group_v = group[:, 0], group[:, 1]
    local_idx = tile_index - inner * group_u.shape[0]
    live_mask = slot_mask.astype(F32)[..., None, None]
    tile_u = jnp.take(group_u, local_idx, axis=0)
    tile_v = jnp.take(group_v, local_idx, axis=0)
    pairing = jnp.einsum("osna,osnb->osab", tile_v, right_u, preferred_element_type=F32)
    probes = jnp.einsum("osnb,ont->osbt", right_v, sketch, preferred_element_type=F32)
    mixing = (live_mask * jnp.einsum("osab,osbt->osat", pairing, probes, precision=HIGH)).astype(BF)
    partial = jnp.einsum("osna,osat->ont", tile_u, mixing, preferred_element_type=F32)
    total = pick(partial, y)
    for step in range(1, YS):
        total = total + shift_y(pick(partial, (y + step) % YS).astype(BF), step, zs).astype(F32)
    rows = NB // zs
    blocks = total.reshape(zs, rows, R)
    mine = pick(blocks, z)
    for step in range(1, zs):
        mine = mine + shift_z(pick(blocks, (z + step) % zs), step, zs)
    summed = jnp.zeros((zs, rows, R), F32)
    summed = lax.dynamic_update_index_in_dim(summed, mine, z, 0)
    for step in range(1, zs):
        summed = lax.dynamic_update_index_in_dim(summed, shift_z(mine, step, zs), (z - step) % zs, 0)
    summed = summed.reshape(1, NB, R)
    gram = jnp.einsum("ona,onb->oab", summed, summed, precision=HIGH)
    factor = jnp.linalg.cholesky(gram)
    solved = jax.scipy.linalg.solve_triangular(factor, jnp.swapaxes(summed, 1, 2), lower=True)
    ortho = jnp.swapaxes(solved, 1, 2)[0]
    high = ortho.astype(BF)
    low = (ortho - high.astype(F32)).astype(BF)
    out_rows = NB // (zs * YS)
    full = jnp.zeros((YS, NB, R), BF)
    basis = jnp.zeros((YS, out_rows, R), F32)
    for step in range(YS):
        start = (z * YS + (y + step) % YS) * out_rows
        message = jnp.concatenate([high, lax.dynamic_slice_in_dim(low, start, out_rows, 0)])
        if step:
            message = shift_y(message, step, zs)
        tile = (y - step) % YS
        full = lax.dynamic_update_index_in_dim(full, message[:NB], tile, 0)
        kept = lax.dynamic_slice_in_dim(message, inner * out_rows, out_rows, 0).astype(F32)
        kept = (kept + message[NB:].astype(F32)) * math.sqrt(NB)
        basis = lax.dynamic_update_index_in_dim(basis, kept, tile, 0)
    projected = jnp.einsum("osna,ont->osat", tile_u, full, preferred_element_type=F32)
    backward = (live_mask * jnp.einsum("osab,osat->osbt", pairing, projected, precision=HIGH)).astype(BF)
    terms = jnp.einsum("osnb,osbt->ont", right_v, backward, preferred_element_type=F32)
    terms = terms.reshape(terms.shape[0], zs, YS, out_rows, R)
    part = pick(terms, y, 2)
    for step in range(1, YS):
        part = part + shift_y(pick(terms, (y + step) % YS, 2).astype(BF), step, zs).astype(F32)
    coeff = pick(part, z, 1)
    for step in range(1, zs):
        coeff = coeff + shift_z(pick(part, (z + step) % zs, 1), step, zs)
    return (basis, coeff)


def solution(mesh):
    return jax.shard_map(
        body,
        mesh=mesh,
        in_specs=(
            P(("inner", "cols"), None, None),
            P(("inner", "cols"), None, None),
            P("cols", "inner", None, None),
            P("cols", "inner", None, None),
            P("cols", None, None),
            P("cols", "inner"),
            P("cols", "inner"),
        ),
        out_specs=(P("cols", "inner", None), P("cols", "inner", None)),
        check_vma=False,
    )
```

```python
import functools
import math

import jax
import jax.numpy as jnp
from jax import lax
from jax.experimental import pallas as pl
from jax.experimental.pallas import tpu as pltpu
from jax.sharding import PartitionSpec as P

NB = 512
R = 128
YS = 4
BATCH = 4
HIGH = lax.Precision.HIGHEST
BF = jnp.bfloat16
F32 = jnp.float32
VMEM = pltpu.VMEM
NT = (((1,), (1,)), ((), ()))


def dot(a, b):
    return jnp.dot(a, b, preferred_element_type=F32)


def dot_nt(a, b):
    return lax.dot_general(a, b, NT, preferred_element_type=F32)


def halves(a):
    high = a.astype(BF)
    return high, (a - high.astype(F32)).astype(BF)


def in_vmem():
    return pl.BlockSpec(memory_space=VMEM)


def in_place():
    return pl.BlockSpec(memory_space=pltpu.HBM)


def in_smem():
    return pl.BlockSpec(memory_space=pltpu.SMEM)


def fetch(meta, outs, slots, source, held, sems):
    def tile(j, _):
        def one(s, _):
            pltpu.make_async_copy(source.at[j, s], held.at[j * slots + s], sems.at[j * slots + s]).start()
            return 0

        lax.fori_loop(0, meta[outs * slots + j], one, 0)
        return 0

    lax.fori_loop(0, outs, tile, 0)


def arrive(meta, outs, slots, j, s, source, held, sems):
    @pl.when(s < meta[outs * slots + j])
    def _():
        pltpu.make_async_copy(source.at[j, s], held.at[j * slots + s], sems.at[j * slots + s]).wait()


def probe_kernel(outs, slots, meta, right_v, sketch, probe_h, probe_l, held, sems):
    fetch(meta, outs, slots, right_v, held, sems)

    def tile(j, _):
        turned = sketch[j].T

        def batch(first, _):
            base = first * BATCH
            for i in range(BATCH):
                arrive(meta, outs, slots, j, base + i, right_v, held, sems)
            for i in range(BATCH):
                at = j * slots + base + i
                high, low = halves(dot(turned, held[at]))
                probe_h[at] = high
                probe_l[at] = low
            return 0

        lax.fori_loop(0, (meta[outs * slots + j] + BATCH - 1) // BATCH, batch, 0)
        return 0

    lax.fori_loop(0, outs, tile, 0)


def forward_kernel(outs, slots, meta, right_u, group, probe_h, probe_l, own, send1, send2, send3, pair_h, pair_l,
                   held, turned, acc, sems):
    fetch(meta, outs, slots, right_u, held, sems)
    y = meta[outs * slots + outs]

    def turn(k, _):
        turned[k] = group[k, 1].T
        return 0

    lax.fori_loop(0, group.shape[0], turn, 0)

    def tile(order, _):
        j = lax.rem(y + 1 + order, YS)
        count = meta[outs * slots + j]
        acc[...] = jnp.zeros_like(acc)

        def batch(first, _):
            base = first * BATCH
            for i in range(BATCH):
                arrive(meta, outs, slots, j, base + i, right_u, held, sems)
            terms = []
            for i in range(BATCH):
                at = j * slots + base + i
                k = meta[at]
                high, low = halves(dot(turned[k], held[at]))
                pair_h[at] = high
                pair_l[at] = low
                mixing = dot_nt(high, probe_h[at]) + dot_nt(high, probe_l[at]) + dot_nt(low, probe_h[at])
                mixing = jnp.where(base + i < count, mixing, 0.0).astype(BF)
                terms.append(dot(group[k, 0], mixing))
            acc[...] += (terms[0] + terms[1]) + (terms[2] + terms[3])
            return 0

        lax.fori_loop(0, (count + BATCH - 1) // BATCH, batch, 0)
        for place, out in enumerate((send1, send2, send3, own)):
            @pl.when(order == place)
            def _():
                out[...] = acc[...].astype(out.dtype)
        return 0

    lax.fori_loop(0, YS, tile, 0)


def backward_kernel(outs, slots, zs, meta, right_v, group, pair_h, pair_l, msg0, msg1, msg2, msg3,
                    own, send1, send2, send3, basis, held, turned, acc, sems):
    fetch(meta, outs, slots, right_v, held, sems)
    y = meta[outs * slots + outs]
    rows = NB // (zs * YS)
    for step, msg in enumerate((msg0, msg1, msg2, msg3)):
        j = lax.rem(y + YS - step, YS)
        turned[j] = msg[:NB].T
        kept = msg[NB:NB + rows].astype(F32) + msg[NB + rows:].astype(F32)
        basis[j] = kept * math.sqrt(NB)

    def tile(j, _):
        count = meta[outs * slots + j]
        acc[...] = jnp.zeros_like(acc)

        def batch(first, _):
            base = first * BATCH
            for i in range(BATCH):
                arrive(meta, outs, slots, j, base + i, right_v, held, sems)
            terms = []
            for i in range(BATCH):
                at = j * slots + base + i
                live = base + i < count
                high, low = halves(dot(turned[j], group[meta[at], 0]))
                back = dot(high, pair_h[at]) + dot(high, pair_l[at]) + dot(low, pair_h[at])
                back = jnp.where(live, back, 0.0).astype(BF)
                terms.append(dot_nt(jnp.where(live, held[at], jnp.zeros_like(held[at])), back))
            acc[...] += (terms[0] + terms[1]) + (terms[2] + terms[3])
            return 0

        lax.fori_loop(0, (count + BATCH - 1) // BATCH, batch, 0)
        for step, out in enumerate((own, send1, send2, send3)):
            there = lax.rem(y + step, YS)
            for block in range(zs):
                start = pl.multiple_of((block * YS + there) * rows, rows)
                out[block, j] = acc[pl.ds(start, rows)].astype(out.dtype)
        return 0

    lax.fori_loop(0, outs, tile, 0)


def shift_y(array, step, zs):
    pairs = [(z * YS + y, z * YS + (y + step) % YS) for z in range(zs) for y in range(YS)]
    return lax.ppermute(array, "inner", pairs)


def over_z(array, zs):
    groups = [[z * YS + y for z in range(zs)] for y in range(YS)]
    return lax.all_to_all(array, "inner", 0, 0, tiled=True, axis_index_groups=groups)


def params():
    return pltpu.CompilerParams(vmem_limit_bytes=20 << 20)


def body(left_u, left_v, right_u, right_v, sketch, tile_index, slot_mask):
    inner = lax.axis_index("inner")
    zs = lax.axis_size("inner") // YS
    z, y = inner // YS, inner % YS
    outs, slots = tile_index.shape
    tiles = lax.axis_size("cols")
    meta = jnp.concatenate([
        (tile_index - inner * tiles).reshape(-1), jnp.sum(slot_mask, axis=1), y[None]
    ]).astype(jnp.int32)
    shape = jax.ShapeDtypeStruct
    square = shape((outs * slots, R, R), BF)
    fetched = [VMEM((outs * slots, NB, R), BF)]
    sems = [pltpu.SemaphoreType.DMA((outs * slots,))]

    group = lax.all_gather(jnp.stack([left_u, left_v], 1), "cols", axis=0, tiled=True)
    probe_h, probe_l = pl.pallas_call(
        functools.partial(probe_kernel, outs, slots),
        out_shape=(square, square),
        in_specs=[in_smem(), in_place(), in_vmem()],
        out_specs=(in_vmem(),) * 2,
        scratch_shapes=fetched + sems,
        compiler_params=params(),
        cost_estimate=pl.CostEstimate(flops=outs * slots * 2 * NB * R * R, bytes_accessed=6 << 20, transcendentals=0),
        name="probe",
    )(meta, right_v, sketch)
    own, send1, send2, send3, pair_h, pair_l = pl.pallas_call(
        functools.partial(forward_kernel, outs, slots),
        out_shape=(shape((NB, R), F32),) + (shape((NB, R), BF),) * 3 + (square, square),
        in_specs=[in_smem(), in_place()] + [in_vmem()] * 3,
        out_specs=(in_vmem(),) * 6,
        scratch_shapes=fetched + [VMEM((tiles, R, NB), BF), VMEM((NB, R), F32)] + sems,
        compiler_params=params(),
        name="forward",
    )(meta, right_u, group, probe_h, probe_l)
    total = own
    for step, send in enumerate((send1, send2, send3)):
        total = total + shift_y(send, step + 1, zs).astype(F32)
    rows = NB // zs
    mine = jnp.sum(over_z(total.reshape(zs, rows, R), zs), axis=0)
    summed = over_z(jnp.broadcast_to(mine[None], (zs, rows, R)), zs).reshape(1, NB, R)
    gram = jnp.einsum("ona,onb->oab", summed, summed, precision=HIGH)
    factor = jnp.linalg.cholesky(gram)
    solved = jax.scipy.linalg.solve_triangular(factor, jnp.swapaxes(summed, 1, 2), lower=True)
    ortho = jnp.swapaxes(solved, 1, 2)[0]
    high, low = halves(ortho)
    out_rows = NB // (zs * YS)
    messages = []
    for step in range(YS):
        start = (z * YS + (y + step) % YS) * out_rows
        kept = [lax.dynamic_slice_in_dim(half, start, out_rows, 0) for half in (high, low)]
        message = jnp.concatenate([high] + kept)
        messages.append(shift_y(message, step, zs) if step else message)
    pieces = (zs, outs, out_rows, R)
    own, send1, send2, send3, basis = pl.pallas_call(
        functools.partial(backward_kernel, outs, slots, zs),
        out_shape=(shape(pieces, F32),) + (shape(pieces, BF),) * 3 + (shape((outs, out_rows, R), F32),),
        in_specs=[in_smem(), in_place()] + [in_vmem()] * 7,
        out_specs=(in_vmem(),) * 5,
        scratch_shapes=fetched + [VMEM((outs, R, NB), BF), VMEM((NB, R), F32)] + sems,
        compiler_params=params(),
        name="backward",
    )(meta, right_v, group, pair_h, pair_l, *messages)
    part = own
    for step, send in enumerate((send1, send2, send3)):
        part = part + shift_y(send, step + 1, zs).astype(F32)
    coeff = jnp.sum(over_z(part, zs), axis=0)
    return (basis, coeff)


def solution(mesh):
    return jax.shard_map(
        body,
        mesh=mesh,
        in_specs=(
            P(("inner", "cols"), None, None),
            P(("inner", "cols"), None, None),
            P("cols", "inner", None, None),
            P("cols", "inner", None, None),
            P("cols", None, None),
            P("cols", "inner"),
            P("cols", "inner"),
        ),
        out_specs=(P("cols", "inner", None), P("cols", "inner", None)),
        check_vma=False,
    )
```

```python
import functools
import math

import jax
import jax.numpy as jnp
from jax import lax
from jax.experimental import pallas as pl
from jax.experimental.pallas import tpu as pltpu
from jax.sharding import PartitionSpec as P

NB = 512
R = 128
YS = 4
BATCH = 4
HIGH = lax.Precision.HIGHEST
BF = jnp.bfloat16
F32 = jnp.float32
VMEM = pltpu.VMEM
NN = (((1,), (0,)), ((), ()))
NT = (((1,), (1,)), ((), ()))
TN = (((0,), (0,)), ((), ()))


def dot(a, b):
    return jnp.dot(a, b, preferred_element_type=F32)


def dot_nt(a, b):
    return lax.dot_general(a, b, NT, preferred_element_type=F32)


def halves(a):
    high = a.astype(BF)
    return high, (a - high.astype(F32)).astype(BF)


def in_vmem():
    return pl.BlockSpec(memory_space=VMEM)


def in_place():
    return pl.BlockSpec(memory_space=pltpu.HBM)


def in_smem():
    return pl.BlockSpec(memory_space=pltpu.SMEM)


def fetch(meta, outs, slots, source, held, sems):
    def tile(j, _):
        def one(s, _):
            pltpu.make_async_copy(source.at[j, s], held.at[j * slots + s], sems.at[j * slots + s]).start()
            return 0

        lax.fori_loop(0, meta[outs * slots + j], one, 0)
        return 0

    lax.fori_loop(0, outs, tile, 0)


def arrive(meta, outs, slots, j, s, source, held, sems):
    @pl.when(s < meta[outs * slots + j])
    def _():
        pltpu.make_async_copy(source.at[j, s], held.at[j * slots + s], sems.at[j * slots + s]).wait()


def probe_kernel(outs, slots, meta, right_v, sketch, probe_h, probe_l, held, sems):
    fetch(meta, outs, slots, right_v, held, sems)

    def tile(j, _):
        turned = sketch[j].T

        def batch(first, _):
            base = first * BATCH
            for i in range(BATCH):
                arrive(meta, outs, slots, j, base + i, right_v, held, sems)
            for i in range(BATCH):
                at = j * slots + base + i
                high, low = halves(dot(turned, held[at]))
                probe_h[at] = high
                probe_l[at] = low
            return 0

        lax.fori_loop(0, (meta[outs * slots + j] + BATCH - 1) // BATCH, batch, 0)
        return 0

    lax.fori_loop(0, outs, tile, 0)


def tile_ids(meta, at, tiles):
    me = meta[at]
    return [lax.rem(me + 2 * hop, tiles) ^ flip for flip in (0, 1) for hop in (0, tiles // 2 - 1, 1, 2)]


def pair_kernel(outs, slots, meta, right_u, probe_h, probe_l, *rest):
    parts, (pair_h, pair_l, mixing, held, turned, sems) = rest[:-6], rest[-6:]
    fetch(meta, outs, slots, right_u, held, sems)
    for k, part in zip(tile_ids(meta, outs * slots + outs + 2, len(parts)), parts):
        turned[k] = part[0].T

    def tile(j, _):
        count = meta[outs * slots + j]

        def batch(first, _):
            base = first * BATCH
            for i in range(BATCH):
                arrive(meta, outs, slots, j, base + i, right_u, held, sems)
            for i in range(BATCH):
                at = j * slots + base + i
                high, low = halves(dot(turned[meta[at]], held[at]))
                pair_h[at] = high
                pair_l[at] = low
                mixed = dot_nt(high, probe_h[at]) + dot_nt(high, probe_l[at]) + dot_nt(low, probe_h[at])
                mixing[at] = jnp.where(base + i < count, mixed, 0.0).astype(BF)
            return 0

        lax.fori_loop(0, (count + BATCH - 1) // BATCH, batch, 0)
        return 0

    lax.fori_loop(0, outs, tile, 0)


def sketch_kernel(outs, slots, meta, mixing, *rest):
    parts, (own, send1, send2, send3, group, acc) = rest[:-6], rest[-6:]
    for k, part in zip(tile_ids(meta, outs * slots + outs + 2, len(parts)), parts):
        group[k] = part[0]
    y = meta[outs * slots + outs]

    def tile(order, _):
        j = lax.rem(y + 1 + order, YS)
        acc[...] = jnp.zeros_like(acc)

        def batch(first, _):
            base = first * BATCH
            at = [j * slots + base + i for i in range(BATCH)]
            terms = [dot(group[meta[slot]], mixing[slot]) for slot in at]
            acc[...] += (terms[0] + terms[1]) + (terms[2] + terms[3])
            return 0

        lax.fori_loop(0, (meta[outs * slots + j] + BATCH - 1) // BATCH, batch, 0)
        for place, out in enumerate((send1, send2, send3, own)):
            @pl.when(order == place)
            def _():
                out[...] = acc[...].astype(out.dtype)
        return 0

    lax.fori_loop(0, YS, tile, 0)


def exact(a, b, dims):
    return lax.dot_general(a, b, dims, precision=HIGH, preferred_element_type=F32)


def inverse_factor(block):
    n = block.shape[0]
    lanes = 2 * n
    same = lax.broadcasted_iota(jnp.int32, (n, n), 0) == lax.broadcasted_iota(jnp.int32, (n, n), 1)
    full = jnp.concatenate([same.astype(F32), block], axis=1)
    x = [full[8 * i:8 * i + 8] for i in range(n // 8)]
    sub = lax.broadcasted_iota(jnp.int32, (8, lanes), 0)

    def wide(v):
        return jnp.broadcast_to(v, (8, lanes))

    for k in range(0, n, 2):
        i0, r = k // 8, k % 8
        first, second = wide(x[i0][r:r + 1]), wide(x[i0][r + 1:r + 2])
        a, b = wide(first[:, n + k:n + k + 1]), wide(first[:, n + k + 1:n + k + 2])
        c = wide(second[:, n + k + 1:n + k + 2])
        scale = 1.0 / (a * c - b * b)
        p, q = (c * first - b * second) * scale, (a * second - b * first) * scale
        for i in range(i0, n // 8):
            if i == i0 and r == 6:
                continue
            step = wide(x[i][:, n + k:n + k + 1]) * p + wide(x[i][:, n + k + 1:n + k + 2]) * q
            if i == i0:
                step = jnp.where(sub > r + 1, step, 0.0)
            x[i] = x[i] - step
    full = jnp.concatenate(x, axis=0)
    row = lax.broadcasted_iota(jnp.int32, (n, lanes), 0)
    lane = lax.broadcasted_iota(jnp.int32, (n, lanes), 1) - n
    diag = jnp.broadcast_to(jnp.sum(jnp.where(lane == row, full, 0.0), axis=1, keepdims=True), (n, lanes))
    side = jnp.broadcast_to(jnp.sum(jnp.where(lane == row + 1, full, 0.0), axis=1, keepdims=True), (n, lanes))
    ratio = side / diag
    odd = row % 2 == 1
    full = jnp.where(odd, full - pltpu.roll(ratio * full, 1, 0), full)
    diag = jnp.where(odd, diag - pltpu.roll(ratio * side, 1, 0), diag)
    return (full * lax.rsqrt(diag))[:, :n]


def inverse_cholesky(gram):
    half = gram.shape[0] // 2
    upper = inverse_factor(gram[:half, :half])
    across = exact(upper, gram[:half, half:], NN)
    lower = inverse_factor(gram[half:, half:] - exact(across, across, TN))
    corner = -exact(lower, exact(across, upper, TN), NN)
    top = jnp.concatenate([upper, jnp.zeros_like(upper)], axis=1)
    return jnp.concatenate([top, jnp.concatenate([corner, lower], axis=1)], axis=0)


def ortho_kernel(outs, slots, zs, meta, blocks, msg0, msg1, msg2, msg3, ortho):
    y, z = meta[outs * slots + outs], meta[outs * slots + outs + 1]
    rows = NB // (zs * YS)
    summed = blocks[...].reshape(NB, R)
    ortho[...] = exact(summed, inverse_cholesky(exact(summed, summed, TN)), NT)
    high = ortho[...].astype(BF)
    for step, msg in enumerate((msg0, msg1, msg2, msg3)):
        start = pl.multiple_of((z * YS + lax.rem(y + step, YS)) * rows, rows)
        top, low = halves(ortho[pl.ds(start, rows)])
        msg[:NB] = high
        msg[NB:NB + rows] = top
        msg[NB + rows:] = low


def backward_kernel(outs, slots, zs, meta, right_v, group, pair_h, pair_l, msg0, msg1, msg2, msg3,
                    own, send1, send2, send3, basis, held, turned, acc, sems):
    fetch(meta, outs, slots, right_v, held, sems)
    y = meta[outs * slots + outs]
    rows = NB // (zs * YS)
    for step, msg in enumerate((msg0, msg1, msg2, msg3)):
        j = lax.rem(y + YS - step, YS)
        turned[j] = msg[:NB].T
        kept = msg[NB:NB + rows].astype(F32) + msg[NB + rows:].astype(F32)
        basis[j] = kept * math.sqrt(NB)

    def tile(j, _):
        count = meta[outs * slots + j]
        acc[...] = jnp.zeros_like(acc)

        def batch(first, _):
            base = first * BATCH
            for i in range(BATCH):
                arrive(meta, outs, slots, j, base + i, right_v, held, sems)
            terms = []
            for i in range(BATCH):
                at = j * slots + base + i
                live = base + i < count
                high, low = halves(dot(turned[j], group[meta[at]]))
                back = dot(high, pair_h[at]) + dot(high, pair_l[at]) + dot(low, pair_h[at])
                back = jnp.where(live, back, 0.0).astype(BF)
                terms.append(dot_nt(jnp.where(live, held[at], jnp.zeros_like(held[at])), back))
            acc[...] += (terms[0] + terms[1]) + (terms[2] + terms[3])
            return 0

        lax.fori_loop(0, (count + BATCH - 1) // BATCH, batch, 0)
        for step, out in enumerate((own, send1, send2, send3)):
            there = lax.rem(y + step, YS)
            for block in range(zs):
                start = pl.multiple_of((block * YS + there) * rows, rows)
                out[block, j] = acc[pl.ds(start, rows)].astype(out.dtype)
        return 0

    lax.fori_loop(0, outs, tile, 0)


def shift_y(array, step, zs):
    pairs = [(z * YS + y, z * YS + (y + step) % YS) for z in range(zs) for y in range(YS)]
    return lax.ppermute(array, "inner", pairs)


def gather(array, tiles, forward):
    def hop(value, step):
        return lax.ppermute(value, "cols", [(i, (i + 2 * step) % tiles) for i in range(tiles)])

    left, right = hop(array, 1), hop(array, -1)
    far = hop(left, 1) if forward else hop(right, -1)
    mine = [array, left, right, far]
    return mine + [lax.ppermute(value, "cols", [(i, i ^ 1) for i in range(tiles)]) for value in mine]


def over_z(array, zs):
    groups = [[z * YS + y for z in range(zs)] for y in range(YS)]
    return lax.all_to_all(array, "inner", 0, 0, tiled=True, axis_index_groups=groups)


def params():
    return pltpu.CompilerParams(vmem_limit_bytes=20 << 20)


def body(left_u, left_v, right_u, right_v, sketch, tile_index, slot_mask):
    inner = lax.axis_index("inner")
    zs = lax.axis_size("inner") // YS
    z, y = inner // YS, inner % YS
    outs, slots = tile_index.shape
    tiles = lax.axis_size("cols")
    meta = jnp.concatenate([
        (tile_index - inner * tiles).reshape(-1), jnp.sum(slot_mask, axis=1),
        jnp.stack([y, z, lax.axis_index("cols")]),
    ]).astype(jnp.int32)
    shape = jax.ShapeDtypeStruct
    square = shape((outs * slots, R, R), BF)
    fetched = [VMEM((outs * slots, NB, R), BF)]
    sems = [pltpu.SemaphoreType.DMA((outs * slots,))]

    right_u = pltpu.with_memory_space_constraint(right_u, pltpu.HBM)
    right_v = pltpu.with_memory_space_constraint(right_v, pltpu.HBM)
    group_v = gather(left_v, tiles, False)
    group_u = gather(left_u, tiles, True)
    unit = 2 * NB * R * R

    def cost(units, mib):
        return pl.CostEstimate(flops=int(units * unit), bytes_accessed=mib << 20, transcendentals=0)

    probe_h, probe_l = pl.pallas_call(
        functools.partial(probe_kernel, outs, slots),
        out_shape=(square, square),
        in_specs=[in_smem(), in_place(), in_vmem()],
        out_specs=(in_vmem(),) * 2,
        scratch_shapes=fetched + sems,
        compiler_params=params(),
        cost_estimate=cost(outs * slots, 6),
        name="probe",
    )(meta, right_v, sketch)
    pair_h, pair_l, mixing = pl.pallas_call(
        functools.partial(pair_kernel, outs, slots),
        out_shape=(square,) * 3,
        in_specs=[in_smem(), in_place()] + [in_vmem()] * (2 + tiles),
        out_specs=(in_vmem(),) * 3,
        scratch_shapes=fetched + [VMEM((tiles, R, NB), BF)] + sems,
        compiler_params=params(),
        cost_estimate=cost(outs * slots * 1.75, 10),
        name="pair",
    )(meta, right_u, probe_h, probe_l, *group_v)
    own, send1, send2, send3, group = pl.pallas_call(
        functools.partial(sketch_kernel, outs, slots),
        out_shape=(shape((NB, R), F32),) + (shape((NB, R), BF),) * 3 + (shape((tiles, NB, R), BF),),
        in_specs=[in_smem()] + [in_vmem()] * (1 + tiles),
        out_specs=(in_vmem(),) * 5,
        scratch_shapes=[VMEM((NB, R), F32)],
        compiler_params=params(),
        cost_estimate=cost(outs * slots, 4),
        name="sketch",
    )(meta, mixing, *group_u)
    total = own
    for step, send in enumerate((send1, send2, send3)):
        total = total + shift_y(send, step + 1, zs).astype(F32)
    rows = NB // zs
    mine = jnp.sum(over_z(total.reshape(zs, rows, R), zs), axis=0)
    summed = over_z(jnp.broadcast_to(mine[None], (zs, rows, R)), zs)
    out_rows = NB // (zs * YS)
    messages = pl.pallas_call(
        functools.partial(ortho_kernel, outs, slots, zs),
        out_shape=(shape((NB + 2 * out_rows, R), BF),) * YS,
        in_specs=[in_smem(), in_vmem()],
        out_specs=(in_vmem(),) * YS,
        scratch_shapes=[VMEM((NB, R), F32)],
        compiler_params=params(),
        cost_estimate=cost(13, 1),
        name="ortho",
    )(meta, summed)
    messages = [shift_y(message, step, zs) if step else message for step, message in enumerate(messages)]
    pieces = (zs, outs, out_rows, R)
    own, send1, send2, send3, basis = pl.pallas_call(
        functools.partial(backward_kernel, outs, slots, zs),
        out_shape=(shape(pieces, F32),) + (shape(pieces, BF),) * 3 + (shape((outs, out_rows, R), F32),),
        in_specs=[in_smem(), in_place()] + [in_vmem()] * (3 + YS),
        out_specs=(in_vmem(),) * 5,
        scratch_shapes=fetched + [VMEM((outs, R, NB), BF), VMEM((NB, R), F32)] + sems,
        compiler_params=params(),
        cost_estimate=cost(outs * slots * 2.75, 8),
        name="backward",
    )(meta, right_v, group, pair_h, pair_l, *messages)
    part = own
    for step, send in enumerate((send1, send2, send3)):
        part = part + shift_y(send, step + 1, zs).astype(F32)
    coeff = jnp.sum(over_z(part, zs), axis=0)
    return (basis, coeff)


def solution(mesh):
    return jax.shard_map(
        body,
        mesh=mesh,
        in_specs=(
            P(("inner", "cols"), None, None),
            P(("inner", "cols"), None, None),
            P("cols", "inner", None, None),
            P("cols", "inner", None, None),
            P("cols", None, None),
            P("cols", "inner"),
            P("cols", "inner"),
        ),
        out_specs=(P("cols", "inner", None), P("cols", "inner", None)),
        check_vma=False,
    )
```

```python
import functools
import math

import jax
import jax.numpy as jnp
from jax import lax
from jax.experimental import pallas as pl
from jax.experimental.pallas import tpu as pltpu
from jax.sharding import PartitionSpec as P

NB = 512
R = 128
YS = 4
BATCH = 4
HIGH = lax.Precision.HIGHEST
BF = jnp.bfloat16
F32 = jnp.float32
VMEM = pltpu.VMEM
NN = (((1,), (0,)), ((), ()))
NT = (((1,), (1,)), ((), ()))
TN = (((0,), (0,)), ((), ()))


def dot(a, b):
    return jnp.dot(a, b, preferred_element_type=F32)


def dot_nt(a, b):
    return lax.dot_general(a, b, NT, preferred_element_type=F32)


def halves(a):
    high = a.astype(BF)
    return high, (a - high.astype(F32)).astype(BF)


def in_vmem():
    return pl.BlockSpec(memory_space=VMEM)


def in_place():
    return pl.BlockSpec(memory_space=pltpu.HBM)


def in_smem():
    return pl.BlockSpec(memory_space=pltpu.SMEM)


def fetch(meta, outs, slots, source, held, sems):
    def tile(j, _):
        def one(s, _):
            pltpu.make_async_copy(source.at[j, s], held.at[j * slots + s], sems.at[j * slots + s]).start()
            return 0

        lax.fori_loop(0, meta[outs * slots + j], one, 0)
        return 0

    lax.fori_loop(0, outs, tile, 0)


def arrive(meta, outs, slots, j, s, source, held, sems):
    @pl.when(s < meta[outs * slots + j])
    def _():
        pltpu.make_async_copy(source.at[j, s], held.at[j * slots + s], sems.at[j * slots + s]).wait()


def probe_kernel(outs, slots, meta, right_v, sketch, probe_h, probe_l, held, sems):
    fetch(meta, outs, slots, right_v, held, sems)

    def tile(j, _):
        turned = sketch[j].T

        def batch(first, _):
            base = first * BATCH
            for i in range(BATCH):
                arrive(meta, outs, slots, j, base + i, right_v, held, sems)
            for i in range(BATCH):
                at = j * slots + base + i
                high, low = halves(dot(turned, held[at]))
                probe_h[at] = high
                probe_l[at] = low
            return 0

        lax.fori_loop(0, (meta[outs * slots + j] + BATCH - 1) // BATCH, batch, 0)
        return 0

    lax.fori_loop(0, outs, tile, 0)


def tile_ids(meta, at, tiles):
    me = meta[at]
    return [lax.rem(me + 2 * hop, tiles) ^ flip for flip in (0, 1) for hop in (0, tiles // 2 - 1, 1, 2)]


def pair_kernel(outs, slots, meta, right_u, probe_h, probe_l, *rest):
    parts, (pair_h, pair_l, mixing, held, turned, sems) = rest[:-6], rest[-6:]
    fetch(meta, outs, slots, right_u, held, sems)
    for k, part in zip(tile_ids(meta, outs * slots + outs + 2, len(parts)), parts):
        turned[k] = part[0].T

    def tile(j, _):
        count = meta[outs * slots + j]

        def batch(first, _):
            base = first * BATCH
            for i in range(BATCH):
                arrive(meta, outs, slots, j, base + i, right_u, held, sems)
            for i in range(BATCH):
                at = j * slots + base + i
                high, low = halves(dot(turned[meta[at]], held[at]))
                pair_h[at] = high
                pair_l[at] = low
                mixed = dot_nt(high, probe_h[at]) + dot_nt(high, probe_l[at]) + dot_nt(low, probe_h[at])
                mixing[at] = jnp.where(base + i < count, mixed, 0.0).astype(BF)
            return 0

        lax.fori_loop(0, (count + BATCH - 1) // BATCH, batch, 0)
        return 0

    lax.fori_loop(0, outs, tile, 0)


def sketch_kernel(outs, slots, meta, mixing, *rest):
    parts, (own, send1, send2, send3, group, acc) = rest[:-6], rest[-6:]
    for k, part in zip(tile_ids(meta, outs * slots + outs + 2, len(parts)), parts):
        group[k] = part[0]
    y = meta[outs * slots + outs]

    def tile(order, _):
        j = lax.rem(y + 1 + order, YS)
        acc[...] = jnp.zeros_like(acc)

        def batch(first, _):
            base = first * BATCH
            at = [j * slots + base + i for i in range(BATCH)]
            terms = [dot(group[meta[slot]], mixing[slot]) for slot in at]
            acc[...] += (terms[0] + terms[1]) + (terms[2] + terms[3])
            return 0

        lax.fori_loop(0, (meta[outs * slots + j] + BATCH - 1) // BATCH, batch, 0)
        for place, out in enumerate((send1, send2, send3, own)):
            @pl.when(order == place)
            def _():
                out[...] = acc[...].astype(out.dtype)
        return 0

    lax.fori_loop(0, YS, tile, 0)


def exact(a, b, dims):
    return lax.dot_general(a, b, dims, precision=HIGH, preferred_element_type=F32)


def inverse_factor(block):
    n = block.shape[0]
    lanes = 2 * n
    same = lax.broadcasted_iota(jnp.int32, (n, n), 0) == lax.broadcasted_iota(jnp.int32, (n, n), 1)
    full = jnp.concatenate([same.astype(F32), block], axis=1)
    x = [full[8 * i:8 * i + 8] for i in range(n // 8)]
    sub = lax.broadcasted_iota(jnp.int32, (8, lanes), 0)

    def wide(v):
        return jnp.broadcast_to(v, (8, lanes))

    for k in range(0, n, 2):
        i0, r = k // 8, k % 8
        first, second = wide(x[i0][r:r + 1]), wide(x[i0][r + 1:r + 2])
        a, b = wide(first[:, n + k:n + k + 1]), wide(first[:, n + k + 1:n + k + 2])
        c = wide(second[:, n + k + 1:n + k + 2])
        scale = 1.0 / (a * c - b * b)
        p, q = (c * first - b * second) * scale, (a * second - b * first) * scale
        for i in range(i0, n // 8):
            if i == i0 and r == 6:
                continue
            step = wide(x[i][:, n + k:n + k + 1]) * p + wide(x[i][:, n + k + 1:n + k + 2]) * q
            if i == i0:
                step = jnp.where(sub > r + 1, step, 0.0)
            x[i] = x[i] - step
    full = jnp.concatenate(x, axis=0)
    row = lax.broadcasted_iota(jnp.int32, (n, lanes), 0)
    lane = lax.broadcasted_iota(jnp.int32, (n, lanes), 1) - n
    diag = jnp.broadcast_to(jnp.sum(jnp.where(lane == row, full, 0.0), axis=1, keepdims=True), (n, lanes))
    side = jnp.broadcast_to(jnp.sum(jnp.where(lane == row + 1, full, 0.0), axis=1, keepdims=True), (n, lanes))
    ratio = side / diag
    odd = row % 2 == 1
    full = jnp.where(odd, full - pltpu.roll(ratio * full, 1, 0), full)
    diag = jnp.where(odd, diag - pltpu.roll(ratio * side, 1, 0), diag)
    return (full * lax.rsqrt(diag))[:, :n]


def inverse_cholesky(gram):
    half = gram.shape[0] // 2
    upper = inverse_factor(gram[:half, :half])
    across = exact(upper, gram[:half, half:], NN)
    lower = inverse_factor(gram[half:, half:] - exact(across, across, TN))
    corner = -exact(lower, exact(across, upper, TN), NN)
    top = jnp.concatenate([upper, jnp.zeros_like(upper)], axis=1)
    return jnp.concatenate([top, jnp.concatenate([corner, lower], axis=1)], axis=0)


def ortho_kernel(outs, slots, zs, meta, blocks, msg0, msg1, msg2, msg3, ortho):
    y, z = meta[outs * slots + outs], meta[outs * slots + outs + 1]
    rows = NB // (zs * YS)
    summed = blocks[...].reshape(NB, R)
    ortho[...] = exact(summed, inverse_cholesky(exact(summed, summed, TN)), NT)
    high = ortho[...].astype(BF)
    for step, msg in enumerate((msg0, msg1, msg2, msg3)):
        start = pl.multiple_of((z * YS + lax.rem(y + step, YS)) * rows, rows)
        top, low = halves(ortho[pl.ds(start, rows)])
        msg[:NB] = high
        msg[NB:NB + rows] = top
        msg[NB + rows:] = low


def backward_kernel(outs, slots, zs, meta, right_v, group, pair_h, pair_l, msg0, msg1, msg2, msg3,
                    own, send1, send2, send3, basis, held, turned, acc, sems):
    fetch(meta, outs, slots, right_v, held, sems)
    y = meta[outs * slots + outs]
    rows = NB // (zs * YS)
    for step, msg in enumerate((msg0, msg1, msg2, msg3)):
        j = lax.rem(y + YS - step, YS)
        turned[j] = msg[:NB].T
        kept = msg[NB:NB + rows].astype(F32) + msg[NB + rows:].astype(F32)
        basis[j] = kept * math.sqrt(NB)

    def tile(j, _):
        count = meta[outs * slots + j]
        acc[...] = jnp.zeros_like(acc)

        def batch(first, _):
            base = first * BATCH
            for i in range(BATCH):
                arrive(meta, outs, slots, j, base + i, right_v, held, sems)
            terms = []
            for i in range(BATCH):
                at = j * slots + base + i
                live = base + i < count
                high, low = halves(dot(turned[j], group[meta[at]]))
                back = dot(high, pair_h[at]) + dot(high, pair_l[at]) + dot(low, pair_h[at])
                back = jnp.where(live, back, 0.0).astype(BF)
                terms.append(dot_nt(jnp.where(live, held[at], jnp.zeros_like(held[at])), back))
            acc[...] += (terms[0] + terms[1]) + (terms[2] + terms[3])
            return 0

        lax.fori_loop(0, (count + BATCH - 1) // BATCH, batch, 0)
        for step, out in enumerate((own, send1, send2, send3)):
            there = lax.rem(y + step, YS)
            for block in range(zs):
                start = pl.multiple_of((block * YS + there) * rows, rows)
                out[block, j] = acc[pl.ds(start, rows)].astype(out.dtype)
        return 0

    lax.fori_loop(0, outs, tile, 0)


def shift_y(array, step, zs):
    pairs = [(z * YS + y, z * YS + (y + step) % YS) for z in range(zs) for y in range(YS)]
    return lax.ppermute(array, "inner", pairs)


def hop(value, step, tiles):
    return lax.ppermute(value, "cols", [(i, (i + 2 * step) % tiles) for i in range(tiles)])


def swap(value, tiles):
    return lax.ppermute(value, "cols", [(i, i ^ 1) for i in range(tiles)])


def over_z(array, zs):
    groups = [[z * YS + y for z in range(zs)] for y in range(YS)]
    return lax.all_to_all(array, "inner", 0, 0, tiled=True, axis_index_groups=groups)


def params():
    return pltpu.CompilerParams(vmem_limit_bytes=20 << 20)


def body(left_u, left_v, right_u, right_v, sketch, tile_index, slot_mask):
    inner = lax.axis_index("inner")
    zs = lax.axis_size("inner") // YS
    z, y = inner // YS, inner % YS
    outs, slots = tile_index.shape
    tiles = lax.axis_size("cols")
    meta = jnp.concatenate([
        (tile_index - inner * tiles).reshape(-1), jnp.sum(slot_mask, axis=1),
        jnp.stack([y, z, lax.axis_index("cols")]),
    ]).astype(jnp.int32)
    shape = jax.ShapeDtypeStruct
    square = shape((outs * slots, R, R), BF)
    fetched = [VMEM((outs * slots, NB, R), BF)]
    sems = [pltpu.SemaphoreType.DMA((outs * slots,))]

    right_u = pltpu.with_memory_space_constraint(right_u, pltpu.HBM)
    right_v = pltpu.with_memory_space_constraint(right_v, pltpu.HBM)
    unit = 2 * NB * R * R

    def cost(units, mib):
        return pl.CostEstimate(flops=int(units * unit), bytes_accessed=mib << 20, transcendentals=0)

    probe_h, probe_l = pl.pallas_call(
        functools.partial(probe_kernel, outs, slots),
        out_shape=(square, square),
        in_specs=[in_smem(), in_place(), in_vmem()],
        out_specs=(in_vmem(),) * 2,
        scratch_shapes=fetched + sems,
        compiler_params=params(),
        cost_estimate=cost(outs * slots, 6),
        name="probe",
    )(meta, right_v, sketch)
    near = [hop(left_v, 1, tiles), hop(left_v, -1, tiles)]
    *near, probe_h, probe_l, left_u = lax.optimization_barrier((*near, probe_h, probe_l, left_u))
    group_v = [left_v, *near, hop(near[1], -1, tiles)]
    group_v += [swap(value, tiles) for value in group_v]
    near = [hop(left_u, 1, tiles), hop(left_u, -1, tiles)]
    group_u = [left_u, *near]
    other_u = [swap(value, tiles) for value in group_u]
    far_u = hop(near[0], 1, tiles)
    pair_h, pair_l, mixing = pl.pallas_call(
        functools.partial(pair_kernel, outs, slots),
        out_shape=(square,) * 3,
        in_specs=[in_smem(), in_place()] + [in_vmem()] * (2 + tiles),
        out_specs=(in_vmem(),) * 3,
        scratch_shapes=fetched + [VMEM((tiles, R, NB), BF)] + sems,
        compiler_params=params(),
        cost_estimate=cost(outs * slots * 1.75, 10),
        name="pair",
    )(meta, right_u, probe_h, probe_l, *group_v)
    far_u, mixing = lax.optimization_barrier((far_u, mixing))
    group_u += [far_u, *other_u, swap(far_u, tiles)]
    own, send1, send2, send3, group = pl.pallas_call(
        functools.partial(sketch_kernel, outs, slots),
        out_shape=(shape((NB, R), F32),) + (shape((NB, R), BF),) * 3 + (shape((tiles, NB, R), BF),),
        in_specs=[in_smem()] + [in_vmem()] * (1 + tiles),
        out_specs=(in_vmem(),) * 5,
        scratch_shapes=[VMEM((NB, R), F32)],
        compiler_params=params(),
        cost_estimate=cost(outs * slots, 4),
        name="sketch",
    )(meta, mixing, *group_u)
    total = own
    for step, send in enumerate((send1, send2, send3)):
        total = total + shift_y(send, step + 1, zs).astype(F32)
    rows = NB // zs
    mine = jnp.sum(over_z(total.reshape(zs, rows, R), zs), axis=0)
    summed = over_z(jnp.broadcast_to(mine[None], (zs, rows, R)), zs)
    out_rows = NB // (zs * YS)
    messages = pl.pallas_call(
        functools.partial(ortho_kernel, outs, slots, zs),
        out_shape=(shape((NB + 2 * out_rows, R), BF),) * YS,
        in_specs=[in_smem(), in_vmem()],
        out_specs=(in_vmem(),) * YS,
        scratch_shapes=[VMEM((NB, R), F32)],
        compiler_params=params(),
        cost_estimate=cost(13, 1),
        name="ortho",
    )(meta, summed)
    messages = [shift_y(message, step, zs) if step else message for step, message in enumerate(messages)]
    pieces = (zs, outs, out_rows, R)
    own, send1, send2, send3, basis = pl.pallas_call(
        functools.partial(backward_kernel, outs, slots, zs),
        out_shape=(shape(pieces, F32),) + (shape(pieces, BF),) * 3 + (shape((outs, out_rows, R), F32),),
        in_specs=[in_smem(), in_place()] + [in_vmem()] * (3 + YS),
        out_specs=(in_vmem(),) * 5,
        scratch_shapes=fetched + [VMEM((outs, R, NB), BF), VMEM((NB, R), F32)] + sems,
        compiler_params=params(),
        cost_estimate=cost(outs * slots * 2.75, 8),
        name="backward",
    )(meta, right_v, group, pair_h, pair_l, *messages)
    part = own
    for step, send in enumerate((send1, send2, send3)):
        part = part + shift_y(send, step + 1, zs).astype(F32)
    coeff = jnp.sum(over_z(part, zs), axis=0)
    return (basis, coeff)


def solution(mesh):
    return jax.shard_map(
        body,
        mesh=mesh,
        in_specs=(
            P(("inner", "cols"), None, None),
            P(("inner", "cols"), None, None),
            P("cols", "inner", None, None),
            P("cols", "inner", None, None),
            P("cols", None, None),
            P("cols", "inner"),
            P("cols", "inner"),
        ),
        out_specs=(P("cols", "inner", None), P("cols", "inner", None)),
        check_vma=False,
    )
```

```python
import functools
import math

import jax
import jax.numpy as jnp
from jax import lax
from jax.experimental import pallas as pl
from jax.experimental.pallas import tpu as pltpu
from jax.sharding import PartitionSpec as P

NB = 512
R = 128
YS = 4
BATCH = 4
HIGH = lax.Precision.HIGHEST
BF = jnp.bfloat16
F32 = jnp.float32
VMEM = pltpu.VMEM
NN = (((1,), (0,)), ((), ()))
NT = (((1,), (1,)), ((), ()))
TN = (((0,), (0,)), ((), ()))


def dot(a, b):
    return jnp.dot(a, b, preferred_element_type=F32)


def dot_nt(a, b):
    return lax.dot_general(a, b, NT, preferred_element_type=F32)


def halves(a):
    high = a.astype(BF)
    return high, (a - high.astype(F32)).astype(BF)


def in_vmem():
    return pl.BlockSpec(memory_space=VMEM)


def in_place():
    return pl.BlockSpec(memory_space=pltpu.HBM)


def in_smem():
    return pl.BlockSpec(memory_space=pltpu.SMEM)


def fetch(meta, outs, slots, source, held, sems):
    def tile(j, _):
        def one(s, _):
            pltpu.make_async_copy(source.at[j, s], held.at[j * slots + s], sems.at[j * slots + s]).start()
            return 0

        lax.fori_loop(0, meta[outs * slots + j], one, 0)
        return 0

    lax.fori_loop(0, outs, tile, 0)


def arrive(meta, outs, slots, j, s, source, held, sems):
    @pl.when(s < meta[outs * slots + j])
    def _():
        pltpu.make_async_copy(source.at[j, s], held.at[j * slots + s], sems.at[j * slots + s]).wait()


def beside(a, b):
    return jnp.concatenate([a, b], axis=1)


def above(a, b):
    return jnp.concatenate([a, b], axis=0)


def slots_of(j, base, slots, count):
    return [j * slots + jnp.minimum(base + i, count - 1) for i in range(BATCH)]


def probe_kernel(outs, slots, meta, right_u, right_v, sketch, probes, held_u, held, sems_u, sems):
    fetch(meta, outs, slots, right_v, held, sems)
    fetch(meta, outs, slots, right_u, held_u, sems_u)

    def tile(j, _):
        turned = sketch[j].T
        count = meta[outs * slots + j]

        def batch(first, _):
            base = first * BATCH
            for i in range(BATCH):
                arrive(meta, outs, slots, j, base + i, right_v, held, sems)
            at = slots_of(j, base, slots, count)
            products = [dot(turned, held[slot]) for slot in at]
            for slot, product in zip(at, products):
                probes[slot] = beside(*halves(product))
            for i in range(BATCH):
                arrive(meta, outs, slots, j, base + i, right_u, held_u, sems_u)
            return 0

        lax.fori_loop(0, (count + BATCH - 1) // BATCH, batch, 0)
        return 0

    lax.fori_loop(0, outs, tile, 0)


def tile_ids(meta, at, tiles):
    me = meta[at]
    return [lax.rem(me + 2 * hop, tiles) ^ flip for flip in (0, 1) for hop in (0, tiles // 2 - 1, 1, 2)]


def pair_kernel(outs, slots, meta, held, probes, *rest):
    parts, (pairs, mixing, turned) = rest[:-3], rest[-3:]
    for k, part in zip(tile_ids(meta, outs * slots + outs + 2, len(parts)), parts):
        turned[k] = part[0].T

    def tile(j, _):
        count = meta[outs * slots + j]

        def batch(first, _):
            base = first * BATCH
            at = slots_of(j, base, slots, count)
            products = [halves(dot(turned[meta[slot]], held[slot])) for slot in at]
            mixes = []
            for slot, (high, low) in zip(at, products):
                probe = probes[slot]
                mixes.append(dot_nt(high, probe[:, :R]) + dot_nt(high, probe[:, R:]) + dot_nt(low, probe[:, :R]))
            for i in range(BATCH):
                pairs[at[i]] = above(*products[i])
                mixing[j * slots + base + i] = jnp.where(base + i < count, mixes[i], 0.0).astype(BF)
            return 0

        lax.fori_loop(0, (count + BATCH - 1) // BATCH, batch, 0)
        return 0

    lax.fori_loop(0, outs, tile, 0)


def sketch_kernel(outs, slots, meta, mixing, *rest):
    parts, (own, send1, send2, send3, group, acc) = rest[:-6], rest[-6:]
    for k, part in zip(tile_ids(meta, outs * slots + outs + 2, len(parts)), parts):
        group[k] = part[0]
    y = meta[outs * slots + outs]

    def tile(order, _):
        j = lax.rem(y + 1 + order, YS)
        acc[...] = jnp.zeros_like(acc)

        def batch(first, _):
            base = first * BATCH
            at = [j * slots + base + i for i in range(BATCH)]
            tiles = [group[meta[slot]] for slot in at]
            terms = [
                dot(beside(tiles[i], tiles[i + 1]), above(mixing[at[i]], mixing[at[i + 1]])) for i in range(0, BATCH, 2)
            ]
            acc[...] += terms[0] + terms[1]
            return 0

        lax.fori_loop(0, (meta[outs * slots + j] + BATCH - 1) // BATCH, batch, 0)
        for place, out in enumerate((send1, send2, send3, own)):
            @pl.when(order == place)
            def _():
                out[...] = acc[...].astype(out.dtype)
        return 0

    lax.fori_loop(0, YS, tile, 0)


def exact(a, b, dims):
    return lax.dot_general(a, b, dims, precision=HIGH, preferred_element_type=F32)


def inverse_factor(block):
    n = block.shape[0]
    lanes = 2 * n
    same = lax.broadcasted_iota(jnp.int32, (n, n), 0) == lax.broadcasted_iota(jnp.int32, (n, n), 1)
    full = jnp.concatenate([same.astype(F32), block], axis=1)
    x = [full[8 * i:8 * i + 8] for i in range(n // 8)]
    sub = lax.broadcasted_iota(jnp.int32, (8, lanes), 0)

    def wide(v):
        return jnp.broadcast_to(v, (8, lanes))

    for k in range(0, n, 2):
        i0, r = k // 8, k % 8
        first, second = wide(x[i0][r:r + 1]), wide(x[i0][r + 1:r + 2])
        a, b = wide(first[:, n + k:n + k + 1]), wide(first[:, n + k + 1:n + k + 2])
        c = wide(second[:, n + k + 1:n + k + 2])
        scale = 1.0 / (a * c - b * b)
        p, q = (c * first - b * second) * scale, (a * second - b * first) * scale
        for i in range(i0, n // 8):
            if i == i0 and r == 6:
                continue
            step = wide(x[i][:, n + k:n + k + 1]) * p + wide(x[i][:, n + k + 1:n + k + 2]) * q
            if i == i0:
                step = jnp.where(sub > r + 1, step, 0.0)
            x[i] = x[i] - step
    full = jnp.concatenate(x, axis=0)
    row = lax.broadcasted_iota(jnp.int32, (n, lanes), 0)
    lane = lax.broadcasted_iota(jnp.int32, (n, lanes), 1) - n
    diag = jnp.broadcast_to(jnp.sum(jnp.where(lane == row, full, 0.0), axis=1, keepdims=True), (n, lanes))
    side = jnp.broadcast_to(jnp.sum(jnp.where(lane == row + 1, full, 0.0), axis=1, keepdims=True), (n, lanes))
    ratio = side / diag
    odd = row % 2 == 1
    full = jnp.where(odd, full - pltpu.roll(ratio * full, 1, 0), full)
    diag = jnp.where(odd, diag - pltpu.roll(ratio * side, 1, 0), diag)
    return (full * lax.rsqrt(diag))[:, :n]


def inverse_cholesky(gram):
    half = gram.shape[0] // 2
    upper = inverse_factor(gram[:half, :half])
    across = exact(upper, gram[:half, half:], NN)
    lower = inverse_factor(gram[half:, half:] - exact(across, across, TN))
    corner = -exact(lower, exact(across, upper, TN), NN)
    top = jnp.concatenate([upper, jnp.zeros_like(upper)], axis=1)
    return jnp.concatenate([top, jnp.concatenate([corner, lower], axis=1)], axis=0)


def ortho_kernel(outs, slots, zs, meta, blocks, msg0, msg1, msg2, msg3, ortho):
    y, z = meta[outs * slots + outs], meta[outs * slots + outs + 1]
    rows = NB // (zs * YS)
    summed = blocks[...].reshape(NB, R)
    ortho[...] = exact(summed, inverse_cholesky(exact(summed, summed, TN)), NT)
    high = ortho[...].astype(BF)
    for step, msg in enumerate((msg0, msg1, msg2, msg3)):
        start = pl.multiple_of((z * YS + lax.rem(y + step, YS)) * rows, rows)
        top, low = halves(ortho[pl.ds(start, rows)])
        msg[:NB] = high
        msg[NB:NB + rows] = top
        msg[NB + rows:] = low


def backward_kernel(outs, slots, zs, meta, right_v, group, pairs, msg0, msg1, msg2, msg3,
                    own, send1, send2, send3, basis, held, turned, acc, sems):
    fetch(meta, outs, slots, right_v, held, sems)
    y = meta[outs * slots + outs]
    rows = NB // (zs * YS)
    for step, msg in enumerate((msg0, msg1, msg2, msg3)):
        j = lax.rem(y + YS - step, YS)
        turned[j] = msg[:NB].T
        kept = msg[NB:NB + rows].astype(F32) + msg[NB + rows:].astype(F32)
        basis[j] = kept * math.sqrt(NB)

    def tile(j, _):
        count = meta[outs * slots + j]
        acc[...] = jnp.zeros_like(acc)

        def batch(first, _):
            base = first * BATCH
            for i in range(BATCH):
                arrive(meta, outs, slots, j, base + i, right_v, held, sems)
            at = slots_of(j, base, slots, count)
            mine = turned[j]
            products = [halves(dot(mine, group[meta[slot]])) for slot in at]
            backs = []
            for i in range(BATCH):
                high, low = products[i]
                pair = pairs[at[i]]
                back = dot(high, pair[:R]) + dot(high, pair[R:]) + dot(low, pair[:R])
                backs.append(jnp.where(base + i < count, back, 0.0).astype(BF))
            terms = [
                dot_nt(beside(held[at[i]], held[at[i + 1]]), beside(backs[i], backs[i + 1])) for i in range(0, BATCH, 2)
            ]
            acc[...] += terms[0] + terms[1]
            return 0

        lax.fori_loop(0, (count + BATCH - 1) // BATCH, batch, 0)
        for step, out in enumerate((own, send1, send2, send3)):
            there = lax.rem(y + step, YS)
            for block in range(zs):
                start = pl.multiple_of((block * YS + there) * rows, rows)
                out[block, j] = acc[pl.ds(start, rows)].astype(out.dtype)
        return 0

    lax.fori_loop(0, outs, tile, 0)


def shift_y(array, step, zs):
    pairs = [(z * YS + y, z * YS + (y + step) % YS) for z in range(zs) for y in range(YS)]
    return lax.ppermute(array, "inner", pairs)


def hop(value, step, tiles):
    return lax.ppermute(value, "cols", [(i, (i + 2 * step) % tiles) for i in range(tiles)])


def swap(value, tiles):
    return lax.ppermute(value, "cols", [(i, i ^ 1) for i in range(tiles)])


def over_z(array, zs):
    groups = [[z * YS + y for z in range(zs)] for y in range(YS)]
    return lax.all_to_all(array, "inner", 0, 0, tiled=True, axis_index_groups=groups)


def params():
    return pltpu.CompilerParams(vmem_limit_bytes=20 << 20)


def body(left_u, left_v, right_u, right_v, sketch, tile_index, slot_mask):
    inner = lax.axis_index("inner")
    zs = lax.axis_size("inner") // YS
    z, y = inner // YS, inner % YS
    outs, slots = tile_index.shape
    tiles = lax.axis_size("cols")
    meta = jnp.concatenate([
        (tile_index - inner * tiles).reshape(-1), jnp.sum(slot_mask, axis=1),
        jnp.stack([y, z, lax.axis_index("cols")]),
    ]).astype(jnp.int32)
    shape = jax.ShapeDtypeStruct
    count = outs * slots
    right_u = pltpu.with_memory_space_constraint(right_u, pltpu.HBM)
    right_v = pltpu.with_memory_space_constraint(right_v, pltpu.HBM)
    unit = 2 * NB * R * R

    def cost(units, mib):
        return pl.CostEstimate(flops=int(units * unit), bytes_accessed=mib << 20, transcendentals=0)

    probes, held_u = pl.pallas_call(
        functools.partial(probe_kernel, outs, slots),
        out_shape=(shape((count, R, 2 * R), BF),) + (shape((count, NB, R), BF),),
        in_specs=[in_smem(), in_place(), in_place(), in_vmem()],
        out_specs=(in_vmem(),) * 2,
        scratch_shapes=[VMEM((count, NB, R), BF)] + [pltpu.SemaphoreType.DMA((count,))] * 2,
        compiler_params=params(),
        cost_estimate=cost(outs * slots, 6),
        name="probe",
    )(meta, right_u, right_v, sketch)
    near = [hop(left_v, 1, tiles), hop(left_v, -1, tiles)]
    *near, probes, left_u = lax.optimization_barrier((*near, probes, left_u))
    group_v = [left_v, *near, hop(near[1], -1, tiles)]
    group_v += [swap(value, tiles) for value in group_v]
    near = [hop(left_u, 1, tiles), hop(left_u, -1, tiles)]
    group_u = [left_u, *near]
    other_u = [swap(value, tiles) for value in group_u]
    far_u = hop(near[0], 1, tiles)
    pairs, mixing = pl.pallas_call(
        functools.partial(pair_kernel, outs, slots),
        out_shape=(shape((count, 2 * R, R), BF), shape((count, R, R), BF)),
        in_specs=[in_smem()] + [in_vmem()] * (2 + tiles),
        out_specs=(in_vmem(),) * 2,
        scratch_shapes=[VMEM((tiles, R, NB), BF)],
        compiler_params=params(),
        cost_estimate=cost(outs * slots * 1.75, 10),
        name="pair",
    )(meta, held_u, probes, *group_v)
    far_u, mixing = lax.optimization_barrier((far_u, mixing))
    group_u += [far_u, *other_u, swap(far_u, tiles)]
    own, send1, send2, send3, group = pl.pallas_call(
        functools.partial(sketch_kernel, outs, slots),
        out_shape=(shape((NB, R), F32),) + (shape((NB, R), BF),) * 3 + (shape((tiles, NB, R), BF),),
        in_specs=[in_smem()] + [in_vmem()] * (1 + tiles),
        out_specs=(in_vmem(),) * 5,
        scratch_shapes=[VMEM((NB, R), F32)],
        compiler_params=params(),
        cost_estimate=cost(outs * slots, 4),
        name="sketch",
    )(meta, mixing, *group_u)
    total = own
    for step, send in enumerate((send1, send2, send3)):
        total = total + shift_y(send, step + 1, zs).astype(F32)
    rows = NB // zs
    mine = jnp.sum(over_z(total.reshape(zs, rows, R), zs), axis=0)
    summed = over_z(jnp.broadcast_to(mine[None], (zs, rows, R)), zs)
    out_rows = NB // (zs * YS)
    messages = pl.pallas_call(
        functools.partial(ortho_kernel, outs, slots, zs),
        out_shape=(shape((NB + 2 * out_rows, R), BF),) * YS,
        in_specs=[in_smem(), in_vmem()],
        out_specs=(in_vmem(),) * YS,
        scratch_shapes=[VMEM((NB, R), F32)],
        compiler_params=params(),
        cost_estimate=cost(13, 1),
        name="ortho",
    )(meta, summed)
    messages = [shift_y(message, step, zs) if step else message for step, message in enumerate(messages)]
    pieces = (zs, outs, out_rows, R)
    own, send1, send2, send3, basis = pl.pallas_call(
        functools.partial(backward_kernel, outs, slots, zs),
        out_shape=(shape(pieces, F32),) + (shape(pieces, BF),) * 3 + (shape((outs, out_rows, R), F32),),
        in_specs=[in_smem(), in_place()] + [in_vmem()] * (2 + YS),
        out_specs=(in_vmem(),) * 5,
        scratch_shapes=[
            VMEM((count, NB, R), BF), VMEM((outs, R, NB), BF), VMEM((NB, R), F32), pltpu.SemaphoreType.DMA((count,)),
        ],
        compiler_params=params(),
        cost_estimate=cost(outs * slots * 2.75, 8),
        name="backward",
    )(meta, right_v, group, pairs, *messages)
    part = own
    for step, send in enumerate((send1, send2, send3)):
        part = part + shift_y(send, step + 1, zs).astype(F32)
    coeff = jnp.sum(over_z(part, zs), axis=0)
    return (basis, coeff)


def solution(mesh):
    return jax.shard_map(
        body,
        mesh=mesh,
        in_specs=(
            P(("inner", "cols"), None, None),
            P(("inner", "cols"), None, None),
            P("cols", "inner", None, None),
            P("cols", "inner", None, None),
            P("cols", None, None),
            P("cols", "inner"),
            P("cols", "inner"),
        ),
        out_specs=(P("cols", "inner", None), P("cols", "inner", None)),
        check_vma=False,
    )
```

```python
import functools
import math

import jax
import jax.numpy as jnp
from jax import lax
from jax.experimental import pallas as pl
from jax.experimental.pallas import tpu as pltpu
from jax.sharding import PartitionSpec as P

NB = 512
R = 128
YS = 4
BATCH = 4
HIGH = lax.Precision.HIGHEST
BF = jnp.bfloat16
F32 = jnp.float32
VMEM = pltpu.VMEM
NN = (((1,), (0,)), ((), ()))
NT = (((1,), (1,)), ((), ()))
TN = (((0,), (0,)), ((), ()))


def dot(a, b):
    return jnp.dot(a, b, preferred_element_type=F32)


def dot_nt(a, b):
    return lax.dot_general(a, b, NT, preferred_element_type=F32)


def halves(a):
    high = a.astype(BF)
    return high, (a - high.astype(F32)).astype(BF)


def in_vmem():
    return pl.BlockSpec(memory_space=VMEM)


def in_place():
    return pl.BlockSpec(memory_space=pltpu.HBM)


def in_smem():
    return pl.BlockSpec(memory_space=pltpu.SMEM)


def live(meta, j):
    mask = meta[1]
    count = mask[j, 0]
    for s in range(1, mask.shape[1]):
        count += mask[j, s]
    return count


def tile_of(meta, at):
    index = meta[0]
    slots = index.shape[1]
    return index[lax.div(at, slots), lax.rem(at, slots)] - lax.axis_index("inner") * lax.axis_size("cols")


def y_of():
    return lax.rem(lax.axis_index("inner"), YS)


def fetch(meta, outs, slots, source, held, sems):
    def tile(j, _):
        def one(s, _):
            pltpu.make_async_copy(source.at[j, s], held.at[j * slots + s], sems.at[j * slots + s]).start()
            return 0

        lax.fori_loop(0, live(meta, j), one, 0)
        return 0

    lax.fori_loop(0, outs, tile, 0)


def arrive(count, slots, j, s, source, held, sems):
    @pl.when(s < count)
    def _():
        pltpu.make_async_copy(source.at[j, s], held.at[j * slots + s], sems.at[j * slots + s]).wait()


def beside(a, b):
    return jnp.concatenate([a, b], axis=1)


def above(a, b):
    return jnp.concatenate([a, b], axis=0)


def slots_of(j, base, slots, count):
    return [j * slots + jnp.minimum(base + i, count - 1) for i in range(BATCH)]


def probe_kernel(outs, slots, index, mask, right_u, right_v, sketch, probes, held_u, held, plain, sems_u, sems, sem):
    meta = index, mask
    copy = pltpu.make_async_copy(sketch, plain, sem)
    copy.start()
    fetch(meta, outs, slots, right_v, held, sems)
    fetch(meta, outs, slots, right_u, held_u, sems_u)
    copy.wait()

    def tile(j, _):
        turned = plain[j].T
        count = live(meta, j)

        def batch(first, _):
            base = first * BATCH
            for i in range(BATCH):
                arrive(count, slots, j, base + i, right_v, held, sems)
            at = slots_of(j, base, slots, count)
            products = [dot(turned, held[slot]) for slot in at]
            for slot, product in zip(at, products):
                probes[slot] = beside(*halves(product))
            for i in range(BATCH):
                arrive(count, slots, j, base + i, right_u, held_u, sems_u)
            return 0

        lax.fori_loop(0, (count + BATCH - 1) // BATCH, batch, 0)
        return 0

    lax.fori_loop(0, outs, tile, 0)


def tile_ids(tiles):
    me = lax.axis_index("cols")
    return [lax.rem(me + 2 * hop, tiles) ^ flip for flip in (0, 1) for hop in (0, tiles // 2 - 1, 1, 2)]


def pair_kernel(outs, slots, index, mask, held, probes, *rest):
    meta = index, mask
    parts, (pairs, mixing, turned) = rest[:-3], rest[-3:]
    for k, part in zip(tile_ids(len(parts)), parts):
        turned[k] = part[0].T

    def tile(j, _):
        count = live(meta, j)

        def batch(first, _):
            base = first * BATCH
            at = slots_of(j, base, slots, count)
            products = [halves(dot(turned[tile_of(meta, slot)], held[slot])) for slot in at]
            mixes = []
            for slot, (high, low) in zip(at, products):
                probe = probes[slot]
                mixes.append(dot_nt(high, probe[:, :R]) + dot_nt(high, probe[:, R:]) + dot_nt(low, probe[:, :R]))
            for i in range(BATCH):
                pairs[at[i]] = above(*products[i])
                mixing[j * slots + base + i] = jnp.where(base + i < count, mixes[i], 0.0).astype(BF)
            return 0

        lax.fori_loop(0, (count + BATCH - 1) // BATCH, batch, 0)
        return 0

    lax.fori_loop(0, outs, tile, 0)


def sketch_kernel(outs, slots, index, mask, mixing, *rest):
    meta = index, mask
    parts, (own, send1, send2, send3, group, acc) = rest[:-6], rest[-6:]
    for k, part in zip(tile_ids(len(parts)), parts):
        group[k] = part[0]
    y = y_of()

    def tile(order, _):
        j = lax.rem(y + 1 + order, YS)
        acc[...] = jnp.zeros_like(acc)

        def batch(first, _):
            base = first * BATCH
            at = [j * slots + base + i for i in range(BATCH)]
            tiles = [group[tile_of(meta, slot)] for slot in at]
            terms = [
                dot(beside(tiles[i], tiles[i + 1]), above(mixing[at[i]], mixing[at[i + 1]])) for i in range(0, BATCH, 2)
            ]
            acc[...] += terms[0] + terms[1]
            return 0

        lax.fori_loop(0, (live(meta, j) + BATCH - 1) // BATCH, batch, 0)
        for place, out in enumerate((send1, send2, send3, own)):
            @pl.when(order == place)
            def _():
                out[...] = acc[...].astype(out.dtype)
        return 0

    lax.fori_loop(0, YS, tile, 0)


def exact(a, b, dims):
    return lax.dot_general(a, b, dims, precision=HIGH, preferred_element_type=F32)


def inverse_factor(block):
    n = block.shape[0]
    lanes = 2 * n
    same = lax.broadcasted_iota(jnp.int32, (n, n), 0) == lax.broadcasted_iota(jnp.int32, (n, n), 1)
    full = jnp.concatenate([same.astype(F32), block], axis=1)
    x = [full[8 * i:8 * i + 8] for i in range(n // 8)]
    sub = lax.broadcasted_iota(jnp.int32, (8, lanes), 0)

    def wide(v):
        return jnp.broadcast_to(v, (8, lanes))

    for k in range(0, n, 2):
        i0, r = k // 8, k % 8
        first, second = wide(x[i0][r:r + 1]), wide(x[i0][r + 1:r + 2])
        a, b = wide(first[:, n + k:n + k + 1]), wide(first[:, n + k + 1:n + k + 2])
        c = wide(second[:, n + k + 1:n + k + 2])
        scale = 1.0 / (a * c - b * b)
        p, q = (c * first - b * second) * scale, (a * second - b * first) * scale
        for i in range(i0, n // 8):
            if i == i0 and r == 6:
                continue
            step = wide(x[i][:, n + k:n + k + 1]) * p + wide(x[i][:, n + k + 1:n + k + 2]) * q
            if i == i0:
                step = jnp.where(sub > r + 1, step, 0.0)
            x[i] = x[i] - step
    full = jnp.concatenate(x, axis=0)
    row = lax.broadcasted_iota(jnp.int32, (n, lanes), 0)
    lane = lax.broadcasted_iota(jnp.int32, (n, lanes), 1) - n
    diag = jnp.broadcast_to(jnp.sum(jnp.where(lane == row, full, 0.0), axis=1, keepdims=True), (n, lanes))
    side = jnp.broadcast_to(jnp.sum(jnp.where(lane == row + 1, full, 0.0), axis=1, keepdims=True), (n, lanes))
    ratio = side / diag
    odd = row % 2 == 1
    full = jnp.where(odd, full - pltpu.roll(ratio * full, 1, 0), full)
    diag = jnp.where(odd, diag - pltpu.roll(ratio * side, 1, 0), diag)
    return (full * lax.rsqrt(diag))[:, :n]


def inverse_cholesky(gram):
    half = gram.shape[0] // 2
    upper = inverse_factor(gram[:half, :half])
    across = exact(upper, gram[:half, half:], NN)
    lower = inverse_factor(gram[half:, half:] - exact(across, across, TN))
    corner = -exact(lower, exact(across, upper, TN), NN)
    top = jnp.concatenate([upper, jnp.zeros_like(upper)], axis=1)
    return jnp.concatenate([top, jnp.concatenate([corner, lower], axis=1)], axis=0)


def ortho_kernel(zs, blocks, msg0, msg1, msg2, msg3, ortho):
    inner = lax.axis_index("inner")
    y, z = lax.rem(inner, YS), lax.div(inner, YS)
    rows = NB // (zs * YS)
    summed = blocks[...].reshape(NB, R)
    ortho[...] = exact(summed, inverse_cholesky(exact(summed, summed, TN)), NT)
    high = ortho[...].astype(BF)
    for step, msg in enumerate((msg0, msg1, msg2, msg3)):
        start = pl.multiple_of((z * YS + lax.rem(y + step, YS)) * rows, rows)
        top, low = halves(ortho[pl.ds(start, rows)])
        msg[:NB] = high
        msg[NB:NB + rows] = top
        msg[NB + rows:] = low


def backward_kernel(outs, slots, zs, index, mask, right_v, group, pairs, msg0, msg1, msg2, msg3,
                    own, send1, send2, send3, basis, held, turned, acc, sems):
    meta = index, mask
    fetch(meta, outs, slots, right_v, held, sems)
    y = y_of()
    rows = NB // (zs * YS)
    for step, msg in enumerate((msg0, msg1, msg2, msg3)):
        j = lax.rem(y + YS - step, YS)
        turned[j] = msg[:NB].T
        kept = msg[NB:NB + rows].astype(F32) + msg[NB + rows:].astype(F32)
        basis[j] = kept * math.sqrt(NB)

    def tile(j, _):
        count = live(meta, j)
        acc[...] = jnp.zeros_like(acc)

        def batch(first, _):
            base = first * BATCH
            for i in range(BATCH):
                arrive(count, slots, j, base + i, right_v, held, sems)
            at = slots_of(j, base, slots, count)
            mine = turned[j]
            products = [halves(dot(mine, group[tile_of(meta, slot)])) for slot in at]
            backs = []
            for i in range(BATCH):
                high, low = products[i]
                pair = pairs[at[i]]
                back = dot(high, pair[:R]) + dot(high, pair[R:]) + dot(low, pair[:R])
                backs.append(jnp.where(base + i < count, back, 0.0).astype(BF))
            terms = [
                dot_nt(beside(held[at[i]], held[at[i + 1]]), beside(backs[i], backs[i + 1])) for i in range(0, BATCH, 2)
            ]
            acc[...] += terms[0] + terms[1]
            return 0

        lax.fori_loop(0, (count + BATCH - 1) // BATCH, batch, 0)
        for step, out in enumerate((own, send1, send2, send3)):
            there = lax.rem(y + step, YS)
            for block in range(zs):
                start = pl.multiple_of((block * YS + there) * rows, rows)
                out[block, j] = acc[pl.ds(start, rows)].astype(out.dtype)
        return 0

    lax.fori_loop(0, outs, tile, 0)


def shift_y(array, step, zs):
    pairs = [(z * YS + y, z * YS + (y + step) % YS) for z in range(zs) for y in range(YS)]
    return lax.ppermute(array, "inner", pairs)


def hop(value, step, tiles):
    return lax.ppermute(value, "cols", [(i, (i + 2 * step) % tiles) for i in range(tiles)])


def swap(value, tiles):
    return lax.ppermute(value, "cols", [(i, i ^ 1) for i in range(tiles)])


def over_z(array, zs):
    groups = [[z * YS + y for z in range(zs)] for y in range(YS)]
    return lax.all_to_all(array, "inner", 0, 0, tiled=True, axis_index_groups=groups)


def params():
    return pltpu.CompilerParams(vmem_limit_bytes=20 << 20)


def body(left_u, left_v, right_u, right_v, sketch, tile_index, slot_mask):
    zs = lax.axis_size("inner") // YS
    outs, slots = tile_index.shape
    tiles = lax.axis_size("cols")
    shape = jax.ShapeDtypeStruct
    count = outs * slots
    right_u = pltpu.with_memory_space_constraint(right_u, pltpu.HBM)
    right_v = pltpu.with_memory_space_constraint(right_v, pltpu.HBM)
    sketch = pltpu.with_memory_space_constraint(sketch, pltpu.HBM)
    unit = 2 * NB * R * R

    def cost(units, mib):
        return pl.CostEstimate(flops=int(units * unit), bytes_accessed=mib << 20, transcendentals=0)

    probes, held_u = pl.pallas_call(
        functools.partial(probe_kernel, outs, slots),
        out_shape=(shape((count, R, 2 * R), BF),) + (shape((count, NB, R), BF),),
        in_specs=[in_smem(), in_smem(), in_place(), in_place(), in_place()],
        out_specs=(in_vmem(),) * 2,
        scratch_shapes=[VMEM((count, NB, R), BF), VMEM((outs, NB, R), BF)]
        + [pltpu.SemaphoreType.DMA((count,))] * 2 + [pltpu.SemaphoreType.DMA],
        compiler_params=params(),
        cost_estimate=cost(outs * slots, 6),
        name="probe",
    )(tile_index, slot_mask, right_u, right_v, sketch)
    near = [hop(value, step, tiles) for value in (left_v, left_u) for step in (1, -1)]
    *near, probes = lax.optimization_barrier((*near, probes))
    group_v = [left_v, *near[:2], hop(near[1], -1, tiles)]
    group_v += [swap(value, tiles) for value in group_v]
    group_u = [left_u, *near[2:]]
    other_u = [swap(value, tiles) for value in group_u]
    far_u = hop(near[2], 1, tiles)
    pairs, mixing = pl.pallas_call(
        functools.partial(pair_kernel, outs, slots),
        out_shape=(shape((count, 2 * R, R), BF), shape((count, R, R), BF)),
        in_specs=[in_smem(), in_smem()] + [in_vmem()] * (2 + tiles),
        out_specs=(in_vmem(),) * 2,
        scratch_shapes=[VMEM((tiles, R, NB), BF)],
        compiler_params=params(),
        cost_estimate=cost(outs * slots * 1.75, 10),
        name="pair",
    )(tile_index, slot_mask, held_u, probes, *group_v)
    far_u, mixing = lax.optimization_barrier((far_u, mixing))
    group_u += [far_u, *other_u, swap(far_u, tiles)]
    own, send1, send2, send3, group = pl.pallas_call(
        functools.partial(sketch_kernel, outs, slots),
        out_shape=(shape((NB, R), F32),) + (shape((NB, R), BF),) * 3 + (shape((tiles, NB, R), BF),),
        in_specs=[in_smem(), in_smem()] + [in_vmem()] * (1 + tiles),
        out_specs=(in_vmem(),) * 5,
        scratch_shapes=[VMEM((NB, R), F32)],
        compiler_params=params(),
        cost_estimate=cost(outs * slots, 4),
        name="sketch",
    )(tile_index, slot_mask, mixing, *group_u)
    total = own
    for step, send in enumerate((send1, send2, send3)):
        total = total + shift_y(send, step + 1, zs).astype(F32)
    rows = NB // zs
    mine = jnp.sum(over_z(total.reshape(zs, rows, R), zs), axis=0)
    summed = over_z(jnp.broadcast_to(mine[None], (zs, rows, R)), zs)
    out_rows = NB // (zs * YS)
    messages = pl.pallas_call(
        functools.partial(ortho_kernel, zs),
        out_shape=(shape((NB + 2 * out_rows, R), BF),) * YS,
        in_specs=[in_vmem()],
        out_specs=(in_vmem(),) * YS,
        scratch_shapes=[VMEM((NB, R), F32)],
        compiler_params=params(),
        cost_estimate=cost(13, 1),
        name="ortho",
    )(summed)
    messages = [shift_y(message, step, zs) if step else message for step, message in enumerate(messages)]
    pieces = (zs, outs, out_rows, R)
    own, send1, send2, send3, basis = pl.pallas_call(
        functools.partial(backward_kernel, outs, slots, zs),
        out_shape=(shape(pieces, F32),) + (shape(pieces, BF),) * 3 + (shape((outs, out_rows, R), F32),),
        in_specs=[in_smem(), in_smem(), in_place()] + [in_vmem()] * (2 + YS),
        out_specs=(in_vmem(),) * 5,
        scratch_shapes=[
            VMEM((count, NB, R), BF), VMEM((outs, R, NB), BF), VMEM((NB, R), F32), pltpu.SemaphoreType.DMA((count,)),
        ],
        compiler_params=params(),
        cost_estimate=cost(outs * slots * 2.75, 8),
        name="backward",
    )(tile_index, slot_mask, right_v, group, pairs, *messages)
    part = own
    for step, send in enumerate((send1, send2, send3)):
        part = part + shift_y(send, step + 1, zs).astype(F32)
    coeff = jnp.sum(over_z(part, zs), axis=0)
    return (basis, coeff)


def solution(mesh):
    return jax.shard_map(
        body,
        mesh=mesh,
        in_specs=(
            P(("inner", "cols"), None, None),
            P(("inner", "cols"), None, None),
            P("cols", "inner", None, None),
            P("cols", "inner", None, None),
            P("cols", None, None),
            P("cols", "inner"),
            P("cols", "inner"),
        ),
        out_specs=(P("cols", "inner", None), P("cols", "inner", None)),
        check_vma=False,
    )
```

```python
import functools
import math

import jax
import jax.numpy as jnp
from jax import lax
from jax.experimental import pallas as pl
from jax.experimental.pallas import tpu as pltpu
from jax.sharding import PartitionSpec as P

NB = 512
R = 128
YS = 4
BATCH = 4
HIGH = lax.Precision.HIGHEST
BF = jnp.bfloat16
F32 = jnp.float32
VMEM = pltpu.VMEM
NN = (((1,), (0,)), ((), ()))
NT = (((1,), (1,)), ((), ()))
TN = (((0,), (0,)), ((), ()))


def dot(a, b):
    return jnp.dot(a, b, preferred_element_type=F32)


def dot_nt(a, b):
    return lax.dot_general(a, b, NT, preferred_element_type=F32)


def halves(a):
    high = a.astype(BF)
    return high, (a - high.astype(F32)).astype(BF)


def in_vmem():
    return pl.BlockSpec(memory_space=VMEM)


def in_place():
    return pl.BlockSpec(memory_space=pltpu.HBM)


def in_smem():
    return pl.BlockSpec(memory_space=pltpu.SMEM)


def live(meta, j):
    mask = meta[1]
    count = mask[j, 0]
    for s in range(1, mask.shape[1]):
        count += mask[j, s]
    return count


def tile_of(meta, at):
    index = meta[0]
    slots = index.shape[1]
    return index[lax.div(at, slots), lax.rem(at, slots)] - lax.axis_index("inner") * lax.axis_size("cols")


def y_of():
    return lax.rem(lax.axis_index("inner"), YS)


def fetch(meta, outs, slots, source, held, sems):
    def tile(j, _):
        def one(s, _):
            pltpu.make_async_copy(source.at[j, s], held.at[j * slots + s], sems.at[j * slots + s]).start()
            return 0

        lax.fori_loop(0, live(meta, j), one, 0)
        return 0

    lax.fori_loop(0, outs, tile, 0)


def arrive(count, slots, j, s, source, held, sems):
    @pl.when(s < count)
    def _():
        pltpu.make_async_copy(source.at[j, s], held.at[j * slots + s], sems.at[j * slots + s]).wait()


def beside(a, b):
    return jnp.concatenate([a, b], axis=1)


def above(a, b):
    return jnp.concatenate([a, b], axis=0)


def slots_of(j, base, slots, count):
    return [j * slots + jnp.minimum(base + i, count - 1) for i in range(BATCH)]


def probe_kernel(outs, slots, index, mask, right_u, right_v, sketch, probes, held_u, held, plain, sems_u, sems, sem):
    meta = index, mask
    copy = pltpu.make_async_copy(sketch, plain, sem)
    copy.start()
    fetch(meta, outs, slots, right_v, held, sems)
    fetch(meta, outs, slots, right_u, held_u, sems_u)
    copy.wait()

    def tile(j, _):
        turned = plain[j].T
        count = live(meta, j)

        def batch(first, _):
            base = first * BATCH
            for i in range(BATCH):
                arrive(count, slots, j, base + i, right_v, held, sems)
            at = slots_of(j, base, slots, count)
            products = [dot(turned, held[slot]) for slot in at]
            for slot, product in zip(at, products):
                probes[slot] = beside(*halves(product))
            for i in range(BATCH):
                arrive(count, slots, j, base + i, right_u, held_u, sems_u)
            return 0

        lax.fori_loop(0, (count + BATCH - 1) // BATCH, batch, 0)
        return 0

    lax.fori_loop(0, outs, tile, 0)


def tile_ids(tiles):
    me = lax.axis_index("cols")
    return [lax.rem(me + 2 * hop, tiles) ^ flip for flip in (0, 1) for hop in (0, tiles // 2 - 1, 1, 2)]


def pair_kernel(outs, slots, index, mask, held, probes, *rest):
    meta = index, mask
    parts, (pairs, mixing, turned) = rest[:-3], rest[-3:]
    for k, part in zip(tile_ids(len(parts)), parts):
        turned[k] = part[0].T

    def tile(j, _):
        count = live(meta, j)

        def batch(first, _):
            base = first * BATCH
            at = slots_of(j, base, slots, count)
            products = [halves(dot(turned[tile_of(meta, slot)], held[slot])) for slot in at]
            mixes = []
            for slot, (high, low) in zip(at, products):
                probe = probes[slot]
                mixes.append(dot_nt(high, probe[:, :R]) + dot_nt(high, probe[:, R:]) + dot_nt(low, probe[:, :R]))
            for i in range(BATCH):
                pairs[at[i]] = above(*products[i])
                mixing[j * slots + base + i] = jnp.where(base + i < count, mixes[i], 0.0).astype(BF)
            return 0

        lax.fori_loop(0, (count + BATCH - 1) // BATCH, batch, 0)
        return 0

    lax.fori_loop(0, outs, tile, 0)


def sketch_kernel(outs, slots, index, mask, mixing, *rest):
    meta = index, mask
    parts, (own, send1, send2, send3, group, acc) = rest[:-6], rest[-6:]
    for k, part in zip(tile_ids(len(parts)), parts):
        group[k] = part[0]
    y = y_of()

    def tile(order, _):
        j = lax.rem(y + 1 + order, YS)
        acc[...] = jnp.zeros_like(acc)

        def batch(first, _):
            base = first * BATCH
            at = [j * slots + base + i for i in range(BATCH)]
            tiles = [group[tile_of(meta, slot)] for slot in at]
            terms = [
                dot(beside(tiles[i], tiles[i + 1]), above(mixing[at[i]], mixing[at[i + 1]])) for i in range(0, BATCH, 2)
            ]
            acc[...] += terms[0] + terms[1]
            return 0

        lax.fori_loop(0, (live(meta, j) + BATCH - 1) // BATCH, batch, 0)
        for place, out in enumerate((send1, send2, send3, own)):
            @pl.when(order == place)
            def _():
                out[...] = acc[...].astype(out.dtype)
        return 0

    lax.fori_loop(0, YS, tile, 0)


def exact(a, b, dims):
    return lax.dot_general(a, b, dims, precision=HIGH, preferred_element_type=F32)


def inverse_factor(block):
    n = block.shape[0]
    lanes = 2 * n
    same = lax.broadcasted_iota(jnp.int32, (n, n), 0) == lax.broadcasted_iota(jnp.int32, (n, n), 1)
    full = jnp.concatenate([same.astype(F32), block], axis=1)
    x = [full[8 * i:8 * i + 8] for i in range(n // 8)]
    done = list(x)
    sub = lax.broadcasted_iota(jnp.int32, (8, lanes), 0)

    def wide(v):
        return jnp.broadcast_to(v, (8, lanes))

    for k in range(0, n, 4):
        i0, r = k // 8, k % 8
        row = [wide(x[i0][r + t:r + t + 1]) for t in range(4)]
        b = {(t, u): wide(row[t][:, n + k + u:n + k + u + 1]) for t in range(4) for u in range(t, 4)}
        one = 1.0 / (b[0, 0] * b[1, 1] - b[0, 1] * b[0, 1])
        t00 = (b[1, 1] * b[0, 2] - b[0, 1] * b[1, 2]) * one
        t01 = (b[1, 1] * b[0, 3] - b[0, 1] * b[1, 3]) * one
        t10 = (b[0, 0] * b[1, 2] - b[0, 1] * b[0, 2]) * one
        t11 = (b[0, 0] * b[1, 3] - b[0, 1] * b[0, 3]) * one
        s00 = b[2, 2] - (b[0, 2] * t00 + b[1, 2] * t10)
        s01 = b[2, 3] - (b[0, 2] * t01 + b[1, 2] * t11)
        s11 = b[3, 3] - (b[0, 3] * t01 + b[1, 3] * t11)
        two = 1.0 / (s00 * s11 - s01 * s01)
        e2 = row[2] - (t00 * row[0] + t10 * row[1])
        e3 = row[3] - (t01 * row[0] + t11 * row[1])
        p2, p3 = (s11 * e2 - s01 * e3) * two, (s00 * e3 - s01 * e2) * two
        p0 = (b[1, 1] * row[0] - b[0, 1] * row[1]) * one - (t00 * p2 + t01 * p3)
        p1 = (b[0, 0] * row[1] - b[0, 1] * row[0]) * one - (t10 * p2 + t11 * p3)
        for i in range(i0, n // 8):
            if i == i0 and r == 4:
                continue
            u = [wide(x[i][:, n + k + t:n + k + t + 1]) for t in range(4)]
            step = (u[0] * p0 + u[1] * p1) + (u[2] * p2 + u[3] * p3)
            if i == i0:
                step = jnp.where(sub > r + 3, step, 0.0)
            x[i] = x[i] - step
        for t, (a, c, d, first, second) in enumerate((
            (b[0, 0], b[0, 1], b[1, 1], row[0], row[1]), (s00, s01, s11, e2, e3)
        )):
            root = lax.rsqrt(a)
            off = c * root
            first = first * root
            second = (second - off * first) * lax.rsqrt(d - off * off)
            done[i0] = jnp.where(sub == r + 2 * t, first, jnp.where(sub == r + 2 * t + 1, second, done[i0]))
    return jnp.concatenate(done, axis=0)[:, :n]


def inverse_cholesky(gram):
    half = gram.shape[0] // 2
    upper = inverse_factor(gram[:half, :half])
    across = exact(upper, gram[:half, half:], NN)
    lower = inverse_factor(gram[half:, half:] - exact(across, across, TN))
    corner = -exact(lower, exact(across, upper, TN), NN)
    top = jnp.concatenate([upper, jnp.zeros_like(upper)], axis=1)
    return jnp.concatenate([top, jnp.concatenate([corner, lower], axis=1)], axis=0)


def ortho_kernel(zs, blocks, msg0, msg1, msg2, msg3, ortho):
    inner = lax.axis_index("inner")
    y, z = lax.rem(inner, YS), lax.div(inner, YS)
    rows = NB // (zs * YS)
    summed = blocks[...].reshape(NB, R)
    ortho[...] = exact(summed, inverse_cholesky(exact(summed, summed, TN)), NT)
    high = ortho[...].astype(BF)
    for step, msg in enumerate((msg0, msg1, msg2, msg3)):
        start = pl.multiple_of((z * YS + lax.rem(y + step, YS)) * rows, rows)
        top, low = halves(ortho[pl.ds(start, rows)])
        msg[:NB] = high
        msg[NB:NB + rows] = top
        msg[NB + rows:] = low


def backward_kernel(outs, slots, zs, index, mask, right_v, group, pairs, msg0, msg1, msg2, msg3,
                    own, send1, send2, send3, basis, held, turned, acc, sems):
    meta = index, mask
    fetch(meta, outs, slots, right_v, held, sems)
    y = y_of()
    rows = NB // (zs * YS)
    for step, msg in enumerate((msg0, msg1, msg2, msg3)):
        j = lax.rem(y + YS - step, YS)
        turned[j] = msg[:NB].T
        kept = msg[NB:NB + rows].astype(F32) + msg[NB + rows:].astype(F32)
        basis[j] = kept * math.sqrt(NB)

    def tile(j, _):
        count = live(meta, j)
        acc[...] = jnp.zeros_like(acc)

        def batch(first, _):
            base = first * BATCH
            for i in range(BATCH):
                arrive(count, slots, j, base + i, right_v, held, sems)
            at = slots_of(j, base, slots, count)
            mine = turned[j]
            products = [halves(dot(mine, group[tile_of(meta, slot)])) for slot in at]
            backs = []
            for i in range(BATCH):
                high, low = products[i]
                pair = pairs[at[i]]
                back = dot(high, pair[:R]) + dot(high, pair[R:]) + dot(low, pair[:R])
                backs.append(jnp.where(base + i < count, back, 0.0).astype(BF))
            terms = [
                dot_nt(beside(held[at[i]], held[at[i + 1]]), beside(backs[i], backs[i + 1])) for i in range(0, BATCH, 2)
            ]
            acc[...] += terms[0] + terms[1]
            return 0

        lax.fori_loop(0, (count + BATCH - 1) // BATCH, batch, 0)
        for step, out in enumerate((own, send1, send2, send3)):
            there = lax.rem(y + step, YS)
            for block in range(zs):
                start = pl.multiple_of((block * YS + there) * rows, rows)
                out[block, j] = acc[pl.ds(start, rows)].astype(out.dtype)
        return 0

    lax.fori_loop(0, outs, tile, 0)


def shift_y(array, step, zs):
    pairs = [(z * YS + y, z * YS + (y + step) % YS) for z in range(zs) for y in range(YS)]
    return lax.ppermute(array, "inner", pairs)


def hop(value, step, tiles):
    return lax.ppermute(value, "cols", [(i, (i + 2 * step) % tiles) for i in range(tiles)])


def swap(value, tiles):
    return lax.ppermute(value, "cols", [(i, i ^ 1) for i in range(tiles)])


def over_z(array, zs):
    groups = [[z * YS + y for z in range(zs)] for y in range(YS)]
    return lax.all_to_all(array, "inner", 0, 0, tiled=True, axis_index_groups=groups)


def params():
    return pltpu.CompilerParams(vmem_limit_bytes=20 << 20)


def body(left_u, left_v, right_u, right_v, sketch, tile_index, slot_mask):
    zs = lax.axis_size("inner") // YS
    outs, slots = tile_index.shape
    tiles = lax.axis_size("cols")
    shape = jax.ShapeDtypeStruct
    count = outs * slots
    right_u = pltpu.with_memory_space_constraint(right_u, pltpu.HBM)
    right_v = pltpu.with_memory_space_constraint(right_v, pltpu.HBM)
    unit = 2 * NB * R * R

    def cost(units, mib):
        return pl.CostEstimate(flops=int(units * unit), bytes_accessed=mib << 20, transcendentals=0)

    near = [hop(value, step, tiles) for value in (left_v, left_u) for step in (1, -1)]
    *near, sketch = lax.optimization_barrier((*near, sketch))
    far_v, far_u = hop(near[1], -1, tiles), hop(near[2], 1, tiles)
    sketch = pltpu.with_memory_space_constraint(sketch, pltpu.HBM)
    probes, held_u = pl.pallas_call(
        functools.partial(probe_kernel, outs, slots),
        out_shape=(shape((count, R, 2 * R), BF),) + (shape((count, NB, R), BF),),
        in_specs=[in_smem(), in_smem(), in_place(), in_place(), in_place()],
        out_specs=(in_vmem(),) * 2,
        scratch_shapes=[VMEM((count, NB, R), BF), VMEM((outs, NB, R), BF)]
        + [pltpu.SemaphoreType.DMA((count,))] * 2 + [pltpu.SemaphoreType.DMA],
        compiler_params=params(),
        cost_estimate=cost(outs * slots, 6),
        name="probe",
    )(tile_index, slot_mask, right_u, right_v, sketch)
    *near, far_v, far_u, probes = lax.optimization_barrier((*near, far_v, far_u, probes))
    group_v = [left_v, *near[:2], far_v]
    group_v += [swap(value, tiles) for value in group_v]
    group_u = [left_u, *near[2:], far_u]
    group_u += [swap(value, tiles) for value in group_u]
    pairs, mixing = pl.pallas_call(
        functools.partial(pair_kernel, outs, slots),
        out_shape=(shape((count, 2 * R, R), BF), shape((count, R, R), BF)),
        in_specs=[in_smem(), in_smem()] + [in_vmem()] * (2 + tiles),
        out_specs=(in_vmem(),) * 2,
        scratch_shapes=[VMEM((tiles, R, NB), BF)],
        compiler_params=params(),
        cost_estimate=cost(outs * slots * 1.75, 10),
        name="pair",
    )(tile_index, slot_mask, held_u, probes, *group_v)
    own, send1, send2, send3, group = pl.pallas_call(
        functools.partial(sketch_kernel, outs, slots),
        out_shape=(shape((NB, R), F32),) + (shape((NB, R), BF),) * 3 + (shape((tiles, NB, R), BF),),
        in_specs=[in_smem(), in_smem()] + [in_vmem()] * (1 + tiles),
        out_specs=(in_vmem(),) * 5,
        scratch_shapes=[VMEM((NB, R), F32)],
        compiler_params=params(),
        cost_estimate=cost(outs * slots, 4),
        name="sketch",
    )(tile_index, slot_mask, mixing, *group_u)
    total = own
    for step, send in enumerate((send1, send2, send3)):
        total = total + shift_y(send, step + 1, zs).astype(F32)
    rows = NB // zs
    mine = jnp.sum(over_z(total.reshape(zs, rows, R), zs), axis=0)
    summed = over_z(jnp.broadcast_to(mine[None], (zs, rows, R)), zs)
    out_rows = NB // (zs * YS)
    messages = pl.pallas_call(
        functools.partial(ortho_kernel, zs),
        out_shape=(shape((NB + 2 * out_rows, R), BF),) * YS,
        in_specs=[in_vmem()],
        out_specs=(in_vmem(),) * YS,
        scratch_shapes=[VMEM((NB, R), F32)],
        compiler_params=params(),
        cost_estimate=cost(13, 1),
        name="ortho",
    )(summed)
    messages = [shift_y(message, step, zs) if step else message for step, message in enumerate(messages)]
    pieces = (zs, outs, out_rows, R)
    own, send1, send2, send3, basis = pl.pallas_call(
        functools.partial(backward_kernel, outs, slots, zs),
        out_shape=(shape(pieces, F32),) + (shape(pieces, BF),) * 3 + (shape((outs, out_rows, R), F32),),
        in_specs=[in_smem(), in_smem(), in_place()] + [in_vmem()] * (2 + YS),
        out_specs=(in_vmem(),) * 5,
        scratch_shapes=[
            VMEM((count, NB, R), BF), VMEM((outs, R, NB), BF), VMEM((NB, R), F32), pltpu.SemaphoreType.DMA((count,)),
        ],
        compiler_params=params(),
        cost_estimate=cost(outs * slots * 2.75, 8),
        name="backward",
    )(tile_index, slot_mask, right_v, group, pairs, *messages)
    part = own
    for step, send in enumerate((send1, send2, send3)):
        part = part + shift_y(send, step + 1, zs).astype(F32)
    coeff = jnp.sum(over_z(part, zs), axis=0)
    return (basis, coeff)


def solution(mesh):
    return jax.shard_map(
        body,
        mesh=mesh,
        in_specs=(
            P(("inner", "cols"), None, None),
            P(("inner", "cols"), None, None),
            P("cols", "inner", None, None),
            P("cols", "inner", None, None),
            P("cols", None, None),
            P("cols", "inner"),
            P("cols", "inner"),
        ),
        out_specs=(P("cols", "inner", None), P("cols", "inner", None)),
        check_vma=False,
    )
```

```python
import functools
import math

import jax
import jax.numpy as jnp
from jax import lax
from jax.experimental import pallas as pl
from jax.experimental.pallas import tpu as pltpu
from jax.sharding import PartitionSpec as P

NB = 512
R = 128
YS = 4
BATCH = 4
HIGH = lax.Precision.HIGHEST
BF = jnp.bfloat16
F32 = jnp.float32
VMEM = pltpu.VMEM
NN = (((1,), (0,)), ((), ()))
NT = (((1,), (1,)), ((), ()))
TN = (((0,), (0,)), ((), ()))


def dot(a, b):
    return jnp.dot(a, b, preferred_element_type=F32)


def dot_nt(a, b):
    return lax.dot_general(a, b, NT, preferred_element_type=F32)


def halves(a):
    high = a.astype(BF)
    return high, (a - high.astype(F32)).astype(BF)


def in_vmem():
    return pl.BlockSpec(memory_space=VMEM)


def in_place():
    return pl.BlockSpec(memory_space=pltpu.HBM)


def in_smem():
    return pl.BlockSpec(memory_space=pltpu.SMEM)


def live(packed, j):
    count = packed[j, 0] & 1
    for s in range(1, packed.shape[1]):
        count += packed[j, s] & 1
    return count


def tile_of(packed, at):
    slots = packed.shape[1]
    return packed[lax.div(at, slots), lax.rem(at, slots)] >> 1


def y_of():
    return lax.rem(lax.axis_index("inner"), YS)


def fetch(meta, outs, slots, source, held, sems):
    def tile(j, _):
        def one(s, _):
            pltpu.make_async_copy(source.at[j, s], held.at[j * slots + s], sems.at[j * slots + s]).start()
            return 0

        lax.fori_loop(0, live(meta, j), one, 0)
        return 0

    lax.fori_loop(0, outs, tile, 0)


def arrive(count, slots, j, s, source, held, sems):
    @pl.when(s < count)
    def _():
        pltpu.make_async_copy(source.at[j, s], held.at[j * slots + s], sems.at[j * slots + s]).wait()


def beside(a, b):
    return jnp.concatenate([a, b], axis=1)


def above(a, b):
    return jnp.concatenate([a, b], axis=0)


def slots_of(j, base, slots, count):
    return [j * slots + jnp.minimum(base + i, count - 1) for i in range(BATCH)]


def probe_kernel(outs, slots, meta, right_u, right_v, sketch, probes, held_u, held, plain, sems_u, sems, sem):
    copy = pltpu.make_async_copy(sketch, plain, sem)
    copy.start()
    fetch(meta, outs, slots, right_v, held, sems)
    fetch(meta, outs, slots, right_u, held_u, sems_u)
    copy.wait()

    def tile(j, _):
        turned = plain[j].T
        count = live(meta, j)

        def batch(first, _):
            base = first * BATCH
            for i in range(BATCH):
                arrive(count, slots, j, base + i, right_v, held, sems)
            at = slots_of(j, base, slots, count)
            products = [dot(turned, held[slot]) for slot in at]
            for slot, product in zip(at, products):
                probes[slot] = beside(*halves(product))
            for i in range(BATCH):
                arrive(count, slots, j, base + i, right_u, held_u, sems_u)
            return 0

        lax.fori_loop(0, (count + BATCH - 1) // BATCH, batch, 0)
        return 0

    lax.fori_loop(0, outs, tile, 0)


def tile_ids(tiles):
    me = lax.axis_index("cols")
    return [lax.rem(me + 2 * hop, tiles) ^ flip for flip in (0, 1) for hop in (0, tiles // 2 - 1, 1, 2)]


def pair_kernel(outs, slots, meta, held, probes, *rest):
    parts, (pairs, mixing, turned) = rest[:-3], rest[-3:]
    for k, part in zip(tile_ids(len(parts)), parts):
        turned[k] = part[0].T

    def tile(j, _):
        count = live(meta, j)

        def batch(first, _):
            base = first * BATCH
            at = slots_of(j, base, slots, count)
            products = [halves(dot(turned[tile_of(meta, slot)], held[slot])) for slot in at]
            mixes = []
            for slot, (high, low) in zip(at, products):
                probe = probes[slot]
                mixes.append(dot_nt(high, probe[:, :R]) + dot_nt(high, probe[:, R:]) + dot_nt(low, probe[:, :R]))
            for i in range(BATCH):
                pairs[at[i]] = above(*products[i])
                mixing[j * slots + base + i] = jnp.where(base + i < count, mixes[i], 0.0).astype(BF)
            return 0

        lax.fori_loop(0, (count + BATCH - 1) // BATCH, batch, 0)
        return 0

    lax.fori_loop(0, outs, tile, 0)


def sketch_kernel(outs, slots, meta, mixing, *rest):
    parts, (own, send1, send2, send3, group, acc) = rest[:-6], rest[-6:]
    for k, part in zip(tile_ids(len(parts)), parts):
        group[k] = part[0]
    y = y_of()

    def tile(order, _):
        j = lax.rem(y + 1 + order, YS)
        acc[...] = jnp.zeros_like(acc)

        def batch(first, _):
            base = first * BATCH
            at = [j * slots + base + i for i in range(BATCH)]
            tiles = [group[tile_of(meta, slot)] for slot in at]
            terms = [
                dot(beside(tiles[i], tiles[i + 1]), above(mixing[at[i]], mixing[at[i + 1]])) for i in range(0, BATCH, 2)
            ]
            acc[...] += terms[0] + terms[1]
            return 0

        lax.fori_loop(0, (live(meta, j) + BATCH - 1) // BATCH, batch, 0)
        for place, out in enumerate((send1, send2, send3, own)):
            @pl.when(order == place)
            def _():
                out[...] = acc[...].astype(out.dtype)
        return 0

    lax.fori_loop(0, YS, tile, 0)


def exact(a, b, dims):
    return lax.dot_general(a, b, dims, precision=HIGH, preferred_element_type=F32)


def inverse_factor(block):
    n = block.shape[0]
    lanes = 2 * n
    same = lax.broadcasted_iota(jnp.int32, (n, n), 0) == lax.broadcasted_iota(jnp.int32, (n, n), 1)
    full = jnp.concatenate([same.astype(F32), block], axis=1)
    x = [full[8 * i:8 * i + 8] for i in range(n // 8)]
    done = list(x)
    sub = lax.broadcasted_iota(jnp.int32, (8, lanes), 0)

    def wide(v):
        return jnp.broadcast_to(v, (8, lanes))

    for k in range(0, n, 4):
        i0, r = k // 8, k % 8
        row = [wide(x[i0][r + t:r + t + 1]) for t in range(4)]
        b = {(t, u): wide(row[t][:, n + k + u:n + k + u + 1]) for t in range(4) for u in range(t, 4)}
        one = 1.0 / (b[0, 0] * b[1, 1] - b[0, 1] * b[0, 1])
        t00 = (b[1, 1] * b[0, 2] - b[0, 1] * b[1, 2]) * one
        t01 = (b[1, 1] * b[0, 3] - b[0, 1] * b[1, 3]) * one
        t10 = (b[0, 0] * b[1, 2] - b[0, 1] * b[0, 2]) * one
        t11 = (b[0, 0] * b[1, 3] - b[0, 1] * b[0, 3]) * one
        s00 = b[2, 2] - (b[0, 2] * t00 + b[1, 2] * t10)
        s01 = b[2, 3] - (b[0, 2] * t01 + b[1, 2] * t11)
        s11 = b[3, 3] - (b[0, 3] * t01 + b[1, 3] * t11)
        two = 1.0 / (s00 * s11 - s01 * s01)
        e2 = row[2] - (t00 * row[0] + t10 * row[1])
        e3 = row[3] - (t01 * row[0] + t11 * row[1])
        p2, p3 = (s11 * e2 - s01 * e3) * two, (s00 * e3 - s01 * e2) * two
        p0 = (b[1, 1] * row[0] - b[0, 1] * row[1]) * one - (t00 * p2 + t01 * p3)
        p1 = (b[0, 0] * row[1] - b[0, 1] * row[0]) * one - (t10 * p2 + t11 * p3)
        for i in range(i0, n // 8):
            if i == i0 and r == 4:
                continue
            u = [wide(x[i][:, n + k + t:n + k + t + 1]) for t in range(4)]
            step = (u[0] * p0 + u[1] * p1) + (u[2] * p2 + u[3] * p3)
            if i == i0:
                step = jnp.where(sub > r + 3, step, 0.0)
            x[i] = x[i] - step
        for t, (a, c, d, first, second) in enumerate((
            (b[0, 0], b[0, 1], b[1, 1], row[0], row[1]), (s00, s01, s11, e2, e3)
        )):
            root = lax.rsqrt(a)
            off = c * root
            first = first * root
            second = (second - off * first) * lax.rsqrt(d - off * off)
            done[i0] = jnp.where(sub == r + 2 * t, first, jnp.where(sub == r + 2 * t + 1, second, done[i0]))
    return jnp.concatenate(done, axis=0)[:, :n]


def inverse_cholesky(gram):
    half = gram.shape[0] // 2
    upper = inverse_factor(gram[:half, :half])
    across = exact(upper, gram[:half, half:], NN)
    lower = inverse_factor(gram[half:, half:] - exact(across, across, TN))
    corner = -exact(lower, exact(across, upper, TN), NN)
    top = jnp.concatenate([upper, jnp.zeros_like(upper)], axis=1)
    return jnp.concatenate([top, jnp.concatenate([corner, lower], axis=1)], axis=0)


def ortho_kernel(zs, blocks, msg0, msg1, msg2, msg3, ortho):
    inner = lax.axis_index("inner")
    y, z = lax.rem(inner, YS), lax.div(inner, YS)
    rows = NB // (zs * YS)
    summed = blocks[...].reshape(NB, R)
    ortho[...] = exact(summed, inverse_cholesky(exact(summed, summed, TN)), NT)
    high = ortho[...].astype(BF)
    for step, msg in enumerate((msg0, msg1, msg2, msg3)):
        start = pl.multiple_of((z * YS + lax.rem(y + step, YS)) * rows, rows)
        top, low = halves(ortho[pl.ds(start, rows)])
        msg[:NB] = high
        msg[NB:NB + rows] = top
        msg[NB + rows:] = low


def backward_tile(slots, meta, j, mine, group, pairs, held, acc, ready):
    count = live(meta, j)
    acc[...] = jnp.zeros_like(acc)

    def batch(first, _):
        base = first * BATCH
        ready(count, base)
        at = slots_of(j, base, slots, count)
        products = [halves(dot(mine, group[tile_of(meta, slot)])) for slot in at]
        backs = []
        for i in range(BATCH):
            high, low = products[i]
            pair = pairs[at[i]]
            back = dot(high, pair[:R]) + dot(high, pair[R:]) + dot(low, pair[:R])
            backs.append(jnp.where(base + i < count, back, 0.0).astype(BF))
        terms = [
            dot_nt(beside(held[at[i]], held[at[i + 1]]), beside(backs[i], backs[i + 1])) for i in range(0, BATCH, 2)
        ]
        acc[...] += terms[0] + terms[1]
        return 0

    lax.fori_loop(0, (count + BATCH - 1) // BATCH, batch, 0)


def backward_own_kernel(outs, slots, meta, right_v, group, pairs, msg, mine, held, sems):
    fetch(meta, outs, slots, right_v, held, sems)
    y = y_of()

    def ready(count, base):
        for i in range(BATCH):
            arrive(count, slots, y, base + i, right_v, held, sems)

    backward_tile(slots, meta, y, msg[:NB].T, group, pairs, held, mine, ready)

    def tile(order, _):
        j = lax.rem(y + order, YS)

        def one(s, _):
            pltpu.make_async_copy(right_v.at[j, s], held.at[j * slots + s], sems.at[j * slots + s]).wait()
            return 0

        lax.fori_loop(0, live(meta, j), one, 0)
        return 0

    lax.fori_loop(1, YS, tile, 0)


def backward_kernel(slots, zs, meta, held, group, pairs, mine, msg0, msg1, msg2, msg3,
                    own, send1, send2, send3, basis, turned, acc):
    y = y_of()
    rows = NB // (zs * YS)
    for step, msg in enumerate((msg0, msg1, msg2, msg3)):
        j = lax.rem(y + YS - step, YS)
        if step:
            turned[step] = msg[:NB].T
        kept = msg[NB:NB + rows].astype(F32) + msg[NB + rows:].astype(F32)
        basis[j] = kept * math.sqrt(NB)

    def write(j, source):
        for step, out in enumerate((own, send1, send2, send3)):
            there = lax.rem(y + step, YS)
            for block in range(zs):
                start = pl.multiple_of((block * YS + there) * rows, rows)
                out[block, j] = source[pl.ds(start, rows)].astype(out.dtype)

    write(y, mine)

    def tile(step, _):
        j = lax.rem(y + YS - step, YS)
        backward_tile(slots, meta, j, turned[step], group, pairs, held, acc, lambda count, base: None)
        write(j, acc)
        return 0

    lax.fori_loop(1, YS, tile, 0)


def shift_y(array, step, zs):
    pairs = [(z * YS + y, z * YS + (y + step) % YS) for z in range(zs) for y in range(YS)]
    return lax.ppermute(array, "inner", pairs)


def hop(value, step, tiles):
    return lax.ppermute(value, "cols", [(i, (i + 2 * step) % tiles) for i in range(tiles)])


def swap(value, tiles):
    return lax.ppermute(value, "cols", [(i, i ^ 1) for i in range(tiles)])


def over_z(array, zs):
    groups = [[z * YS + y for z in range(zs)] for y in range(YS)]
    return lax.all_to_all(array, "inner", 0, 0, tiled=True, axis_index_groups=groups)


def params():
    return pltpu.CompilerParams(vmem_limit_bytes=20 << 20)


def body(left_u, left_v, right_u, right_v, sketch, tile_index, slot_mask):
    zs = lax.axis_size("inner") // YS
    outs, slots = tile_index.shape
    tiles = lax.axis_size("cols")
    shape = jax.ShapeDtypeStruct
    count = outs * slots
    packed = (tile_index - lax.axis_index("inner") * tiles) * 2 + slot_mask
    right_u = pltpu.with_memory_space_constraint(right_u, pltpu.HBM)
    right_v = pltpu.with_memory_space_constraint(right_v, pltpu.HBM)
    unit = 2 * NB * R * R

    def cost(units, mib):
        return pl.CostEstimate(flops=int(units * unit), bytes_accessed=mib << 20, transcendentals=0)

    near = [hop(value, step, tiles) for value in (left_v, left_u) for step in (1, -1)]
    near_v, near_u = near[:2], near[2:]
    *near_v, sketch, packed = lax.optimization_barrier((*near_v, sketch, packed))
    far_v = hop(near_v[1], -1, tiles)
    sketch = pltpu.with_memory_space_constraint(sketch, pltpu.HBM)
    probes, held_u = pl.pallas_call(
        functools.partial(probe_kernel, outs, slots),
        out_shape=(shape((count, R, 2 * R), BF),) + (shape((count, NB, R), BF),),
        in_specs=[in_smem(), in_place(), in_place(), in_place()],
        out_specs=(in_vmem(),) * 2,
        scratch_shapes=[VMEM((count, NB, R), BF), VMEM((outs, NB, R), BF)]
        + [pltpu.SemaphoreType.DMA((count,))] * 2 + [pltpu.SemaphoreType.DMA],
        compiler_params=params(),
        cost_estimate=cost(outs * slots, 6),
        name="probe",
    )(packed, right_u, right_v, sketch)
    *near_u, far_v, probes = lax.optimization_barrier((*near_u, far_v, probes))
    far_u = hop(near_u[0], 1, tiles)
    group_v = [left_v, *near_v, far_v]
    group_v += [swap(value, tiles) for value in group_v]
    group_u = [left_u, *near_u]
    other_u = [swap(value, tiles) for value in group_u]
    pairs, mixing = pl.pallas_call(
        functools.partial(pair_kernel, outs, slots),
        out_shape=(shape((count, 2 * R, R), BF), shape((count, R, R), BF)),
        in_specs=[in_smem()] + [in_vmem()] * (2 + tiles),
        out_specs=(in_vmem(),) * 2,
        scratch_shapes=[VMEM((tiles, R, NB), BF)],
        compiler_params=params(),
        cost_estimate=cost(outs * slots * 1.75, 10),
        name="pair",
    )(packed, held_u, probes, *group_v)
    far_u, mixing = lax.optimization_barrier((far_u, mixing))
    group_u += [far_u, *other_u, swap(far_u, tiles)]
    own, send1, send2, send3, group = pl.pallas_call(
        functools.partial(sketch_kernel, outs, slots),
        out_shape=(shape((NB, R), F32),) + (shape((NB, R), BF),) * 3 + (shape((tiles, NB, R), BF),),
        in_specs=[in_smem()] + [in_vmem()] * (1 + tiles),
        out_specs=(in_vmem(),) * 5,
        scratch_shapes=[VMEM((NB, R), F32)],
        compiler_params=params(),
        cost_estimate=cost(outs * slots, 4),
        name="sketch",
    )(packed, mixing, *group_u)
    total = own
    for step, send in enumerate((send1, send2, send3)):
        total = total + shift_y(send, step + 1, zs).astype(F32)
    rows = NB // zs
    mine = jnp.sum(over_z(total.reshape(zs, rows, R), zs), axis=0)
    summed = over_z(jnp.broadcast_to(mine[None], (zs, rows, R)), zs)
    out_rows = NB // (zs * YS)
    messages = pl.pallas_call(
        functools.partial(ortho_kernel, zs),
        out_shape=(shape((NB + 2 * out_rows, R), BF),) * YS,
        in_specs=[in_vmem()],
        out_specs=(in_vmem(),) * YS,
        scratch_shapes=[VMEM((NB, R), F32)],
        compiler_params=params(),
        cost_estimate=cost(13, 1),
        name="ortho",
    )(summed)
    mine, held_v = pl.pallas_call(
        functools.partial(backward_own_kernel, outs, slots),
        out_shape=(shape((NB, R), F32), shape((count, NB, R), BF)),
        in_specs=[in_smem(), in_place()] + [in_vmem()] * 3,
        out_specs=(in_vmem(),) * 2,
        scratch_shapes=[pltpu.SemaphoreType.DMA((count,))],
        compiler_params=params(),
        cost_estimate=cost(slots * 2.75, 4),
        name="backward_own",
    )(packed, right_v, group, pairs, messages[0])
    messages = [shift_y(message, step, zs) if step else message for step, message in enumerate(messages)]
    pieces = (zs, outs, out_rows, R)
    own, send1, send2, send3, basis = pl.pallas_call(
        functools.partial(backward_kernel, slots, zs),
        out_shape=(shape(pieces, F32),) + (shape(pieces, BF),) * 3 + (shape((outs, out_rows, R), F32),),
        in_specs=[in_smem()] + [in_vmem()] * (4 + YS),
        out_specs=(in_vmem(),) * 5,
        scratch_shapes=[VMEM((outs, R, NB), BF), VMEM((NB, R), F32)],
        compiler_params=params(),
        cost_estimate=cost(outs * slots * 2, 8),
        name="backward",
    )(packed, held_v, group, pairs, mine, *messages)
    part = own
    for step, send in enumerate((send1, send2, send3)):
        part = part + shift_y(send, step + 1, zs).astype(F32)
    coeff = jnp.sum(over_z(part, zs), axis=0)
    return (basis, coeff)


def solution(mesh):
    return jax.shard_map(
        body,
        mesh=mesh,
        in_specs=(
            P(("inner", "cols"), None, None),
            P(("inner", "cols"), None, None),
            P("cols", "inner", None, None),
            P("cols", "inner", None, None),
            P("cols", None, None),
            P("cols", "inner"),
            P("cols", "inner"),
        ),
        out_specs=(P("cols", "inner", None), P("cols", "inner", None)),
        check_vma=False,
    )
```

```python
import functools
import math

import jax
import jax.numpy as jnp
from jax import lax
from jax.experimental import pallas as pl
from jax.experimental.pallas import tpu as pltpu
from jax.sharding import PartitionSpec as P

NB = 512
R = 128
YS = 4
BATCH = 4
HIGH = lax.Precision.HIGHEST
BF = jnp.bfloat16
F32 = jnp.float32
VMEM = pltpu.VMEM
NN = (((1,), (0,)), ((), ()))
NT = (((1,), (1,)), ((), ()))
TN = (((0,), (0,)), ((), ()))


def dot(a, b):
    return jnp.dot(a, b, preferred_element_type=F32)


def dot_nt(a, b):
    return lax.dot_general(a, b, NT, preferred_element_type=F32)


def halves(a):
    high = a.astype(BF)
    return high, (a - high.astype(F32)).astype(BF)


def in_vmem():
    return pl.BlockSpec(memory_space=VMEM)


def in_place():
    return pl.BlockSpec(memory_space=pltpu.HBM)


def in_smem():
    return pl.BlockSpec(memory_space=pltpu.SMEM)


def live(packed, j):
    count = packed[j, 0] & 1
    for s in range(1, packed.shape[1]):
        count += packed[j, s] & 1
    return count


def tile_of(packed, at):
    slots = packed.shape[1]
    return packed[lax.div(at, slots), lax.rem(at, slots)] >> 1


def y_of():
    return lax.rem(lax.axis_index("inner"), YS)


def fetch(meta, outs, slots, source, held, sems):
    def tile(j, _):
        def one(s, _):
            pltpu.make_async_copy(source.at[j, s], held.at[j * slots + s], sems.at[j * slots + s]).start()
            return 0

        lax.fori_loop(0, live(meta, j), one, 0)
        return 0

    lax.fori_loop(0, outs, tile, 0)


def arrive(count, slots, j, s, source, held, sems):
    @pl.when(s < count)
    def _():
        pltpu.make_async_copy(source.at[j, s], held.at[j * slots + s], sems.at[j * slots + s]).wait()


def beside(a, b):
    return jnp.concatenate([a, b], axis=1)


def above(a, b):
    return jnp.concatenate([a, b], axis=0)


def sweep(meta, together, work):
    for tiles in together:
        work([(place, j, 0, live(meta, j)) for place, j in tiles], True)

    def rest(place, j):
        count = live(meta, j)

        def batch(first, _):
            work([(place, j, first * BATCH, count)], False)
            return 0

        lax.fori_loop(1, (count + BATCH - 1) // BATCH, batch, 0)

    for tiles in together:
        for place, j in tiles:
            rest(place, j)


def batches(items, slots):
    return [
        (j * slots + jnp.minimum(base + i, count - 1), j * slots + base + i, base + i < count)
        for _, j, base, count in items for i in range(BATCH)
    ]


def two_by_two(tiles):
    return [tiles[:2], tiles[2:]]


def probe_kernel(outs, slots, meta, right_u, right_v, sketch, probes, held_u, held, plain, sems_u, sems, sem):
    copy = pltpu.make_async_copy(sketch, plain, sem)
    copy.start()
    fetch(meta, outs, slots, right_v, held, sems)
    fetch(meta, outs, slots, right_u, held_u, sems_u)
    copy.wait()

    def work(items, first):
        for _, j, base, count in items:
            for i in range(BATCH):
                arrive(count, slots, j, base + i, right_v, held, sems)
        turned = [plain[j].T for _, j, _, _ in items]
        at = batches(items, slots)
        products = [dot(turned[n // BATCH], held[slot]) for n, (slot, _, _) in enumerate(at)]
        for (slot, _, _), product in zip(at, products):
            probes[slot] = beside(*halves(product))

    sweep(meta, two_by_two([(j, j) for j in range(outs)]), work)

    def tile(j, _):
        def one(s, _):
            pltpu.make_async_copy(right_u.at[j, s], held_u.at[j * slots + s], sems_u.at[j * slots + s]).wait()
            return 0

        lax.fori_loop(0, live(meta, j), one, 0)
        return 0

    lax.fori_loop(0, outs, tile, 0)


def tile_ids(tiles):
    me = lax.axis_index("cols")
    return [lax.rem(me + 2 * hop, tiles) ^ flip for flip in (0, 1) for hop in (0, tiles // 2 - 1, 1, 2)]


def pair_kernel(outs, slots, meta, held, probes, *rest):
    parts, (pairs, mixing, turned) = rest[:-3], rest[-3:]
    for k, part in zip(tile_ids(len(parts)), parts):
        turned[k] = part[0].T

    def work(items, first):
        at = batches(items, slots)
        products = [halves(dot(turned[tile_of(meta, slot)], held[slot])) for slot, _, _ in at]
        mixes = []
        for (slot, _, _), (high, low) in zip(at, products):
            probe = probes[slot]
            mixes.append(dot_nt(high, probe[:, :R]) + dot_nt(high, probe[:, R:]) + dot_nt(low, probe[:, :R]))
        for (slot, place, alive), product, mixed in zip(at, products, mixes):
            pairs[slot] = above(*product)
            mixing[place] = jnp.where(alive, mixed, 0.0).astype(BF)

    sweep(meta, two_by_two([(j, j) for j in range(outs)]), work)


def sketch_kernel(outs, slots, meta, mixing, *rest):
    parts, (own, send1, send2, send3, group, acc) = rest[:-6], rest[-6:]
    for k, part in zip(tile_ids(len(parts)), parts):
        group[k] = part[0]
    y = y_of()

    def work(items, first):
        at = batches(items, slots)
        tiles = [group[tile_of(meta, slot)] for slot, _, _ in at]
        terms = [
            dot(beside(tiles[i], tiles[i + 1]), above(mixing[at[i][1]], mixing[at[i + 1][1]]))
            for i in range(0, len(at), 2)
        ]
        for n, (place, _, _, _) in enumerate(items):
            term = terms[2 * n] + terms[2 * n + 1]
            acc[place] = term if first else acc[place] + term

    sweep(meta, two_by_two([(step, lax.rem(y + step, YS)) for step in range(YS)]), work)
    for step, out in enumerate((own, send1, send2, send3)):
        out[...] = acc[step].astype(out.dtype)


def exact(a, b, dims):
    return lax.dot_general(a, b, dims, precision=HIGH, preferred_element_type=F32)


def inverse_factor(block):
    n = block.shape[0]
    lanes = 2 * n
    same = lax.broadcasted_iota(jnp.int32, (n, n), 0) == lax.broadcasted_iota(jnp.int32, (n, n), 1)
    full = jnp.concatenate([same.astype(F32), block], axis=1)
    x = [full[8 * i:8 * i + 8] for i in range(n // 8)]
    done = list(x)
    sub = lax.broadcasted_iota(jnp.int32, (8, lanes), 0)

    def wide(v):
        return jnp.broadcast_to(v, (8, lanes))

    for k in range(0, n, 4):
        i0, r = k // 8, k % 8
        row = [wide(x[i0][r + t:r + t + 1]) for t in range(4)]
        b = {(t, u): wide(row[t][:, n + k + u:n + k + u + 1]) for t in range(4) for u in range(t, 4)}
        one = 1.0 / (b[0, 0] * b[1, 1] - b[0, 1] * b[0, 1])
        t00 = (b[1, 1] * b[0, 2] - b[0, 1] * b[1, 2]) * one
        t01 = (b[1, 1] * b[0, 3] - b[0, 1] * b[1, 3]) * one
        t10 = (b[0, 0] * b[1, 2] - b[0, 1] * b[0, 2]) * one
        t11 = (b[0, 0] * b[1, 3] - b[0, 1] * b[0, 3]) * one
        s00 = b[2, 2] - (b[0, 2] * t00 + b[1, 2] * t10)
        s01 = b[2, 3] - (b[0, 2] * t01 + b[1, 2] * t11)
        s11 = b[3, 3] - (b[0, 3] * t01 + b[1, 3] * t11)
        two = 1.0 / (s00 * s11 - s01 * s01)
        e2 = row[2] - (t00 * row[0] + t10 * row[1])
        e3 = row[3] - (t01 * row[0] + t11 * row[1])
        p2, p3 = (s11 * e2 - s01 * e3) * two, (s00 * e3 - s01 * e2) * two
        p0 = (b[1, 1] * row[0] - b[0, 1] * row[1]) * one - (t00 * p2 + t01 * p3)
        p1 = (b[0, 0] * row[1] - b[0, 1] * row[0]) * one - (t10 * p2 + t11 * p3)
        for i in range(i0, n // 8):
            if i == i0 and r == 4:
                continue
            u = [wide(x[i][:, n + k + t:n + k + t + 1]) for t in range(4)]
            step = (u[0] * p0 + u[1] * p1) + (u[2] * p2 + u[3] * p3)
            if i == i0:
                step = jnp.where(sub > r + 3, step, 0.0)
            x[i] = x[i] - step
        for t, (a, c, d, first, second) in enumerate((
            (b[0, 0], b[0, 1], b[1, 1], row[0], row[1]), (s00, s01, s11, e2, e3)
        )):
            root = lax.rsqrt(a)
            off = c * root
            first = first * root
            second = (second - off * first) * lax.rsqrt(d - off * off)
            done[i0] = jnp.where(sub == r + 2 * t, first, jnp.where(sub == r + 2 * t + 1, second, done[i0]))
    return jnp.concatenate(done, axis=0)[:, :n]


def inverse_cholesky(gram):
    half = gram.shape[0] // 2
    upper = inverse_factor(gram[:half, :half])
    across = exact(upper, gram[:half, half:], NN)
    lower = inverse_factor(gram[half:, half:] - exact(across, across, TN))
    corner = -exact(lower, exact(across, upper, TN), NN)
    top = jnp.concatenate([upper, jnp.zeros_like(upper)], axis=1)
    return jnp.concatenate([top, jnp.concatenate([corner, lower], axis=1)], axis=0)


def ortho_kernel(zs, blocks, msg0, msg1, msg2, msg3, ortho):
    inner = lax.axis_index("inner")
    y, z = lax.rem(inner, YS), lax.div(inner, YS)
    rows = NB // (zs * YS)
    summed = blocks[...].reshape(NB, R)
    ortho[...] = exact(summed, inverse_cholesky(exact(summed, summed, TN)), NT)
    high = ortho[...].astype(BF)
    for step, msg in enumerate((msg0, msg1, msg2, msg3)):
        start = pl.multiple_of((z * YS + lax.rem(y + step, YS)) * rows, rows)
        top, low = halves(ortho[pl.ds(start, rows)])
        msg[:NB] = high
        msg[NB:NB + rows] = top
        msg[NB + rows:] = low


def backward_work(slots, meta, turned, group, pairs, held, acc, items, first):
    at = batches(items, slots)
    mine = [turned[place] for place, _, _, _ in items]
    products = [halves(dot(mine[n // BATCH], group[tile_of(meta, slot)])) for n, (slot, _, _) in enumerate(at)]
    backs = []
    for (slot, _, alive), (high, low) in zip(at, products):
        pair = pairs[slot]
        back = dot(high, pair[:R]) + dot(high, pair[R:]) + dot(low, pair[:R])
        backs.append(jnp.where(alive, back, 0.0).astype(BF))
    terms = [
        dot_nt(beside(held[at[i][0]], held[at[i + 1][0]]), beside(backs[i], backs[i + 1]))
        for i in range(0, len(at), 2)
    ]
    for n, (place, _, _, _) in enumerate(items):
        term = terms[2 * n] + terms[2 * n + 1]
        acc[place] = term if first else acc[place] + term


def backward_own_kernel(outs, slots, meta, right_v, group, pairs, msg, mine, held, turned, sems):
    fetch(meta, outs, slots, right_v, held, sems)
    y = y_of()
    turned[0] = msg[:NB].T

    def work(items, first):
        for _, j, base, count in items:
            for i in range(BATCH):
                arrive(count, slots, j, base + i, right_v, held, sems)
        backward_work(slots, meta, turned, group, pairs, held, mine, items, first)

    sweep(meta, [[(0, y)]], work)

    def tile(order, _):
        j = lax.rem(y + order, YS)

        def one(s, _):
            pltpu.make_async_copy(right_v.at[j, s], held.at[j * slots + s], sems.at[j * slots + s]).wait()
            return 0

        lax.fori_loop(0, live(meta, j), one, 0)
        return 0

    lax.fori_loop(1, YS, tile, 0)


def backward_kernel(slots, zs, meta, held, group, pairs, mine, msg0, msg1, msg2, msg3,
                    own, send1, send2, send3, basis, turned, acc):
    y = y_of()
    rows = NB // (zs * YS)
    tiles = [lax.rem(y + YS - step, YS) for step in range(YS)]
    for step, msg in enumerate((msg0, msg1, msg2, msg3)):
        if step:
            turned[step] = msg[:NB].T
        kept = msg[NB:NB + rows].astype(F32) + msg[NB + rows:].astype(F32)
        basis[tiles[step]] = kept * math.sqrt(NB)

    def work(items, first):
        backward_work(slots, meta, turned, group, pairs, held, acc, items, first)

    sweep(meta, [[(step, tiles[step]) for step in range(1, YS)]], work)
    acc[0] = mine[0]
    for step, out in enumerate((own, send1, send2, send3)):
        there = lax.rem(y + step, YS)
        for block in range(zs):
            start = pl.multiple_of((block * YS + there) * rows, rows)
            for place in range(YS):
                out[block, tiles[place]] = acc[place, pl.ds(start, rows)].astype(out.dtype)


def shift_y(array, step, zs):
    pairs = [(z * YS + y, z * YS + (y + step) % YS) for z in range(zs) for y in range(YS)]
    return lax.ppermute(array, "inner", pairs)


def hop(value, step, tiles):
    return lax.ppermute(value, "cols", [(i, (i + 2 * step) % tiles) for i in range(tiles)])


def swap(value, tiles):
    return lax.ppermute(value, "cols", [(i, i ^ 1) for i in range(tiles)])


def spread(sends, zs):
    got = {step: shift_y(sends[step - 1], step, zs) for step in (2, 1, 3)}
    return [got[step] for step in (1, 2, 3)]


def over_z(array, zs):
    groups = [[z * YS + y for z in range(zs)] for y in range(YS)]
    return lax.all_to_all(array, "inner", 0, 0, tiled=True, axis_index_groups=groups)


def params():
    return pltpu.CompilerParams(vmem_limit_bytes=20 << 20)


def body(left_u, left_v, right_u, right_v, sketch, tile_index, slot_mask):
    zs = lax.axis_size("inner") // YS
    outs, slots = tile_index.shape
    tiles = lax.axis_size("cols")
    shape = jax.ShapeDtypeStruct
    count = outs * slots
    packed = (tile_index - lax.axis_index("inner") * tiles) * 2 + slot_mask
    right_u = pltpu.with_memory_space_constraint(right_u, pltpu.HBM)
    right_v = pltpu.with_memory_space_constraint(right_v, pltpu.HBM)
    unit = 2 * NB * R * R

    def cost(units, mib):
        return pl.CostEstimate(flops=int(units * unit), bytes_accessed=mib << 20, transcendentals=0)

    near = [hop(value, step, tiles) for value in (left_v, left_u) for step in (1, -1)]
    near_v, near_u = near[:2], near[2:]
    *near_v, sketch, packed = lax.optimization_barrier((*near_v, sketch, packed))
    far_v = hop(near_v[1], -1, tiles)
    sketch = pltpu.with_memory_space_constraint(sketch, pltpu.HBM)
    probes, held_u = pl.pallas_call(
        functools.partial(probe_kernel, outs, slots),
        out_shape=(shape((count, R, 2 * R), BF),) + (shape((count, NB, R), BF),),
        in_specs=[in_smem(), in_place(), in_place(), in_place()],
        out_specs=(in_vmem(),) * 2,
        scratch_shapes=[VMEM((count, NB, R), BF), VMEM((outs, NB, R), BF)]
        + [pltpu.SemaphoreType.DMA((count,))] * 2 + [pltpu.SemaphoreType.DMA],
        compiler_params=params(),
        cost_estimate=cost(outs * slots, 6),
        name="probe",
    )(packed, right_u, right_v, sketch)
    *near_u, far_v, probes = lax.optimization_barrier((*near_u, far_v, probes))
    far_u = hop(near_u[0], 1, tiles)
    group_v = [left_v, *near_v, far_v]
    group_v += [swap(value, tiles) for value in group_v]
    group_u = [left_u, *near_u]
    other_u = [swap(value, tiles) for value in group_u]
    pairs, mixing = pl.pallas_call(
        functools.partial(pair_kernel, outs, slots),
        out_shape=(shape((count, 2 * R, R), BF), shape((count, R, R), BF)),
        in_specs=[in_smem()] + [in_vmem()] * (2 + tiles),
        out_specs=(in_vmem(),) * 2,
        scratch_shapes=[VMEM((tiles, R, NB), BF)],
        compiler_params=params(),
        cost_estimate=cost(outs * slots * 1.75, 10),
        name="pair",
    )(packed, held_u, probes, *group_v)
    far_u, mixing = lax.optimization_barrier((far_u, mixing))
    group_u += [far_u, *other_u, swap(far_u, tiles)]
    own, send1, send2, send3, group = pl.pallas_call(
        functools.partial(sketch_kernel, outs, slots),
        out_shape=(shape((NB, R), F32),) + (shape((NB, R), BF),) * 3 + (shape((tiles, NB, R), BF),),
        in_specs=[in_smem()] + [in_vmem()] * (1 + tiles),
        out_specs=(in_vmem(),) * 5,
        scratch_shapes=[VMEM((YS, NB, R), F32)],
        compiler_params=params(),
        cost_estimate=cost(outs * slots, 4),
        name="sketch",
    )(packed, mixing, *group_u)
    total = own
    for got in spread((send1, send2, send3), zs):
        total = total + got.astype(F32)
    rows = NB // zs
    mine = jnp.sum(over_z(total.reshape(zs, rows, R), zs), axis=0)
    summed = over_z(jnp.broadcast_to(mine[None], (zs, rows, R)), zs)
    out_rows = NB // (zs * YS)
    messages = pl.pallas_call(
        functools.partial(ortho_kernel, zs),
        out_shape=(shape((NB + 2 * out_rows, R), BF),) * YS,
        in_specs=[in_vmem()],
        out_specs=(in_vmem(),) * YS,
        scratch_shapes=[VMEM((NB, R), F32)],
        compiler_params=params(),
        cost_estimate=cost(13, 1),
        name="ortho",
    )(summed)
    mine, held_v = pl.pallas_call(
        functools.partial(backward_own_kernel, outs, slots),
        out_shape=(shape((1, NB, R), F32), shape((count, NB, R), BF)),
        in_specs=[in_smem(), in_place()] + [in_vmem()] * 3,
        out_specs=(in_vmem(),) * 2,
        scratch_shapes=[VMEM((1, R, NB), BF), pltpu.SemaphoreType.DMA((count,))],
        compiler_params=params(),
        cost_estimate=cost(slots * 2.75, 4),
        name="backward_own",
    )(packed, right_v, group, pairs, messages[0])
    messages = [messages[0]] + spread(messages[1:], zs)
    pieces = (zs, outs, out_rows, R)
    own, send1, send2, send3, basis = pl.pallas_call(
        functools.partial(backward_kernel, slots, zs),
        out_shape=(shape(pieces, F32),) + (shape(pieces, BF),) * 3 + (shape((outs, out_rows, R), F32),),
        in_specs=[in_smem()] + [in_vmem()] * (4 + YS),
        out_specs=(in_vmem(),) * 5,
        scratch_shapes=[VMEM((YS, R, NB), BF), VMEM((YS, NB, R), F32)],
        compiler_params=params(),
        cost_estimate=cost(outs * slots * 2, 8),
        name="backward",
    )(packed, held_v, group, pairs, mine, *messages)
    part = own
    for got in spread((send1, send2, send3), zs):
        part = part + got.astype(F32)
    coeff = jnp.sum(over_z(part, zs), axis=0)
    return (basis, coeff)


def solution(mesh):
    return jax.shard_map(
        body,
        mesh=mesh,
        in_specs=(
            P(("inner", "cols"), None, None),
            P(("inner", "cols"), None, None),
            P("cols", "inner", None, None),
            P("cols", "inner", None, None),
            P("cols", None, None),
            P("cols", "inner"),
            P("cols", "inner"),
        ),
        out_specs=(P("cols", "inner", None), P("cols", "inner", None)),
        check_vma=False,
    )
```

```python
import functools
import math

import jax
import jax.numpy as jnp
from jax import lax
from jax.experimental import pallas as pl
from jax.experimental.pallas import tpu as pltpu
from jax.sharding import PartitionSpec as P

NB = 512
R = 128
YS = 4
BATCH = 4
HIGH = lax.Precision.HIGHEST
BF = jnp.bfloat16
F32 = jnp.float32
VMEM = pltpu.VMEM
NN = (((1,), (0,)), ((), ()))
NT = (((1,), (1,)), ((), ()))
TN = (((0,), (0,)), ((), ()))


def dot(a, b):
    return jnp.dot(a, b, preferred_element_type=F32)


def dot_nt(a, b):
    return lax.dot_general(a, b, NT, preferred_element_type=F32)


def halves(a):
    high = a.astype(BF)
    return high, (a - high.astype(F32)).astype(BF)


def in_vmem():
    return pl.BlockSpec(memory_space=VMEM)


def in_place():
    return pl.BlockSpec(memory_space=pltpu.HBM)


def in_smem():
    return pl.BlockSpec(memory_space=pltpu.SMEM)


def live(packed, j):
    count = packed[j, 0] & 1
    for s in range(1, packed.shape[1]):
        count += packed[j, s] & 1
    return count


def tile_of(packed, at):
    slots = packed.shape[1]
    return packed[lax.div(at, slots), lax.rem(at, slots)] >> 1


def y_of():
    return lax.rem(lax.axis_index("inner"), YS)


def fetch(meta, outs, slots, source, held, sems):
    def tile(j, _):
        def one(s, _):
            pltpu.make_async_copy(source.at[j, s], held.at[j * slots + s], sems.at[j * slots + s]).start()
            return 0

        lax.fori_loop(0, live(meta, j), one, 0)
        return 0

    lax.fori_loop(0, outs, tile, 0)


def arrive(count, slots, j, s, source, held, sems):
    @pl.when(s < count)
    def _():
        pltpu.make_async_copy(source.at[j, s], held.at[j * slots + s], sems.at[j * slots + s]).wait()


def beside(a, b):
    return jnp.concatenate([a, b], axis=1)


def above(a, b):
    return jnp.concatenate([a, b], axis=0)


def sweep(meta, together, work):
    for tiles in together:
        work([(place, j, 0, live(meta, j)) for place, j in tiles], True)

    def rest(place, j):
        count = live(meta, j)

        def batch(first, _):
            work([(place, j, first * BATCH, count)], False)
            return 0

        lax.fori_loop(1, (count + BATCH - 1) // BATCH, batch, 0)

    for tiles in together:
        for place, j in tiles:
            rest(place, j)


def batches(items, slots):
    return [
        (j * slots + jnp.minimum(base + i, count - 1), j * slots + base + i, base + i < count)
        for _, j, base, count in items for i in range(BATCH)
    ]


def two_by_two(tiles):
    return [tiles[:2], tiles[2:]]


def load_kernel(outs, slots, meta, right_u, right_v, sketch, held_u, held_v, plain, sems_u, sems_v, sem):
    copy = pltpu.make_async_copy(sketch, plain, sem)
    copy.start()
    fetch(meta, outs, slots, right_v, held_v, sems_v)
    fetch(meta, outs, slots, right_u, held_u, sems_u)
    copy.wait()

    def tile(j, _):
        def one(s, _):
            at = j * slots + s
            pltpu.make_async_copy(right_v.at[j, s], held_v.at[at], sems_v.at[at]).wait()
            pltpu.make_async_copy(right_u.at[j, s], held_u.at[at], sems_u.at[at]).wait()
            return 0

        lax.fori_loop(0, live(meta, j), one, 0)
        return 0

    lax.fori_loop(0, outs, tile, 0)


def probe_kernel(outs, slots, meta, held, sketch, probes):
    def work(items, first):
        turned = [sketch[j].T for _, j, _, _ in items]
        at = batches(items, slots)
        products = [dot(turned[n // BATCH], held[slot]) for n, (slot, _, _) in enumerate(at)]
        for (slot, _, _), product in zip(at, products):
            probes[slot] = beside(*halves(product))

    sweep(meta, two_by_two([(j, j) for j in range(outs)]), work)


def tile_ids(tiles):
    me = lax.axis_index("cols")
    return [lax.rem(me + 2 * hop, tiles) ^ flip for flip in (0, 1) for hop in (0, tiles // 2 - 1, 1, 2)]


def pair_kernel(outs, slots, meta, held, probes, *rest):
    parts, (pairs, mixing, turned) = rest[:-3], rest[-3:]
    for k, part in zip(tile_ids(len(parts)), parts):
        turned[k] = part[0].T

    def work(items, first):
        at = batches(items, slots)
        products = [halves(dot(turned[tile_of(meta, slot)], held[slot])) for slot, _, _ in at]
        mixes = []
        for (slot, _, _), (high, low) in zip(at, products):
            probe = probes[slot]
            mixes.append(dot_nt(high, probe[:, :R]) + dot_nt(high, probe[:, R:]) + dot_nt(low, probe[:, :R]))
        for (slot, place, alive), product, mixed in zip(at, products, mixes):
            pairs[slot] = above(*product)
            mixing[place] = jnp.where(alive, mixed, 0.0).astype(BF)

    sweep(meta, two_by_two([(j, j) for j in range(outs)]), work)


def sketch_kernel(outs, slots, meta, mixing, *rest):
    parts, (own, send1, send2, send3, group, acc) = rest[:-6], rest[-6:]
    for k, part in zip(tile_ids(len(parts)), parts):
        group[k] = part[0]
    y = y_of()

    def work(items, first):
        at = batches(items, slots)
        tiles = [group[tile_of(meta, slot)] for slot, _, _ in at]
        terms = [
            dot(beside(tiles[i], tiles[i + 1]), above(mixing[at[i][1]], mixing[at[i + 1][1]]))
            for i in range(0, len(at), 2)
        ]
        for n, (place, _, _, _) in enumerate(items):
            term = terms[2 * n] + terms[2 * n + 1]
            acc[place] = term if first else acc[place] + term

    sweep(meta, two_by_two([(step, lax.rem(y + step, YS)) for step in range(YS)]), work)
    for step, out in enumerate((own, send1, send2, send3)):
        out[...] = acc[step].astype(out.dtype)


def exact(a, b, dims):
    return lax.dot_general(a, b, dims, precision=HIGH, preferred_element_type=F32)


def inverse_factor(block):
    n = block.shape[0]
    lanes = 2 * n
    same = lax.broadcasted_iota(jnp.int32, (n, n), 0) == lax.broadcasted_iota(jnp.int32, (n, n), 1)
    full = jnp.concatenate([same.astype(F32), block], axis=1)
    x = [full[8 * i:8 * i + 8] for i in range(n // 8)]
    done = list(x)
    sub = lax.broadcasted_iota(jnp.int32, (8, lanes), 0)

    def wide(v):
        return jnp.broadcast_to(v, (8, lanes))

    for k in range(0, n, 4):
        i0, r = k // 8, k % 8
        row = [wide(x[i0][r + t:r + t + 1]) for t in range(4)]
        b = {(t, u): wide(row[t][:, n + k + u:n + k + u + 1]) for t in range(4) for u in range(t, 4)}
        one = 1.0 / (b[0, 0] * b[1, 1] - b[0, 1] * b[0, 1])
        t00 = (b[1, 1] * b[0, 2] - b[0, 1] * b[1, 2]) * one
        t01 = (b[1, 1] * b[0, 3] - b[0, 1] * b[1, 3]) * one
        t10 = (b[0, 0] * b[1, 2] - b[0, 1] * b[0, 2]) * one
        t11 = (b[0, 0] * b[1, 3] - b[0, 1] * b[0, 3]) * one
        s00 = b[2, 2] - (b[0, 2] * t00 + b[1, 2] * t10)
        s01 = b[2, 3] - (b[0, 2] * t01 + b[1, 2] * t11)
        s11 = b[3, 3] - (b[0, 3] * t01 + b[1, 3] * t11)
        two = 1.0 / (s00 * s11 - s01 * s01)
        e2 = row[2] - (t00 * row[0] + t10 * row[1])
        e3 = row[3] - (t01 * row[0] + t11 * row[1])
        p2, p3 = (s11 * e2 - s01 * e3) * two, (s00 * e3 - s01 * e2) * two
        p0 = (b[1, 1] * row[0] - b[0, 1] * row[1]) * one - (t00 * p2 + t01 * p3)
        p1 = (b[0, 0] * row[1] - b[0, 1] * row[0]) * one - (t10 * p2 + t11 * p3)
        for i in range(i0, n // 8):
            if i == i0 and r == 4:
                continue
            u = [wide(x[i][:, n + k + t:n + k + t + 1]) for t in range(4)]
            step = (u[0] * p0 + u[1] * p1) + (u[2] * p2 + u[3] * p3)
            if i == i0:
                step = jnp.where(sub > r + 3, step, 0.0)
            x[i] = x[i] - step
        for t, (a, c, d, first, second) in enumerate((
            (b[0, 0], b[0, 1], b[1, 1], row[0], row[1]), (s00, s01, s11, e2, e3)
        )):
            root = lax.rsqrt(a)
            off = c * root
            first = first * root
            second = (second - off * first) * lax.rsqrt(d - off * off)
            done[i0] = jnp.where(sub == r + 2 * t, first, jnp.where(sub == r + 2 * t + 1, second, done[i0]))
    return jnp.concatenate(done, axis=0)[:, :n]


def inverse_cholesky(gram):
    half = gram.shape[0] // 2
    upper = inverse_factor(gram[:half, :half])
    across = exact(upper, gram[:half, half:], NN)
    lower = inverse_factor(gram[half:, half:] - exact(across, across, TN))
    corner = -exact(lower, exact(across, upper, TN), NN)
    top = jnp.concatenate([upper, jnp.zeros_like(upper)], axis=1)
    return jnp.concatenate([top, jnp.concatenate([corner, lower], axis=1)], axis=0)


def ortho_kernel(zs, blocks, msg0, msg1, msg2, msg3, ortho):
    inner = lax.axis_index("inner")
    y, z = lax.rem(inner, YS), lax.div(inner, YS)
    rows = NB // (zs * YS)
    summed = blocks[...].reshape(NB, R)
    ortho[...] = exact(summed, inverse_cholesky(exact(summed, summed, TN)), NT)
    high = ortho[...].astype(BF)
    for step, msg in enumerate((msg0, msg1, msg2, msg3)):
        start = pl.multiple_of((z * YS + lax.rem(y + step, YS)) * rows, rows)
        top, low = halves(ortho[pl.ds(start, rows)])
        msg[:NB] = high
        msg[NB:NB + rows] = top
        msg[NB + rows:] = low


def backward_work(slots, meta, turned, group, pairs, held, acc, items, first):
    at = batches(items, slots)
    mine = [turned[place] for place, _, _, _ in items]
    products = [halves(dot(mine[n // BATCH], group[tile_of(meta, slot)])) for n, (slot, _, _) in enumerate(at)]
    backs = []
    for (slot, _, alive), (high, low) in zip(at, products):
        pair = pairs[slot]
        back = dot(high, pair[:R]) + dot(high, pair[R:]) + dot(low, pair[:R])
        backs.append(jnp.where(alive, back, 0.0).astype(BF))
    terms = [
        dot_nt(beside(held[at[i][0]], held[at[i + 1][0]]), beside(backs[i], backs[i + 1]))
        for i in range(0, len(at), 2)
    ]
    for n, (place, _, _, _) in enumerate(items):
        term = terms[2 * n] + terms[2 * n + 1]
        acc[place] = term if first else acc[place] + term


def backward_own_kernel(outs, slots, meta, right_v, group, pairs, msg, mine, held, turned, sems):
    fetch(meta, outs, slots, right_v, held, sems)
    y = y_of()
    turned[0] = msg[:NB].T

    def work(items, first):
        for _, j, base, count in items:
            for i in range(BATCH):
                arrive(count, slots, j, base + i, right_v, held, sems)
        backward_work(slots, meta, turned, group, pairs, held, mine, items, first)

    sweep(meta, [[(0, y)]], work)

    def tile(order, _):
        j = lax.rem(y + order, YS)

        def one(s, _):
            pltpu.make_async_copy(right_v.at[j, s], held.at[j * slots + s], sems.at[j * slots + s]).wait()
            return 0

        lax.fori_loop(0, live(meta, j), one, 0)
        return 0

    lax.fori_loop(1, YS, tile, 0)


def backward_kernel(slots, zs, meta, held, group, pairs, mine, msg0, msg1, msg2, msg3,
                    own, send1, send2, send3, basis, turned, acc):
    y = y_of()
    rows = NB // (zs * YS)
    tiles = [lax.rem(y + YS - step, YS) for step in range(YS)]
    for step, msg in enumerate((msg0, msg1, msg2, msg3)):
        if step:
            turned[step] = msg[:NB].T
        kept = msg[NB:NB + rows].astype(F32) + msg[NB + rows:].astype(F32)
        basis[tiles[step]] = kept * math.sqrt(NB)

    def work(items, first):
        backward_work(slots, meta, turned, group, pairs, held, acc, items, first)

    sweep(meta, [[(step, tiles[step]) for step in range(1, YS)]], work)
    acc[0] = mine[0]
    for step, out in enumerate((own, send1, send2, send3)):
        there = lax.rem(y + step, YS)
        for block in range(zs):
            start = pl.multiple_of((block * YS + there) * rows, rows)
            for place in range(YS):
                out[block, tiles[place]] = acc[place, pl.ds(start, rows)].astype(out.dtype)


def shift_y(array, step, zs):
    pairs = [(z * YS + y, z * YS + (y + step) % YS) for z in range(zs) for y in range(YS)]
    return lax.ppermute(array, "inner", pairs)


def hop(value, step, tiles):
    return lax.ppermute(value, "cols", [(i, (i + 2 * step) % tiles) for i in range(tiles)])


def swap(value, tiles):
    return lax.ppermute(value, "cols", [(i, i ^ 1) for i in range(tiles)])


def spread(sends, zs):
    got = {step: shift_y(sends[step - 1], step, zs) for step in (2, 1, 3)}
    return [got[step] for step in (1, 2, 3)]


def over_z(array, zs):
    groups = [[z * YS + y for z in range(zs)] for y in range(YS)]
    return lax.all_to_all(array, "inner", 0, 0, tiled=True, axis_index_groups=groups)


def params():
    return pltpu.CompilerParams(vmem_limit_bytes=20 << 20)


def body(left_u, left_v, right_u, right_v, sketch, tile_index, slot_mask):
    zs = lax.axis_size("inner") // YS
    outs, slots = tile_index.shape
    tiles = lax.axis_size("cols")
    shape = jax.ShapeDtypeStruct
    count = outs * slots
    packed = (tile_index - lax.axis_index("inner") * tiles) * 2 + slot_mask
    right_u = pltpu.with_memory_space_constraint(right_u, pltpu.HBM)
    right_v = pltpu.with_memory_space_constraint(right_v, pltpu.HBM)
    unit = 2 * NB * R * R

    def cost(units, mib):
        return pl.CostEstimate(flops=int(units * unit), bytes_accessed=mib << 20, transcendentals=0)

    near = [hop(value, step, tiles) for value in (left_v, left_u) for step in (1, -1)]
    near_v, near_u = near[:2], near[2:]
    sketch = pltpu.with_memory_space_constraint(sketch, pltpu.HBM)
    held_u, held_v, sketch = pl.pallas_call(
        functools.partial(load_kernel, outs, slots),
        out_shape=(shape((count, NB, R), BF),) * 2 + (shape(sketch.shape, BF),),
        in_specs=[in_smem()] + [in_place()] * 3,
        out_specs=(in_vmem(),) * 3,
        scratch_shapes=[pltpu.SemaphoreType.DMA((count,))] * 2 + [pltpu.SemaphoreType.DMA],
        compiler_params=params(),
        cost_estimate=cost(0, 9),
        name="load",
    )(packed, right_u, right_v, sketch)
    *near_v, sketch = lax.optimization_barrier((*near_v, sketch))
    far_v = hop(near_v[1], -1, tiles)
    probes = pl.pallas_call(
        functools.partial(probe_kernel, outs, slots),
        out_shape=shape((count, R, 2 * R), BF),
        in_specs=[in_smem()] + [in_vmem()] * 2,
        out_specs=in_vmem(),
        compiler_params=params(),
        cost_estimate=cost(outs * slots, 6),
        name="probe",
    )(packed, held_v, sketch)
    *near_u, far_v, probes = lax.optimization_barrier((*near_u, far_v, probes))
    far_u = hop(near_u[0], 1, tiles)
    group_v = [left_v, *near_v, far_v]
    group_v += [swap(value, tiles) for value in group_v]
    group_u = [left_u, *near_u]
    other_u = [swap(value, tiles) for value in group_u]
    pairs, mixing = pl.pallas_call(
        functools.partial(pair_kernel, outs, slots),
        out_shape=(shape((count, 2 * R, R), BF), shape((count, R, R), BF)),
        in_specs=[in_smem()] + [in_vmem()] * (2 + tiles),
        out_specs=(in_vmem(),) * 2,
        scratch_shapes=[VMEM((tiles, R, NB), BF)],
        compiler_params=params(),
        cost_estimate=cost(outs * slots * 1.75, 10),
        name="pair",
    )(packed, held_u, probes, *group_v)
    far_u, mixing = lax.optimization_barrier((far_u, mixing))
    group_u += [far_u, *other_u, swap(far_u, tiles)]
    own, send1, send2, send3, group = pl.pallas_call(
        functools.partial(sketch_kernel, outs, slots),
        out_shape=(shape((NB, R), F32),) + (shape((NB, R), BF),) * 3 + (shape((tiles, NB, R), BF),),
        in_specs=[in_smem()] + [in_vmem()] * (1 + tiles),
        out_specs=(in_vmem(),) * 5,
        scratch_shapes=[VMEM((YS, NB, R), F32)],
        compiler_params=params(),
        cost_estimate=cost(outs * slots, 4),
        name="sketch",
    )(packed, mixing, *group_u)
    total = own
    for got in spread((send1, send2, send3), zs):
        total = total + got.astype(F32)
    rows = NB // zs
    mine = jnp.sum(over_z(total.reshape(zs, rows, R), zs), axis=0)
    summed = over_z(jnp.broadcast_to(mine[None], (zs, rows, R)), zs)
    out_rows = NB // (zs * YS)
    messages = pl.pallas_call(
        functools.partial(ortho_kernel, zs),
        out_shape=(shape((NB + 2 * out_rows, R), BF),) * YS,
        in_specs=[in_vmem()],
        out_specs=(in_vmem(),) * YS,
        scratch_shapes=[VMEM((NB, R), F32)],
        compiler_params=params(),
        cost_estimate=cost(13, 1),
        name="ortho",
    )(summed)
    mine, held = pl.pallas_call(
        functools.partial(backward_own_kernel, outs, slots),
        out_shape=(shape((1, NB, R), F32), shape((count, NB, R), BF)),
        in_specs=[in_smem(), in_place()] + [in_vmem()] * 3,
        out_specs=(in_vmem(),) * 2,
        scratch_shapes=[VMEM((1, R, NB), BF), pltpu.SemaphoreType.DMA((count,))],
        compiler_params=params(),
        cost_estimate=cost(slots * 2.75, 4),
        name="backward_own",
    )(packed, right_v, group, pairs, messages[0])
    messages = [messages[0]] + spread(messages[1:], zs)
    pieces = (zs, outs, out_rows, R)
    own, send1, send2, send3, basis = pl.pallas_call(
        functools.partial(backward_kernel, slots, zs),
        out_shape=(shape(pieces, F32),) + (shape(pieces, BF),) * 3 + (shape((outs, out_rows, R), F32),),
        in_specs=[in_smem()] + [in_vmem()] * (4 + YS),
        out_specs=(in_vmem(),) * 5,
        scratch_shapes=[VMEM((YS, R, NB), BF), VMEM((YS, NB, R), F32)],
        compiler_params=params(),
        cost_estimate=cost(outs * slots * 2, 8),
        name="backward",
    )(packed, held, group, pairs, mine, *messages)
    part = own
    for got in spread((send1, send2, send3), zs):
        part = part + got.astype(F32)
    coeff = jnp.sum(over_z(part.astype(BF), zs).astype(F32), axis=0)
    return (basis, coeff)


def solution(mesh):
    return jax.shard_map(
        body,
        mesh=mesh,
        in_specs=(
            P(("inner", "cols"), None, None),
            P(("inner", "cols"), None, None),
            P("cols", "inner", None, None),
            P("cols", "inner", None, None),
            P("cols", None, None),
            P("cols", "inner"),
            P("cols", "inner"),
        ),
        out_specs=(P("cols", "inner", None), P("cols", "inner", None)),
        check_vma=False,
    )
```

```python
import functools
import math

import jax
import jax.numpy as jnp
from jax import lax
from jax.experimental import pallas as pl
from jax.experimental.pallas import tpu as pltpu
from jax.sharding import PartitionSpec as P

NB = 512
R = 128
YS = 4
BATCH = 4
HIGH = lax.Precision.HIGHEST
BF = jnp.bfloat16
F32 = jnp.float32
VMEM = pltpu.VMEM
NN = (((1,), (0,)), ((), ()))
NT = (((1,), (1,)), ((), ()))
TN = (((0,), (0,)), ((), ()))


def dot(a, b):
    return jnp.dot(a, b, preferred_element_type=F32)


def dot_nt(a, b):
    return lax.dot_general(a, b, NT, preferred_element_type=F32)


def halves(a):
    high = a.astype(BF)
    return high, (a - high.astype(F32)).astype(BF)


def in_vmem():
    return pl.BlockSpec(memory_space=VMEM)


def in_place():
    return pl.BlockSpec(memory_space=pltpu.HBM)


def in_smem():
    return pl.BlockSpec(memory_space=pltpu.SMEM)


def live(packed, j):
    count = packed[j, 0] & 1
    for s in range(1, packed.shape[1]):
        count += packed[j, s] & 1
    return count


def tile_of(packed, at):
    slots = packed.shape[1]
    return packed[lax.div(at, slots), lax.rem(at, slots)] >> 1


def y_of():
    return lax.rem(lax.axis_index("inner"), YS)


def fetch(meta, outs, slots, source, held, sems):
    def tile(j, _):
        def one(s, _):
            pltpu.make_async_copy(source.at[j, s], held.at[j * slots + s], sems.at[j * slots + s]).start()
            return 0

        lax.fori_loop(0, live(meta, j), one, 0)
        return 0

    lax.fori_loop(0, outs, tile, 0)


def arrive(count, slots, j, s, source, held, sems):
    @pl.when(s < count)
    def _():
        pltpu.make_async_copy(source.at[j, s], held.at[j * slots + s], sems.at[j * slots + s]).wait()


def beside(a, b):
    return jnp.concatenate([a, b], axis=1)


def above(a, b):
    return jnp.concatenate([a, b], axis=0)


def sweep(meta, together, work):
    for tiles in together:
        work([(place, j, 0, live(meta, j)) for place, j in tiles], True)

    def rest(place, j):
        count = live(meta, j)

        def batch(first, _):
            work([(place, j, first * BATCH, count)], False)
            return 0

        lax.fori_loop(1, (count + BATCH - 1) // BATCH, batch, 0)

    for tiles in together:
        for place, j in tiles:
            rest(place, j)


def batches(items, slots):
    return [
        (j * slots + jnp.minimum(base + i, count - 1), j * slots + base + i, base + i < count)
        for _, j, base, count in items for i in range(BATCH)
    ]


def two_by_two(tiles):
    return [tiles[:2], tiles[2:]]


def settle(meta, outs, slots, source, held, sems):
    def tile(j, _):
        def one(s, _):
            pltpu.make_async_copy(source.at[j, s], held.at[j * slots + s], sems.at[j * slots + s]).wait()
            return 0

        lax.fori_loop(0, live(meta, j), one, 0)
        return 0

    lax.fori_loop(0, outs, tile, 0)


def load_kernel(outs, slots, meta, right_v, sketch, held, plain, sems, sem):
    fetch(meta, outs, slots, right_v, held, sems)
    copy = pltpu.make_async_copy(sketch, plain, sem)
    copy.start()
    settle(meta, outs, slots, right_v, held, sems)
    copy.wait()


def probe_kernel(outs, slots, meta, right_u, held, sketch, probes, held_u, sems):
    fetch(meta, outs, slots, right_u, held_u, sems)

    def work(items, first):
        turned = [sketch[j].T for _, j, _, _ in items]
        at = batches(items, slots)
        products = [dot(turned[n // BATCH], held[slot]) for n, (slot, _, _) in enumerate(at)]
        for (slot, _, _), product in zip(at, products):
            probes[slot] = beside(*halves(product))

    sweep(meta, two_by_two([(j, j) for j in range(outs)]), work)
    settle(meta, outs, slots, right_u, held_u, sems)


def tile_ids(tiles):
    me = lax.axis_index("cols")
    return [lax.rem(me + 2 * hop, tiles) ^ flip for flip in (0, 1) for hop in (0, tiles // 2 - 1, 1, 2)]


def pair_kernel(outs, slots, meta, held, probes, *rest):
    parts, (pairs, mixing, turned) = rest[:-3], rest[-3:]
    for k, part in zip(tile_ids(len(parts)), parts):
        turned[k] = part[0].T

    def work(items, first):
        at = batches(items, slots)
        products = [halves(dot(turned[tile_of(meta, slot)], held[slot])) for slot, _, _ in at]
        mixes = []
        for (slot, _, _), (high, low) in zip(at, products):
            probe = probes[slot]
            mixes.append(dot_nt(high, probe[:, :R]) + dot_nt(high, probe[:, R:]) + dot_nt(low, probe[:, :R]))
        for (slot, place, alive), product, mixed in zip(at, products, mixes):
            pairs[slot] = above(*product)
            mixing[place] = jnp.where(alive, mixed, 0.0).astype(BF)

    sweep(meta, two_by_two([(j, j) for j in range(outs)]), work)


def sketch_kernel(outs, slots, meta, mixing, *rest):
    parts, (own, send1, send2, send3, group, acc) = rest[:-6], rest[-6:]
    for k, part in zip(tile_ids(len(parts)), parts):
        group[k] = part[0]
    y = y_of()

    def work(items, first):
        at = batches(items, slots)
        tiles = [group[tile_of(meta, slot)] for slot, _, _ in at]
        terms = [
            dot(beside(tiles[i], tiles[i + 1]), above(mixing[at[i][1]], mixing[at[i + 1][1]]))
            for i in range(0, len(at), 2)
        ]
        for n, (place, _, _, _) in enumerate(items):
            term = terms[2 * n] + terms[2 * n + 1]
            acc[place] = term if first else acc[place] + term

    sweep(meta, two_by_two([(step, lax.rem(y + step, YS)) for step in range(YS)]), work)
    for step, out in enumerate((own, send1, send2, send3)):
        out[...] = acc[step].astype(out.dtype)


def exact(a, b, dims):
    return lax.dot_general(a, b, dims, precision=HIGH, preferred_element_type=F32)


def inverse_factor(block):
    n = block.shape[0]
    lanes = 2 * n
    same = lax.broadcasted_iota(jnp.int32, (n, n), 0) == lax.broadcasted_iota(jnp.int32, (n, n), 1)
    full = jnp.concatenate([same.astype(F32), block], axis=1)
    x = [full[8 * i:8 * i + 8] for i in range(n // 8)]
    done = list(x)
    sub = lax.broadcasted_iota(jnp.int32, (8, lanes), 0)

    def wide(v):
        return jnp.broadcast_to(v, (8, lanes))

    for k in range(0, n, 4):
        i0, r = k // 8, k % 8
        row = [wide(x[i0][r + t:r + t + 1]) for t in range(4)]
        b = {(t, u): wide(row[t][:, n + k + u:n + k + u + 1]) for t in range(4) for u in range(t, 4)}
        one = 1.0 / (b[0, 0] * b[1, 1] - b[0, 1] * b[0, 1])
        t00 = (b[1, 1] * b[0, 2] - b[0, 1] * b[1, 2]) * one
        t01 = (b[1, 1] * b[0, 3] - b[0, 1] * b[1, 3]) * one
        t10 = (b[0, 0] * b[1, 2] - b[0, 1] * b[0, 2]) * one
        t11 = (b[0, 0] * b[1, 3] - b[0, 1] * b[0, 3]) * one
        s00 = b[2, 2] - (b[0, 2] * t00 + b[1, 2] * t10)
        s01 = b[2, 3] - (b[0, 2] * t01 + b[1, 2] * t11)
        s11 = b[3, 3] - (b[0, 3] * t01 + b[1, 3] * t11)
        two = 1.0 / (s00 * s11 - s01 * s01)
        e2 = row[2] - (t00 * row[0] + t10 * row[1])
        e3 = row[3] - (t01 * row[0] + t11 * row[1])
        p2, p3 = (s11 * e2 - s01 * e3) * two, (s00 * e3 - s01 * e2) * two
        p0 = (b[1, 1] * row[0] - b[0, 1] * row[1]) * one - (t00 * p2 + t01 * p3)
        p1 = (b[0, 0] * row[1] - b[0, 1] * row[0]) * one - (t10 * p2 + t11 * p3)
        for i in range(i0, n // 8):
            if i == i0 and r == 4:
                continue
            u = [wide(x[i][:, n + k + t:n + k + t + 1]) for t in range(4)]
            step = (u[0] * p0 + u[1] * p1) + (u[2] * p2 + u[3] * p3)
            if i == i0:
                step = jnp.where(sub > r + 3, step, 0.0)
            x[i] = x[i] - step
        for t, (a, c, d, first, second) in enumerate((
            (b[0, 0], b[0, 1], b[1, 1], row[0], row[1]), (s00, s01, s11, e2, e3)
        )):
            root = lax.rsqrt(a)
            off = c * root
            first = first * root
            second = (second - off * first) * lax.rsqrt(d - off * off)
            done[i0] = jnp.where(sub == r + 2 * t, first, jnp.where(sub == r + 2 * t + 1, second, done[i0]))
    return jnp.concatenate(done, axis=0)[:, :n]


def inverse_cholesky(gram):
    half = gram.shape[0] // 2
    upper = inverse_factor(gram[:half, :half])
    across = exact(upper, gram[:half, half:], NN)
    lower = inverse_factor(gram[half:, half:] - exact(across, across, TN))
    corner = -exact(lower, exact(across, upper, TN), NN)
    top = jnp.concatenate([upper, jnp.zeros_like(upper)], axis=1)
    return jnp.concatenate([top, jnp.concatenate([corner, lower], axis=1)], axis=0)


def ortho_kernel(zs, blocks, msg0, msg1, msg2, msg3, ortho):
    inner = lax.axis_index("inner")
    y, z = lax.rem(inner, YS), lax.div(inner, YS)
    rows = NB // (zs * YS)
    summed = blocks[...].reshape(NB, R)
    ortho[...] = exact(summed, inverse_cholesky(exact(summed, summed, TN)), NT)
    high = ortho[...].astype(BF)
    for step, msg in enumerate((msg0, msg1, msg2, msg3)):
        start = pl.multiple_of((z * YS + lax.rem(y + step, YS)) * rows, rows)
        top, low = halves(ortho[pl.ds(start, rows)])
        msg[:NB] = high
        msg[NB:NB + rows] = top
        msg[NB + rows:] = low


def backward_work(slots, meta, turned, group, pairs, held, acc, items, first):
    at = batches(items, slots)
    mine = [turned[place] for place, _, _, _ in items]
    products = [halves(dot(mine[n // BATCH], group[tile_of(meta, slot)])) for n, (slot, _, _) in enumerate(at)]
    backs = []
    for (slot, _, alive), (high, low) in zip(at, products):
        pair = pairs[slot]
        back = dot(high, pair[:R]) + dot(high, pair[R:]) + dot(low, pair[:R])
        backs.append(jnp.where(alive, back, 0.0).astype(BF))
    terms = [
        dot_nt(beside(held[at[i][0]], held[at[i + 1][0]]), beside(backs[i], backs[i + 1]))
        for i in range(0, len(at), 2)
    ]
    for n, (place, _, _, _) in enumerate(items):
        term = terms[2 * n] + terms[2 * n + 1]
        acc[place] = term if first else acc[place] + term


def backward_own_kernel(outs, slots, meta, right_v, group, pairs, msg, mine, held, turned, sems):
    fetch(meta, outs, slots, right_v, held, sems)
    y = y_of()
    turned[0] = msg[:NB].T

    def work(items, first):
        for _, j, base, count in items:
            for i in range(BATCH):
                arrive(count, slots, j, base + i, right_v, held, sems)
        backward_work(slots, meta, turned, group, pairs, held, mine, items, first)

    sweep(meta, [[(0, y)]], work)

    def tile(order, _):
        j = lax.rem(y + order, YS)

        def one(s, _):
            pltpu.make_async_copy(right_v.at[j, s], held.at[j * slots + s], sems.at[j * slots + s]).wait()
            return 0

        lax.fori_loop(0, live(meta, j), one, 0)
        return 0

    lax.fori_loop(1, YS, tile, 0)


def backward_kernel(slots, zs, meta, held, group, pairs, mine, msg0, msg1, msg2, msg3,
                    own, send1, send2, send3, basis, turned, acc):
    y = y_of()
    rows = NB // (zs * YS)
    tiles = [lax.rem(y + YS - step, YS) for step in range(YS)]
    for step, msg in enumerate((msg0, msg1, msg2, msg3)):
        if step:
            turned[step] = msg[:NB].T
        kept = msg[NB:NB + rows].astype(F32) + msg[NB + rows:].astype(F32)
        basis[tiles[step]] = kept * math.sqrt(NB)

    def work(items, first):
        backward_work(slots, meta, turned, group, pairs, held, acc, items, first)

    sweep(meta, [[(step, tiles[step]) for step in range(1, YS)]], work)
    acc[0] = mine[0]
    for step, out in enumerate((own, send1, send2, send3)):
        there = lax.rem(y + step, YS)
        for block in range(zs):
            start = pl.multiple_of((block * YS + there) * rows, rows)
            for place in range(YS):
                out[block, tiles[place]] = acc[place, pl.ds(start, rows)].astype(out.dtype)


def shift_y(array, step, zs):
    pairs = [(z * YS + y, z * YS + (y + step) % YS) for z in range(zs) for y in range(YS)]
    return lax.ppermute(array, "inner", pairs)


def hop(value, step, tiles):
    return lax.ppermute(value, "cols", [(i, (i + 2 * step) % tiles) for i in range(tiles)])


def swap(value, tiles):
    return lax.ppermute(value, "cols", [(i, i ^ 1) for i in range(tiles)])


def spread(sends, zs):
    got = {step: shift_y(sends[step - 1], step, zs) for step in (2, 1, 3)}
    return [got[step] for step in (1, 2, 3)]


def over_z(array, zs):
    groups = [[z * YS + y for z in range(zs)] for y in range(YS)]
    return lax.all_to_all(array, "inner", 0, 0, tiled=True, axis_index_groups=groups)


def params():
    return pltpu.CompilerParams(vmem_limit_bytes=20 << 20)


def body(left_u, left_v, right_u, right_v, sketch, tile_index, slot_mask):
    zs = lax.axis_size("inner") // YS
    outs, slots = tile_index.shape
    tiles = lax.axis_size("cols")
    shape = jax.ShapeDtypeStruct
    count = outs * slots
    packed = (tile_index - lax.axis_index("inner") * tiles) * 2 + slot_mask
    right_u = pltpu.with_memory_space_constraint(right_u, pltpu.HBM)
    right_v = pltpu.with_memory_space_constraint(right_v, pltpu.HBM)
    unit = 2 * NB * R * R

    def cost(units, mib):
        return pl.CostEstimate(flops=int(units * unit), bytes_accessed=mib << 20, transcendentals=0)

    near = [hop(value, step, tiles) for value in (left_v, left_u) for step in (1, -1)]
    near_v, near_u = near[:2], near[2:]
    sketch = pltpu.with_memory_space_constraint(sketch, pltpu.HBM)
    held_v, sketch = pl.pallas_call(
        functools.partial(load_kernel, outs, slots),
        out_shape=(shape((count, NB, R), BF), shape(sketch.shape, BF)),
        in_specs=[in_smem()] + [in_place()] * 2,
        out_specs=(in_vmem(),) * 2,
        scratch_shapes=[pltpu.SemaphoreType.DMA((count,)), pltpu.SemaphoreType.DMA],
        compiler_params=params(),
        cost_estimate=cost(0, 5),
        name="load",
    )(packed, right_v, sketch)
    *near_v, sketch = lax.optimization_barrier((*near_v, sketch))
    far_v = hop(near_v[1], -1, tiles)
    probes, held_u = pl.pallas_call(
        functools.partial(probe_kernel, outs, slots),
        out_shape=(shape((count, R, 2 * R), BF), shape((count, NB, R), BF)),
        in_specs=[in_smem(), in_place()] + [in_vmem()] * 2,
        out_specs=(in_vmem(),) * 2,
        scratch_shapes=[pltpu.SemaphoreType.DMA((count,))],
        compiler_params=params(),
        cost_estimate=cost(outs * slots, 6),
        name="probe",
    )(packed, right_u, held_v, sketch)
    *near_u, far_v, probes = lax.optimization_barrier((*near_u, far_v, probes))
    far_u = hop(near_u[0], 1, tiles)
    group_v = [left_v, *near_v, far_v]
    group_v += [swap(value, tiles) for value in group_v]
    group_u = [left_u, *near_u]
    other_u = [swap(value, tiles) for value in group_u]
    pairs, mixing = pl.pallas_call(
        functools.partial(pair_kernel, outs, slots),
        out_shape=(shape((count, 2 * R, R), BF), shape((count, R, R), BF)),
        in_specs=[in_smem()] + [in_vmem()] * (2 + tiles),
        out_specs=(in_vmem(),) * 2,
        scratch_shapes=[VMEM((tiles, R, NB), BF)],
        compiler_params=params(),
        cost_estimate=cost(outs * slots * 1.75, 10),
        name="pair",
    )(packed, held_u, probes, *group_v)
    far_u, mixing = lax.optimization_barrier((far_u, mixing))
    group_u += [far_u, *other_u, swap(far_u, tiles)]
    own, send1, send2, send3, group = pl.pallas_call(
        functools.partial(sketch_kernel, outs, slots),
        out_shape=(shape((NB, R), F32),) + (shape((NB, R), BF),) * 3 + (shape((tiles, NB, R), BF),),
        in_specs=[in_smem()] + [in_vmem()] * (1 + tiles),
        out_specs=(in_vmem(),) * 5,
        scratch_shapes=[VMEM((YS, NB, R), F32)],
        compiler_params=params(),
        cost_estimate=cost(outs * slots, 4),
        name="sketch",
    )(packed, mixing, *group_u)
    total = own
    for got in spread((send1, send2, send3), zs):
        total = total + got.astype(F32)
    rows = NB // zs
    mine = jnp.sum(over_z(total.reshape(zs, rows, R), zs), axis=0)
    summed = over_z(jnp.broadcast_to(mine[None], (zs, rows, R)), zs)
    out_rows = NB // (zs * YS)
    messages = pl.pallas_call(
        functools.partial(ortho_kernel, zs),
        out_shape=(shape((NB + 2 * out_rows, R), BF),) * YS,
        in_specs=[in_vmem()],
        out_specs=(in_vmem(),) * YS,
        scratch_shapes=[VMEM((NB, R), F32)],
        compiler_params=params(),
        cost_estimate=cost(13, 1),
        name="ortho",
    )(summed)
    mine, held = pl.pallas_call(
        functools.partial(backward_own_kernel, outs, slots),
        out_shape=(shape((1, NB, R), F32), shape((count, NB, R), BF)),
        in_specs=[in_smem(), in_place()] + [in_vmem()] * 3,
        out_specs=(in_vmem(),) * 2,
        scratch_shapes=[VMEM((1, R, NB), BF), pltpu.SemaphoreType.DMA((count,))],
        compiler_params=params(),
        cost_estimate=cost(slots * 2.75, 4),
        name="backward_own",
    )(packed, right_v, group, pairs, messages[0])
    messages = [messages[0]] + spread(messages[1:], zs)
    pieces = (zs, outs, out_rows, R)
    own, send1, send2, send3, basis = pl.pallas_call(
        functools.partial(backward_kernel, slots, zs),
        out_shape=(shape(pieces, F32),) + (shape(pieces, BF),) * 3 + (shape((outs, out_rows, R), F32),),
        in_specs=[in_smem()] + [in_vmem()] * (4 + YS),
        out_specs=(in_vmem(),) * 5,
        scratch_shapes=[VMEM((YS, R, NB), BF), VMEM((YS, NB, R), F32)],
        compiler_params=params(),
        cost_estimate=cost(outs * slots * 2, 8),
        name="backward",
    )(packed, held, group, pairs, mine, *messages)
    part = own
    for got in spread((send1, send2, send3), zs):
        part = part + got.astype(F32)
    coeff = jnp.sum(over_z(part.astype(BF), zs).astype(F32), axis=0)
    return (basis, coeff)


def solution(mesh):
    return jax.shard_map(
        body,
        mesh=mesh,
        in_specs=(
            P(("inner", "cols"), None, None),
            P(("inner", "cols"), None, None),
            P("cols", "inner", None, None),
            P("cols", "inner", None, None),
            P("cols", None, None),
            P("cols", "inner"),
            P("cols", "inner"),
        ),
        out_specs=(P("cols", "inner", None), P("cols", "inner", None)),
        check_vma=False,
    )
```

```python
import functools
import math

import jax
import jax.numpy as jnp
from jax import lax
from jax.experimental import pallas as pl
from jax.experimental.pallas import tpu as pltpu
from jax.sharding import PartitionSpec as P

NB = 512
R = 128
YS = 4
BATCH = 4
FIRST = (2, 1, 3)
HIGH = lax.Precision.HIGHEST
BF = jnp.bfloat16
F32 = jnp.float32
VMEM = pltpu.VMEM
NN = (((1,), (0,)), ((), ()))
NT = (((1,), (1,)), ((), ()))
TN = (((0,), (0,)), ((), ()))


def dot(a, b):
    return jnp.dot(a, b, preferred_element_type=F32)


def dot_nt(a, b):
    return lax.dot_general(a, b, NT, preferred_element_type=F32)


def halves(a):
    high = a.astype(BF)
    return high, (a - high.astype(F32)).astype(BF)


def in_vmem():
    return pl.BlockSpec(memory_space=VMEM)


def in_place():
    return pl.BlockSpec(memory_space=pltpu.HBM)


def in_smem():
    return pl.BlockSpec(memory_space=pltpu.SMEM)


def live(packed, j):
    count = packed[j, 0] & 1
    for s in range(1, packed.shape[1]):
        count += packed[j, s] & 1
    return count


def tile_of(packed, at):
    slots = packed.shape[1]
    return packed[lax.div(at, slots), lax.rem(at, slots)] >> 1


def y_of():
    return lax.rem(lax.axis_index("inner"), YS)


def fetch(meta, outs, slots, source, held, sems):
    def tile(j, _):
        def one(s, _):
            pltpu.make_async_copy(source.at[j, s], held.at[j * slots + s], sems.at[j * slots + s]).start()
            return 0

        lax.fori_loop(0, live(meta, j), one, 0)
        return 0

    lax.fori_loop(0, outs, tile, 0)


def arrive(count, slots, j, s, source, held, sems):
    @pl.when(s < count)
    def _():
        pltpu.make_async_copy(source.at[j, s], held.at[j * slots + s], sems.at[j * slots + s]).wait()


def beside(a, b):
    return jnp.concatenate([a, b], axis=1)


def above(a, b):
    return jnp.concatenate([a, b], axis=0)


def sweep(meta, together, work):
    for tiles in together:
        work([(place, j, 0, live(meta, j)) for place, j in tiles], True)

    def rest(place, j):
        count = live(meta, j)

        def batch(first, _):
            work([(place, j, first * BATCH, count)], False)
            return 0

        lax.fori_loop(1, (count + BATCH - 1) // BATCH, batch, 0)

    for tiles in together:
        for place, j in tiles:
            rest(place, j)


def batches(items, slots):
    return [
        (j * slots + jnp.minimum(base + i, count - 1), j * slots + base + i, base + i < count)
        for _, j, base, count in items for i in range(BATCH)
    ]


def two_by_two(tiles):
    return [tiles[:2], tiles[2:]]


def settle(meta, outs, slots, source, held, sems):
    def tile(j, _):
        def one(s, _):
            pltpu.make_async_copy(source.at[j, s], held.at[j * slots + s], sems.at[j * slots + s]).wait()
            return 0

        lax.fori_loop(0, live(meta, j), one, 0)
        return 0

    lax.fori_loop(0, outs, tile, 0)


def load_kernel(outs, slots, meta, right_v, sketch, held, plain, sems, sem):
    fetch(meta, outs, slots, right_v, held, sems)
    copy = pltpu.make_async_copy(sketch, plain, sem)
    copy.start()
    settle(meta, outs, slots, right_v, held, sems)
    copy.wait()


def probe_kernel(outs, slots, meta, right_u, held, sketch, probes, held_u, sems):
    fetch(meta, outs, slots, right_u, held_u, sems)

    def work(items, first):
        turned = [sketch[j].T for _, j, _, _ in items]
        at = batches(items, slots)
        products = [dot(turned[n // BATCH], held[slot]) for n, (slot, _, _) in enumerate(at)]
        for (slot, _, _), product in zip(at, products):
            probes[slot] = beside(*halves(product))

    sweep(meta, two_by_two([(j, j) for j in range(outs)]), work)
    settle(meta, outs, slots, right_u, held_u, sems)


def tile_ids(tiles):
    me = lax.axis_index("cols")
    return [lax.rem(me + 2 * hop, tiles) ^ flip for flip in (0, 1) for hop in (0, tiles // 2 - 1, 1, 2)]


def pair_kernel(outs, slots, meta, held, probes, *rest):
    parts, (pairs, mixing, turned) = rest[:-3], rest[-3:]
    for k, part in zip(tile_ids(len(parts)), parts):
        turned[k] = part[0].T

    def work(items, first):
        at = batches(items, slots)
        products = [halves(dot(turned[tile_of(meta, slot)], held[slot])) for slot, _, _ in at]
        mixes = []
        for (slot, _, _), (high, low) in zip(at, products):
            probe = probes[slot]
            mixes.append(dot_nt(high, probe[:, :R]) + dot_nt(high, probe[:, R:]) + dot_nt(low, probe[:, :R]))
        for (slot, place, alive), product, mixed in zip(at, products, mixes):
            pairs[slot] = above(*product)
            mixing[place] = jnp.where(alive, mixed, 0.0).astype(BF)

    sweep(meta, two_by_two([(j, j) for j in range(outs)]), work)


def sketch_kernel(outs, slots, meta, mixing, *rest):
    parts, (own, send1, send2, send3, group, acc) = rest[:-6], rest[-6:]
    for k, part in zip(tile_ids(len(parts)), parts):
        group[k] = part[0]
    y = y_of()

    def work(items, first):
        at = batches(items, slots)
        tiles = [group[tile_of(meta, slot)] for slot, _, _ in at]
        terms = [
            dot(beside(tiles[i], tiles[i + 1]), above(mixing[at[i][1]], mixing[at[i + 1][1]]))
            for i in range(0, len(at), 2)
        ]
        for n, (place, _, _, _) in enumerate(items):
            term = terms[2 * n] + terms[2 * n + 1]
            acc[place] = term if first else acc[place] + term

    sweep(meta, two_by_two([(step, lax.rem(y + step, YS)) for step in range(YS)]), work)
    for step, out in enumerate((own, send1, send2, send3)):
        out[...] = acc[step].astype(out.dtype)


def exact(a, b, dims):
    return lax.dot_general(a, b, dims, precision=HIGH, preferred_element_type=F32)


def inverse_factor(block):
    n = block.shape[0]
    lanes = 2 * n
    same = lax.broadcasted_iota(jnp.int32, (n, n), 0) == lax.broadcasted_iota(jnp.int32, (n, n), 1)
    full = jnp.concatenate([same.astype(F32), block], axis=1)
    x = [full[8 * i:8 * i + 8] for i in range(n // 8)]
    done = list(x)
    sub = lax.broadcasted_iota(jnp.int32, (8, lanes), 0)

    def wide(v):
        return jnp.broadcast_to(v, (8, lanes))

    for k in range(0, n, 4):
        i0, r = k // 8, k % 8
        row = [wide(x[i0][r + t:r + t + 1]) for t in range(4)]
        b = {(t, u): wide(row[t][:, n + k + u:n + k + u + 1]) for t in range(4) for u in range(t, 4)}
        one = 1.0 / (b[0, 0] * b[1, 1] - b[0, 1] * b[0, 1])
        t00 = (b[1, 1] * b[0, 2] - b[0, 1] * b[1, 2]) * one
        t01 = (b[1, 1] * b[0, 3] - b[0, 1] * b[1, 3]) * one
        t10 = (b[0, 0] * b[1, 2] - b[0, 1] * b[0, 2]) * one
        t11 = (b[0, 0] * b[1, 3] - b[0, 1] * b[0, 3]) * one
        s00 = b[2, 2] - (b[0, 2] * t00 + b[1, 2] * t10)
        s01 = b[2, 3] - (b[0, 2] * t01 + b[1, 2] * t11)
        s11 = b[3, 3] - (b[0, 3] * t01 + b[1, 3] * t11)
        two = 1.0 / (s00 * s11 - s01 * s01)
        e2 = row[2] - (t00 * row[0] + t10 * row[1])
        e3 = row[3] - (t01 * row[0] + t11 * row[1])
        p2, p3 = (s11 * e2 - s01 * e3) * two, (s00 * e3 - s01 * e2) * two
        p0 = (b[1, 1] * row[0] - b[0, 1] * row[1]) * one - (t00 * p2 + t01 * p3)
        p1 = (b[0, 0] * row[1] - b[0, 1] * row[0]) * one - (t10 * p2 + t11 * p3)
        for i in range(i0, n // 8):
            if i == i0 and r == 4:
                continue
            u = [wide(x[i][:, n + k + t:n + k + t + 1]) for t in range(4)]
            step = (u[0] * p0 + u[1] * p1) + (u[2] * p2 + u[3] * p3)
            if i == i0:
                step = jnp.where(sub > r + 3, step, 0.0)
            x[i] = x[i] - step
        for t, (a, c, d, first, second) in enumerate((
            (b[0, 0], b[0, 1], b[1, 1], row[0], row[1]), (s00, s01, s11, e2, e3)
        )):
            root = lax.rsqrt(a)
            off = c * root
            first = first * root
            second = (second - off * first) * lax.rsqrt(d - off * off)
            done[i0] = jnp.where(sub == r + 2 * t, first, jnp.where(sub == r + 2 * t + 1, second, done[i0]))
    return jnp.concatenate(done, axis=0)[:, :n]


def inverse_cholesky(gram):
    half = gram.shape[0] // 2
    upper = inverse_factor(gram[:half, :half])
    across = exact(upper, gram[:half, half:], NN)
    lower = inverse_factor(gram[half:, half:] - exact(across, across, TN))
    corner = -exact(lower, exact(across, upper, TN), NN)
    top = jnp.concatenate([upper, jnp.zeros_like(upper)], axis=1)
    return jnp.concatenate([top, jnp.concatenate([corner, lower], axis=1)], axis=0)


def ortho_kernel(zs, blocks, msg0, msg1, msg2, msg3, ortho):
    inner = lax.axis_index("inner")
    y, z = lax.rem(inner, YS), lax.div(inner, YS)
    rows = NB // (zs * YS)
    summed = blocks[...].reshape(NB, R)
    ortho[...] = exact(summed, inverse_cholesky(exact(summed, summed, TN)), NT)
    high = ortho[...].astype(BF)
    for step, msg in enumerate((msg0, msg1, msg2, msg3)):
        start = pl.multiple_of((z * YS + lax.rem(y + step, YS)) * rows, rows)
        top, low = halves(ortho[pl.ds(start, rows)])
        msg[:NB] = high
        msg[NB:NB + rows] = top
        msg[NB + rows:] = low


def backward_work(slots, meta, turned, group, pairs, held, acc, items, first):
    at = batches(items, slots)
    mine = [turned[place] for place, _, _, _ in items]
    products = [halves(dot(mine[n // BATCH], group[tile_of(meta, slot)])) for n, (slot, _, _) in enumerate(at)]
    backs = []
    for (slot, _, alive), (high, low) in zip(at, products):
        pair = pairs[slot]
        back = dot(high, pair[:R]) + dot(high, pair[R:]) + dot(low, pair[:R])
        backs.append(jnp.where(alive, back, 0.0).astype(BF))
    terms = [
        dot_nt(beside(held[at[i][0]], held[at[i + 1][0]]), beside(backs[i], backs[i + 1]))
        for i in range(0, len(at), 2)
    ]
    for n, (place, _, _, _) in enumerate(items):
        term = terms[2 * n] + terms[2 * n + 1]
        acc[place] = term if first else acc[place] + term


def backward_own_kernel(outs, slots, meta, right_v, group, pairs, msg, mine, held, turned, sems):
    fetch(meta, outs, slots, right_v, held, sems)
    y = y_of()
    turned[0] = msg[:NB].T

    def work(items, first):
        for _, j, base, count in items:
            for i in range(BATCH):
                arrive(count, slots, j, base + i, right_v, held, sems)
        backward_work(slots, meta, turned, group, pairs, held, mine, items, first)

    sweep(meta, [[(0, y)]], work)

    def tile(order, _):
        j = lax.rem(y + order, YS)

        def one(s, _):
            pltpu.make_async_copy(right_v.at[j, s], held.at[j * slots + s], sems.at[j * slots + s]).wait()
            return 0

        lax.fori_loop(0, live(meta, j), one, 0)
        return 0

    lax.fori_loop(1, YS, tile, 0)


def backward_kernel(slots, zs, meta, held, group, pairs, mine, msg0, msg_a, msg_b, msg_c,
                    own, send1, send2, send3, basis, turned, acc):
    y = y_of()
    rows = NB // (zs * YS)
    tiles = [lax.rem(y + YS - step, YS) for step in range(YS)]
    for step, msg in zip((0, *FIRST), (msg0, msg_a, msg_b, msg_c)):
        if step:
            turned[step] = msg[:NB].T
        kept = msg[NB:NB + rows].astype(F32) + msg[NB + rows:].astype(F32)
        basis[tiles[step]] = kept * math.sqrt(NB)

    def work(items, first):
        backward_work(slots, meta, turned, group, pairs, held, acc, items, first)

    sweep(meta, [[(step, tiles[step]) for step in range(1, YS)]], work)
    acc[0] = mine[0]
    for step, out in enumerate((own, send1, send2, send3)):
        there = lax.rem(y + step, YS)
        for block in range(zs):
            start = pl.multiple_of((block * YS + there) * rows, rows)
            for place in range(YS):
                out[block, tiles[place]] = acc[place, pl.ds(start, rows)].astype(out.dtype)


def shift_y(array, step, zs):
    pairs = [(z * YS + y, z * YS + (y + step) % YS) for z in range(zs) for y in range(YS)]
    return lax.ppermute(array, "inner", pairs)


def hop(value, step, tiles):
    return lax.ppermute(value, "cols", [(i, (i + 2 * step) % tiles) for i in range(tiles)])


def swap(value, tiles):
    return lax.ppermute(value, "cols", [(i, i ^ 1) for i in range(tiles)])


def spread(sends, zs):
    return [shift_y(sends[step - 1], step, zs) for step in FIRST]


def over_z(array, zs):
    groups = [[z * YS + y for z in range(zs)] for y in range(YS)]
    return lax.all_to_all(array, "inner", 0, 0, tiled=True, axis_index_groups=groups)


def params():
    return pltpu.CompilerParams(vmem_limit_bytes=20 << 20)


def body(left_u, left_v, right_u, right_v, sketch, tile_index, slot_mask):
    zs = lax.axis_size("inner") // YS
    outs, slots = tile_index.shape
    tiles = lax.axis_size("cols")
    shape = jax.ShapeDtypeStruct
    count = outs * slots
    packed = (tile_index - lax.axis_index("inner") * tiles) * 2 + slot_mask
    right_u = pltpu.with_memory_space_constraint(right_u, pltpu.HBM)
    right_v = pltpu.with_memory_space_constraint(right_v, pltpu.HBM)
    unit = 2 * NB * R * R

    def cost(units, mib):
        return pl.CostEstimate(flops=int(units * unit), bytes_accessed=mib << 20, transcendentals=0)

    near = [hop(value, step, tiles) for value in (left_v, left_u) for step in (1, -1)]
    near_v, near_u = near[:2], near[2:]
    sketch = pltpu.with_memory_space_constraint(sketch, pltpu.HBM)
    held_v, sketch = pl.pallas_call(
        functools.partial(load_kernel, outs, slots),
        out_shape=(shape((count, NB, R), BF), shape(sketch.shape, BF)),
        in_specs=[in_smem()] + [in_place()] * 2,
        out_specs=(in_vmem(),) * 2,
        scratch_shapes=[pltpu.SemaphoreType.DMA((count,)), pltpu.SemaphoreType.DMA],
        compiler_params=params(),
        cost_estimate=cost(0, 5),
        name="load",
    )(packed, right_v, sketch)
    *near_v, sketch = lax.optimization_barrier((*near_v, sketch))
    far_v = hop(near_v[1], -1, tiles)
    probes, held_u = pl.pallas_call(
        functools.partial(probe_kernel, outs, slots),
        out_shape=(shape((count, R, 2 * R), BF), shape((count, NB, R), BF)),
        in_specs=[in_smem(), in_place()] + [in_vmem()] * 2,
        out_specs=(in_vmem(),) * 2,
        scratch_shapes=[pltpu.SemaphoreType.DMA((count,))],
        compiler_params=params(),
        cost_estimate=cost(outs * slots, 6),
        name="probe",
    )(packed, right_u, held_v, sketch)
    *near_u, far_v, probes = lax.optimization_barrier((*near_u, far_v, probes))
    far_u = hop(near_u[0], 1, tiles)
    group_v = [left_v, *near_v, far_v]
    group_v += [swap(value, tiles) for value in group_v]
    group_u = [left_u, *near_u]
    other_u = [swap(value, tiles) for value in group_u]
    pairs, mixing = pl.pallas_call(
        functools.partial(pair_kernel, outs, slots),
        out_shape=(shape((count, 2 * R, R), BF), shape((count, R, R), BF)),
        in_specs=[in_smem()] + [in_vmem()] * (2 + tiles),
        out_specs=(in_vmem(),) * 2,
        scratch_shapes=[VMEM((tiles, R, NB), BF)],
        compiler_params=params(),
        cost_estimate=cost(outs * slots * 1.75, 10),
        name="pair",
    )(packed, held_u, probes, *group_v)
    far_u, mixing = lax.optimization_barrier((far_u, mixing))
    group_u += [far_u, *other_u, swap(far_u, tiles)]
    own, send1, send2, send3, group = pl.pallas_call(
        functools.partial(sketch_kernel, outs, slots),
        out_shape=(shape((NB, R), F32),) + (shape((NB, R), BF),) * 3 + (shape((tiles, NB, R), BF),),
        in_specs=[in_smem()] + [in_vmem()] * (1 + tiles),
        out_specs=(in_vmem(),) * 5,
        scratch_shapes=[VMEM((YS, NB, R), F32)],
        compiler_params=params(),
        cost_estimate=cost(outs * slots, 4),
        name="sketch",
    )(packed, mixing, *group_u)
    total = own
    for got in spread((send1, send2, send3), zs):
        total = total + got.astype(F32)
    rows = NB // zs
    mine = jnp.sum(over_z(total.reshape(zs, rows, R), zs), axis=0)
    summed = over_z(jnp.broadcast_to(mine[None], (zs, rows, R)), zs)
    out_rows = NB // (zs * YS)
    messages = pl.pallas_call(
        functools.partial(ortho_kernel, zs),
        out_shape=(shape((NB + 2 * out_rows, R), BF),) * YS,
        in_specs=[in_vmem()],
        out_specs=(in_vmem(),) * YS,
        scratch_shapes=[VMEM((NB, R), F32)],
        compiler_params=params(),
        cost_estimate=cost(13, 1),
        name="ortho",
    )(summed)
    mine, held = pl.pallas_call(
        functools.partial(backward_own_kernel, outs, slots),
        out_shape=(shape((1, NB, R), F32), shape((count, NB, R), BF)),
        in_specs=[in_smem(), in_place()] + [in_vmem()] * 3,
        out_specs=(in_vmem(),) * 2,
        scratch_shapes=[VMEM((1, R, NB), BF), pltpu.SemaphoreType.DMA((count,))],
        compiler_params=params(),
        cost_estimate=cost(slots * 2.75, 4),
        name="backward_own",
    )(packed, right_v, group, pairs, messages[0])
    messages = [messages[0]] + spread(messages[1:], zs)
    pieces = (zs, outs, out_rows, R)
    own, send1, send2, send3, basis = pl.pallas_call(
        functools.partial(backward_kernel, slots, zs),
        out_shape=(shape(pieces, F32),) + (shape(pieces, BF),) * 3 + (shape((outs, out_rows, R), F32),),
        in_specs=[in_smem()] + [in_vmem()] * (4 + YS),
        out_specs=(in_vmem(),) * 5,
        scratch_shapes=[VMEM((YS, R, NB), BF), VMEM((YS, NB, R), F32)],
        compiler_params=params(),
        cost_estimate=cost(outs * slots * 2, 8),
        name="backward",
    )(packed, held, group, pairs, mine, *messages)
    part = own
    for got in spread((send1, send2, send3), zs):
        part = part + got.astype(F32)
    coeff = jnp.sum(over_z(part.astype(BF), zs).astype(F32), axis=0)
    return (basis, coeff)


def solution(mesh):
    return jax.shard_map(
        body,
        mesh=mesh,
        in_specs=(
            P(("inner", "cols"), None, None),
            P(("inner", "cols"), None, None),
            P("cols", "inner", None, None),
            P("cols", "inner", None, None),
            P("cols", None, None),
            P("cols", "inner"),
            P("cols", "inner"),
        ),
        out_specs=(P("cols", "inner", None), P("cols", "inner", None)),
        check_vma=False,
    )
```
